32 devices in a mesh: head: 4 (over y, core), batch: 8 (over z, x).
Axes of the slice: x: 2, y: 2, z: 4, core: 2. Of those that a mesh axis runs over, the one named last changes fastest.
Arguments:
- tokens: bfloat16 [8, 2048, 1024], P('batch'), may hold values from -6 to 6
- seq_lengths: int32 [8, 4], P('batch'), may hold values from 0 to 2048, as said below
- qkv_weight: bfloat16 [3, 1024, 1024], P(None, None, 'head'), may hold values from -0.1875 to 0.1875
- out_weight: bfloat16 [1024, 1024], P('head'), may hold values from -0.1875 to 0.1875
- up_gate_weight: bfloat16 [2, 1024, 4096], P(None, None, 'head'), may hold values from -0.1875 to 0.1875
- down_weight: bfloat16 [4096, 1024], P('head'), may hold values from -0.09375 to 0.09375
- qk_scale: float32 [1024], P('head'), may hold values from 0.9 to 1.8
- mlp_scale: float32 [2, 4096], P(None, 'head'), may hold values from 0.5 to 2
- eigen_rates: float32 [1024, 2], replicated, may hold values from 0.05 to 0.6
- cotangent: bfloat16 [8, 2048, 1024], P('batch', 'head'), may hold values from -6 to 6
- block_order: int32 [4, 256], P('head'), may hold values from 0 to 255, each once within a row
- master_blocks: float32 [4, 256, 128, 128], P('head', 'batch'), may hold values from -0.1875 to 0.1875
- ema_blocks: float32 [4, 256, 128, 128], P('head', 'batch'), may hold values from -0.1875 to 0.1875
- left_stats: float32 [4, 256, 128, 128], P('head', 'batch'), as said below
- right_stats: float32 [4, 256, 128, 128], P('head', 'batch'), as said below
- left_root: float32 [4, 256, 128, 128], P('head', 'batch'), as said below
- right_root: float32 [4, 256, 128, 128], P('head', 'batch'), as said below
Outputs:
- block_out: float32 [8, 2048, 1024], P('batch', 'head')
- input_grad: float32 [8, 2048, 1024], P('batch', 'head')
- grad_blocks: float32 [4, 256, 128, 128], P('head', 'batch')
- new_master: float32 [4, 256, 128, 128], P('head', 'batch')
- new_ema: float32 [4, 256, 128, 128], P('head', 'batch')
- new_left: float32 [4, 256, 128, 128], P('head', 'batch')
- new_right: float32 [4, 256, 128, 128], P('head', 'batch')
- qk_scale_grad: float32 [1024], P('head')
- mlp_scale_out: float32 [2, 2, 4096], P(None, None, 'head')
- rate_grad: float32 [1024, 2], P('head')
- new_gains: float32 [3, 1024], P(None, 'head')
The draws below stay inside these ranges and needn't reach their ends.
Inputs may be any that keep to these rules, and one draw needn't show every extreme that they name: `seq_lengths`: each row holds one sequence of 2048 tokens followed by zeros, or 4 sequences of 512 tokens; half of the rows are of each kind. `block_order`: each row names every block of its head group once. `left_stats`: each block is symmetric. `right_stats`: each block is symmetric. `left_root`: each block is symmetric. `right_root`: each block is symmetric.
All inputs are finite; a program needn't handle non-finite values.
Results may differ from the reference program's by a relative error of at most 0.02.
Values may be sent and summed in bfloat16 or wider, within the bound.
No kernel may reach another device: no remote copies, remote signals or barrier semaphores. Data moves between devices by JAX's collectives and lax.ppermute only.
A program may use at most 192 MiB of HBM per device.

```python
import math
import jax
import jax.numpy as jnp
from jax import lax

D = 1024
HEADS = 16
HEAD_DIM = 64
FF = 4096
TOK_DEV = 2048
SLOTS = 4
BLOCK = 128
TOKENS = 16384
NCOL_DEV = 4096
NBLK = 256
N_HEAD = 4
N_BATCH = 8


def draw_seq_lengths(key, part):
    long_flag = jax.random.permutation(jax.random.fold_in(key, 3), N_BATCH) < N_BATCH // 2
    short_len = TOK_DEV // SLOTS
    long_row = jnp.concatenate([jnp.full((1,), TOK_DEV, jnp.int32), jnp.zeros((SLOTS - 1,), jnp.int32)])
    short_row = jnp.full((SLOTS,), short_len, jnp.int32)
    return jnp.where(long_flag[:, None], long_row[None, :], short_row[None, :]).astype(jnp.int32)


def grad_level():
    return 0.1 * math.sqrt(TOKENS)


def dominant_blocks(key, level, low_end, high_end):
    first, second = jax.random.split(key)
    diagonal = jax.random.uniform(first, (N_HEAD, NBLK, BLOCK), jnp.float32, low_end, high_end) * level
    noise = jax.random.uniform(second, (N_HEAD, NBLK, BLOCK, BLOCK), jnp.float32, -1.0, 1.0)
    noise = 0.5 * (noise + jnp.swapaxes(noise, -1, -2)) * (0.9 * low_end * level / BLOCK)
    identity = jnp.eye(BLOCK, dtype=jnp.float32)
    return noise * (1.0 - identity) + identity * diagonal[..., None]


def draw_left_stats(key, part):
    return dominant_blocks(jax.random.fold_in(key, 11), BLOCK * grad_level() ** 2, 1.0, 4.0)


def draw_right_stats(key, part):
    return dominant_blocks(jax.random.fold_in(key, 12), BLOCK * grad_level() ** 2, 1.0, 4.0)


def draw_left_root(key, part):
    return dominant_blocks(jax.random.fold_in(key, 13), (BLOCK * grad_level() ** 2) ** (-0.25), 0.5, 2.0)


def draw_right_root(key, part):
    return dominant_blocks(jax.random.fold_in(key, 14), (BLOCK * grad_level() ** 2) ** (-0.25), 0.5, 2.0)


def levels(stream_key, shape, shards, least, high):
    def one(dim, parts):
        draws = jax.random.uniform(jax.random.fold_in(jax.random.fold_in(stream_key, 6), dim), (parts,), jnp.float32, least / len(shards), high / len(shards))
        return jnp.repeat(jnp.exp(draws), shape[dim] // parts).reshape((-1,) + (1,) * (len(shape) - dim - 1))

    factor_of = one(*shards[0])
    for cut in shards[1:]:
        factor_of = factor_of * one(*cut)
    return factor_of


def scatter_about(own_key, dims, width, reach, shards=(), kind=jnp.bfloat16):
    values = width * jax.random.normal(own_key, dims, jnp.float32)
    if shards:
        values = values * levels(own_key, dims, shards, -0.22, 0.18)
    return jnp.clip(values, -reach, reach).astype(kind)


def setup_inputs(seed: int = 0) -> dict:
    streams_of = jax.random.split(jax.random.key(seed), 18)
    return {
        "tokens": scatter_about(streams_of[0], (N_BATCH, TOK_DEV, D), 1.0, 6.0, ((0, 8),)),
        "seq_lengths": draw_seq_lengths(jax.random.fold_in(streams_of[17], 71), 0),
        "qkv_weight": scatter_about(streams_of[2], (3, D, HEADS * HEAD_DIM), D ** -0.5, 0.1875, ((2, 4),)),
        "out_weight": scatter_about(streams_of[3], (HEADS * HEAD_DIM, D), (HEADS * HEAD_DIM) ** -0.5, 0.1875, ((0, 4),)),
        "up_gate_weight": scatter_about(streams_of[4], (2, D, FF), D ** -0.5, 0.1875, ((2, 4),)),
        "down_weight": scatter_about(streams_of[5], (FF, D), FF ** -0.5, 0.09375, ((0, 4),)),
        "qk_scale": jnp.clip(jnp.exp(math.log(1.8) - 0.6931472 * jax.random.uniform(streams_of[6], (HEADS * HEAD_DIM,), jnp.float32) ** levels(streams_of[6], (HEADS * HEAD_DIM,), ((0, 4),), -0.2, 0.2)), 0.9, 1.8),
        "mlp_scale": jnp.clip(jnp.exp(math.log(2.0) - 1.3862944 * jax.random.uniform(streams_of[7], (2, FF), jnp.float32) ** levels(streams_of[7], (2, FF), ((1, 4),), -0.2, 0.2)), 0.5, 2.0),
        "eigen_rates": jnp.clip(jnp.exp(jax.random.uniform(streams_of[8], (D, 2), jnp.float32, math.log(0.05), math.log(0.6))), 0.05, 0.6),
        "cotangent": scatter_about(streams_of[9], (N_BATCH, TOK_DEV, D), 1.0, 6.0, ((0, 8), (1, 4))),
        "block_order": jax.vmap(lambda own: jax.random.permutation(own, NBLK))(jax.random.split(streams_of[10], N_HEAD)).reshape((N_HEAD, NBLK)).astype(jnp.int32),
        "master_blocks": scatter_about(streams_of[11], (N_HEAD, NBLK, BLOCK, BLOCK), D ** -0.5, 0.1875, ((0, 4), (1, 8)), jnp.float32),
        "ema_blocks": scatter_about(streams_of[12], (N_HEAD, NBLK, BLOCK, BLOCK), D ** -0.5, 0.1875, ((0, 4), (1, 8)), jnp.float32),
        "left_stats": draw_left_stats(jax.random.fold_in(streams_of[17], 71), 0),
        "right_stats": draw_right_stats(jax.random.fold_in(streams_of[17], 71), 0),
        "left_root": draw_left_root(jax.random.fold_in(streams_of[17], 71), 0),
        "right_root": draw_right_root(jax.random.fold_in(streams_of[17], 71), 0),
    }


@jax.custom_vjp
def low(v):
    return lax.optimization_barrier(v.astype(jnp.bfloat16)).astype(jnp.float32)

@jax.custom_vjp
def low_back(v):
    return v

def low_keep(v):
    return (low(v), None)

def low_pass(kept, grad):
    return (grad,)

def back_keep(v):
    return (v, None)

def back_low(kept, grad):
    return (low(grad),)
low.defvjp(low_keep, low_pass)
low_back.defvjp(back_keep, back_low)

def rms_rows(value):
    return value * lax.rsqrt(lax.optimization_barrier(jnp.mean(value * value, axis=-1, keepdims=True)) + 1e-06)

def positions_of(lengths_row, total_rows):
    ends = jnp.cumsum(lengths_row).astype(jnp.int32)
    starts = ends - lengths_row
    index = jnp.arange(total_rows, dtype=jnp.int32)
    segment = lax.optimization_barrier(jnp.sum((index[:, None] >= ends[None, :]).astype(jnp.int32), axis=1))
    member = (segment[:, None] == jnp.arange(lengths_row.shape[0], dtype=jnp.int32)[None, :]).astype(jnp.int32)
    begin = lax.optimization_barrier(jnp.sum(member * starts[None, :], axis=1))
    return (segment, index - begin)

def rotate(value, positions, direction):
    half = HEAD_DIM // 2
    freq = 10000.0 ** (-jnp.arange(half, dtype=jnp.float32) * 2.0 / HEAD_DIM)
    angle = positions.astype(jnp.float32)[:, None] * freq[None, :]
    cosine = jnp.cos(angle)[:, None, :]
    sine = jnp.sin(angle)[:, None, :] * direction
    first = value[..., :half]
    second = value[..., half:]
    return jnp.concatenate([first * cosine - second * sine, second * cosine + first * sine], axis=-1)

def buffer_forward(x_rows, lengths_row, weights):
    precise = lax.Precision.HIGHEST
    w_query, w_key, w_value, w_out, w_up, w_gate, w_down, gain_qk, scale_up, scale_gate, rates = weights
    segment, positions = positions_of(lengths_row, TOK_DEV)
    shape_heads = (TOK_DEV, HEADS, HEAD_DIM)
    query = low_back(jnp.dot(x_rows, w_query, precision=precise))
    keys = low_back(jnp.dot(x_rows, w_key, precision=precise))
    values = low(low_back(jnp.dot(x_rows, w_value, precision=precise))).reshape(shape_heads)
    gains = gain_qk.reshape(HEADS, HEAD_DIM)
    q_used = low(rms_rows(rotate(query.reshape(shape_heads), positions, 1.0)) * gains)
    k_used = low(rms_rows(rotate(keys.reshape(shape_heads), positions, 1.0)) * gains)
    block_rows = min(512, TOK_DEV)
    key_index = jnp.arange(TOK_DEV, dtype=jnp.int32)

    def attend(offset):
        q_block = lax.dynamic_slice_in_dim(q_used, offset, block_rows, 0)
        seg_block = lax.dynamic_slice_in_dim(segment, offset, block_rows, 0)
        row_index = offset + jnp.arange(block_rows, dtype=jnp.int32)
        scores = low_back(jnp.einsum('qhd,khd->hqk', q_block, k_used, precision=precise) / math.sqrt(HEAD_DIM))
        allowed = (seg_block[:, None] == segment[None, :]) & (key_index[None, :] <= row_index[:, None])
        scores = jnp.where(allowed[None], scores, -1e+30)
        probs = low(jax.nn.softmax(scores, axis=-1))
        return jnp.einsum('hqk,khd->qhd', probs, values, precision=precise)
    offsets = jnp.arange(TOK_DEV // block_rows, dtype=jnp.int32) * block_rows
    attn_out = lax.map(jax.checkpoint(attend), offsets).reshape(TOK_DEV, HEADS * HEAD_DIM)
    attn_out = low(low_back(attn_out))
    branch_attn = low_back(jnp.dot(attn_out, w_out, precision=precise))
    h_attn = rms_rows(branch_attn)
    hidden_state = rms_rows(x_rows + rates[:, 0] * (h_attn - x_rows))
    hidden_low = low(hidden_state)
    up_raw = low_back(jnp.dot(hidden_low, w_up, precision=precise))
    gate_raw = low_back(jnp.dot(hidden_low, w_gate, precision=precise))
    up_proj = up_raw * scale_up
    gate_proj = gate_raw * scale_gate
    mixed = low(up_proj * jax.nn.silu(gate_proj))
    branch_mlp = low_back(jnp.dot(mixed, w_down, precision=precise))
    h_mlp = rms_rows(branch_mlp)
    return rms_rows(hidden_state + rates[:, 1] * (h_mlp - hidden_state))

def reference(tokens, seq_lengths, qkv_weight, out_weight, up_gate_weight, down_weight, qk_scale, mlp_scale, eigen_rates, cotangent, block_order, master_blocks, ema_blocks, left_stats, right_stats, left_root, right_root):
    precise = lax.Precision.HIGHEST
    qkv_full = qkv_weight.astype(jnp.float32)
    ug_full = up_gate_weight.astype(jnp.float32)
    weights = (qkv_full[0], qkv_full[1], qkv_full[2], out_weight.astype(jnp.float32), ug_full[0], ug_full[1], down_weight.astype(jnp.float32), qk_scale, mlp_scale[0], mlp_scale[1], eigen_rates)
    x_all = tokens.astype(jnp.float32)
    one_buffer = jax.checkpoint(buffer_forward)

    def forward(weight_set, inputs):
        return lax.map(lambda item: one_buffer(item[0], item[1], weight_set), (inputs, seq_lengths))
    block_out, pullback = jax.vjp(forward, weights, x_all)
    grads, input_grad = pullback(cotangent.astype(jnp.float32))
    g_query, g_key, g_value, g_out, g_up, g_gate, g_down, g_qk, g_su, g_sv, g_rates = grads
    hd_dev = HEADS * HEAD_DIM // N_HEAD
    ff_dev = FF // N_HEAD
    stacked = []
    for group in range(N_HEAD):
        c_low = group * hd_dev
        f_low = group * ff_dev
        matrix = jnp.concatenate([g_query[:, c_low:c_low + hd_dev], g_key[:, c_low:c_low + hd_dev], g_value[:, c_low:c_low + hd_dev], g_out[c_low:c_low + hd_dev, :].T, g_up[:, f_low:f_low + ff_dev], g_gate[:, f_low:f_low + ff_dev], g_down[f_low:f_low + ff_dev, :].T], axis=1)
        blocks = matrix.reshape(D // BLOCK, BLOCK, NCOL_DEV // BLOCK, BLOCK).transpose(2, 0, 1, 3).reshape(NBLK, BLOCK, BLOCK)
        stacked.append(jnp.take(blocks, block_order[group], axis=0))
    grad_blocks = jnp.stack(stacked)
    new_left = 0.5 * left_stats + 0.5 * jnp.einsum('hsij,hskj->hsik', grad_blocks, grad_blocks, precision=precise)
    new_right = 0.5 * right_stats + 0.5 * jnp.einsum('hsji,hsjk->hsik', grad_blocks, grad_blocks, precision=precise)
    direction = jnp.einsum('hsij,hsjk->hsik', left_root, grad_blocks, precision=precise)
    direction = jnp.einsum('hsij,hsjk->hsik', direction, right_root, precision=precise)
    stepped = master_blocks - 0.3 * direction
    column_sq = lax.optimization_barrier(jnp.sum(stepped * stepped, axis=2))
    panel_of = block_order // (D // BLOCK)
    member = (panel_of[..., None] == jnp.arange(NCOL_DEV // BLOCK, dtype=jnp.int32)).astype(jnp.float32)
    totals = jnp.einsum('hsp,hsb->hpb', member, column_sq, precision=precise)
    norms = jnp.einsum('hsp,hpb->hsb', member, totals, precision=precise)
    new_master = stepped * lax.rsqrt(norms + 1e-06)[:, :, None, :]
    new_ema = 0.5 * ema_blocks + 0.5 * new_master
    gain_step = 0.5 / math.sqrt(TOKENS)
    g_mlp = jnp.stack([g_su, g_sv])
    mlp_scale_out = jnp.stack([g_mlp, mlp_scale - gain_step * g_mlp])
    new_gains = jnp.concatenate([(qk_scale - gain_step * g_qk)[None, :], (eigen_rates - gain_step * g_rates).T], axis=0)
    return (block_out, input_grad, grad_blocks, new_master, new_ema, new_left, new_right, g_qk, mlp_scale_out, g_rates, new_gains)
```

```python
import functools
import math

import jax
import jax.numpy as jnp
from jax import lax
from jax.experimental import pallas as pl
from jax.experimental.pallas import tpu as pltpu
from jax.sharding import PartitionSpec as P

HEAD_DIM = 64
BLOCK = 128
LANES = 128
CHUNKS = 2
F32 = jnp.float32
BF16 = jnp.bfloat16
NN = (((1,), (0,)), ((), ()))
NT = (((1,), (1,)), ((), ()))
TN = (((0,), (0,)), ((), ()))


def mm(a, b, dims=NN):
    return lax.dot_general(a, b, dims, preferred_element_type=F32)


def whole(shape, single=False):
    zeros = (0,) * len(shape)
    if single:
        return pl.BlockSpec(shape, lambda *_: zeros, pipeline_mode=pl.Buffered(1))
    return pl.BlockSpec(shape, lambda *_: zeros)


def rms_rows(value):
    return value * lax.rsqrt(jnp.mean(value * value, axis=-1, keepdims=True) + 1e-06)


def rms_factor(value):
    return lax.rsqrt(jnp.mean(value * value, axis=-1, keepdims=True) + 1e-06)


def rms_back(normed, factor, gradient):
    return factor * (gradient - normed * jnp.mean(gradient * normed, axis=-1, keepdims=True))


def lane_ids():
    return lax.broadcasted_iota(jnp.int32, (1, LANES), 1)


def head_mean(value, ones_block):
    high = value.astype(BF16)
    rest = (value - high.astype(F32)).astype(BF16)
    return (mm(high, ones_block) + mm(rest, ones_block)) * (1.0 / HEAD_DIM)


def ones_block():
    row = lax.broadcasted_iota(jnp.int32, (LANES, LANES), 0) // HEAD_DIM
    col = lax.broadcasted_iota(jnp.int32, (LANES, LANES), 1) // HEAD_DIM
    return jnp.where(row == col, 1.0, 0.0).astype(BF16)


def half_turn(value):
    first = (lane_ids() & (HEAD_DIM - 1)) < HEAD_DIM // 2
    return jnp.where(
        first,
        pltpu.roll(value, LANES - HEAD_DIM // 2, 1),
        pltpu.roll(value, HEAD_DIM // 2, 1),
    )


def angles(tile, near_ref, far_ref):
    cos_r, sin_r = near_ref[0], near_ref[1]
    cos_0 = far_ref[0, pl.ds(tile, 1), :]
    sin_0 = far_ref[1, pl.ds(tile, 1), :]
    first = (lane_ids() & (HEAD_DIM - 1)) < HEAD_DIM // 2
    sine = sin_0 * cos_r + cos_0 * sin_r
    return cos_0 * cos_r - sin_0 * sin_r, jnp.where(first, -sine, sine)


def project_kernel(
    x_ref, w_ref, gain_ref, near_ref, far_ref, q_ref, k_ref, v_ref, q_rot_ref, k_rot_ref
):
    tile = pl.program_id(0)
    cosine, sine = angles(tile, near_ref, far_ref)
    ones = ones_block()
    x = x_ref[...]
    for index, used_ref, rot_ref in ((0, q_ref, q_rot_ref), (1, k_ref, k_rot_ref)):
        raw = mm(x, w_ref[index])
        for pair in range(raw.shape[1] // LANES):
            lanes = slice(pair * LANES, (pair + 1) * LANES)
            value = raw[:, lanes]
            turned = value * cosine + half_turn(value) * sine
            factor = lax.rsqrt(head_mean(turned * turned, ones) + 1e-06)
            rot_ref[:, lanes] = turned
            used_ref[:, lanes] = (turned * factor * gain_ref[:, lanes]).astype(BF16)
    v_ref[...] = mm(x, w_ref[2]).astype(BF16)


def project(x, weight, gains, near, far):
    rows, width = x.shape
    cols = weight.shape[2]
    tile = near.shape[1]
    by_row = lambda w: pl.BlockSpec((tile, w), lambda i: (i, 0))
    return pl.pallas_call(
        project_kernel,
        grid=(rows // tile,),
        in_specs=[
            by_row(width),
            whole(weight.shape, True),
            whole((1, cols)),
            whole(near.shape),
            whole(far.shape),
        ],
        out_specs=[by_row(cols)] * 5,
        out_shape=[jax.ShapeDtypeStruct((rows, cols), BF16)] * 3
        + [jax.ShapeDtypeStruct((rows, cols), F32)] * 2,
        name="project",
    )(x, weight, gains, near, far)


def key_tiles(first_row, start, wide, narrow, visit):
    full = first_row // wide

    def step(index, carry):
        visit(pl.multiple_of(index * wide, wide), wide, False)
        return carry

    lax.fori_loop(start // wide, full, step, 0)
    diagonal = (first_row // narrow) * narrow

    @pl.when(diagonal > full * wide)
    def _():
        visit(pl.multiple_of(full * wide, narrow), narrow, False)

    visit(pl.multiple_of(diagonal, narrow), narrow, True)


def attend_kernel(
    half, wide, tiles, starts, q_ref, k_ref, v_ref, w_ref, o_ref, lse_ref, send_ref, keep_ref, acc
):
    index = pl.program_id(0)
    rows = q_ref.shape[0]
    first_row = tiles[index] * rows
    start = starts[index]
    narrow = wide // 2
    low = lane_ids() < HEAD_DIM
    zero = jnp.zeros((), BF16)
    results = []
    for pair in range(q_ref.shape[1] // LANES):
        lanes = slice(pair * LANES, (pair + 1) * LANES)
        q = q_ref[:, lanes] * jnp.asarray(1.0 / math.sqrt(HEAD_DIM), BF16)
        q_both = jnp.concatenate([jnp.where(low, q, zero), jnp.where(low, zero, q)], axis=0)
        acc[...] = jnp.zeros_like(acc)

        def visit(key_0, size, masked):
            keys = pl.ds(key_0, size)
            weights = jnp.exp(mm(q_both, k_ref[keys, lanes], NT))
            if masked:
                row = lax.broadcasted_iota(jnp.int32, (2 * rows, size), 0)
                row = jnp.where(row < rows, row, row - rows) + first_row
                col = lax.broadcasted_iota(jnp.int32, (2 * rows, size), 1) + key_0
                weights = jnp.where((col <= row) & (col >= start), weights, 0.0)
            total = weights[:, :LANES]
            for part in range(1, size // LANES):
                total = total + weights[:, part * LANES : (part + 1) * LANES]
            acc[:, LANES:] += total
            acc[:, :LANES] += mm(weights.astype(BF16), v_ref[keys, lanes])

        key_tiles(first_row, start, wide, narrow, visit)
        total_a = jnp.sum(acc[:rows, LANES:], axis=1, keepdims=True)
        total_b = jnp.sum(acc[rows:, LANES:], axis=1, keepdims=True)
        summed = jnp.where(low, acc[:rows, :LANES], acc[rows:, :LANES])
        out = (summed / jnp.where(low, total_a, total_b)).astype(BF16)
        o_ref[:, lanes] = out
        lse_ref[:, lanes] = jnp.log(jnp.where(low, total_b, total_a))
        results.append(out)
    part = mm(jnp.concatenate(results, axis=1), w_ref[...]).astype(BF16)

    @pl.when(index < half)
    def _():
        send_ref[...] = part

    @pl.when(index >= half)
    def _():
        keep_ref[...] = part


def attend(q, k, v, weight, tiles, starts, rows):
    count = tiles.shape[0]
    half = count // 2
    total, cols = k.shape
    width = weight.shape[1]
    at_tile = pl.BlockSpec((rows, cols), lambda i, t, s: (t[i], 0))
    at_step = pl.BlockSpec((rows, cols), lambda i, t, s: (i, 0))
    return pl.pallas_call(
        functools.partial(attend_kernel, half, 2 * BLOCK * 2),
        grid_spec=pltpu.PrefetchScalarGridSpec(
            num_scalar_prefetch=2,
            grid=(count,),
            in_specs=[at_tile, whole(k.shape), whole(v.shape), whole(weight.shape)],
            out_specs=[
                at_step,
                at_step,
                pl.BlockSpec((rows, width), lambda i, t, s: (jnp.minimum(i, half - 1), 0)),
                pl.BlockSpec((rows, width), lambda i, t, s: (jnp.maximum(i - half, 0), 0)),
            ],
            scratch_shapes=[pltpu.VMEM((2 * rows, 2 * LANES), F32)],
        ),
        out_shape=[
            jax.ShapeDtypeStruct((count * rows, cols), BF16),
            jax.ShapeDtypeStruct((count * rows, cols), F32),
            jax.ShapeDtypeStruct((half * rows, width), BF16),
            jax.ShapeDtypeStruct((half * rows, width), BF16),
        ],
        name="attend",
    )(tiles, starts, q, k, v, weight)


def attend_back_kernel(blocks, wide, tiles, starts, *refs):
    row_refs = refs[:blocks]
    q_ref, k_ref, v_ref, o_ref, lse_ref, w_ref = refs[blocks : blocks + 6]
    dq_ref, dk_ref, dv_ref, dw_ref, rows_s, acc = refs[blocks + 6 :]
    index = pl.program_id(0)
    rows = q_ref.shape[0]
    narrow = wide // 2

    @pl.when(index == 0)
    def _():
        dk_ref[...] = jnp.zeros_like(dk_ref)
        dv_ref[...] = jnp.zeros_like(dv_ref)
        dw_ref[...] = jnp.zeros_like(dw_ref)

    for block in range(blocks):

        @pl.when(index == block)
        def _(block=block):
            rows_s[...] = row_refs[block][...]

    first_row = tiles[index] * rows
    start = starts[index]
    low = lane_ids() < HEAD_DIM
    place = lane_ids() & (HEAD_DIM - 1)
    zero = jnp.zeros((), BF16)
    ones = jnp.where(place < 3, 1.0, 0.0).astype(BF16)

    def parts(value):
        high = value.astype(BF16).astype(F32)
        rest = value - high
        middle = rest.astype(BF16).astype(F32)
        picked = jnp.where(place == 1, middle, jnp.where(place == 2, rest - middle, 0.0))
        return jnp.where(place == 0, high, picked).astype(BF16)

    d_rows = rows_s[...]
    d_attn = mm(d_rows, w_ref[...], NT).astype(BF16)
    dw_ref[...] += mm(d_rows, o_ref[...], TN)
    for pair in range(q_ref.shape[1] // LANES):
        lanes = slice(pair * LANES, (pair + 1) * LANES)
        q = q_ref[:, lanes] * jnp.asarray(1.0 / math.sqrt(HEAD_DIM), BF16)
        d_out = d_attn[:, lanes]
        minus_lse = parts(-lse_ref[:, lanes])
        product = d_out.astype(F32) * o_ref[:, lanes].astype(F32)
        sum_a = jnp.sum(jnp.where(low, product, 0.0), axis=1, keepdims=True)
        sum_b = jnp.sum(jnp.where(low, 0.0, product), axis=1, keepdims=True)
        minus_delta = parts(-jnp.where(low, sum_b, sum_a))
        q_ext = (jnp.where(low, q, minus_lse), jnp.where(low, minus_lse, q))
        d_ext = (jnp.where(low, d_out, minus_delta), jnp.where(low, minus_delta, d_out))
        q_both = jnp.concatenate([jnp.where(low, q, zero), jnp.where(low, zero, q)], axis=0)
        d_both = jnp.concatenate(
            [jnp.where(low, d_out, zero), jnp.where(low, zero, d_out)], axis=0
        )
        acc[...] = jnp.zeros_like(acc)

        def visit(key_0, size, masked):
            keys = pl.ds(key_0, size)
            k = k_ref[keys, lanes]
            v = v_ref[keys, lanes]
            k_ext = (jnp.where(low, k, ones), jnp.where(low, ones, k))
            v_ext = (jnp.where(low, v, ones), jnp.where(low, ones, v))
            if masked:
                col = lax.broadcasted_iota(jnp.int32, (size, rows), 1) + first_row
                row = lax.broadcasted_iota(jnp.int32, (size, rows), 0) + key_0
                allowed = (row <= col) & (row >= start)
            probs = []
            d_scores = []
            for head in range(2):
                prob = jnp.exp(mm(k_ext[head], q_ext[head], NT))
                if masked:
                    prob = jnp.where(allowed, prob, 0.0)
                d_score = prob * mm(v_ext[head], d_ext[head], NT)
                probs.append(prob.astype(BF16))
                d_scores.append(d_score.astype(BF16))
            dv_ref[keys, lanes] += mm(jnp.concatenate(probs, axis=1), d_both)
            dk_ref[keys, lanes] += mm(jnp.concatenate(d_scores, axis=1), q_both)
            k_both = jnp.concatenate([jnp.where(low, k, zero), jnp.where(low, zero, k)], axis=0)
            acc[...] += mm(jnp.concatenate(d_scores, axis=0), k_both, TN)

        key_tiles(first_row, start, wide, narrow, visit)
        dq_ref[:, lanes] = acc[...] * (1.0 / math.sqrt(HEAD_DIM))


def attend_back(row_blocks, q, k, v, o, lse, weight, tiles, starts, rows):
    count = tiles.shape[0]
    total, cols = k.shape
    width = weight.shape[1]
    at_tile = pl.BlockSpec((rows, cols), lambda i, t, s: (t[i], 0))
    at_step = pl.BlockSpec((rows, cols), lambda i, t, s: (i, 0))
    return pl.pallas_call(
        functools.partial(attend_back_kernel, len(row_blocks), 2 * BLOCK * 2),
        grid_spec=pltpu.PrefetchScalarGridSpec(
            num_scalar_prefetch=2,
            grid=(count,),
            in_specs=[whole(b.shape, True) for b in row_blocks]
            + [at_tile, whole(k.shape), whole(v.shape), at_step, at_step, whole(weight.shape)],
            out_specs=[at_step, whole(k.shape), whole(k.shape), whole((width, cols))],
            scratch_shapes=[pltpu.VMEM((rows, width), BF16), pltpu.VMEM((rows, LANES), F32)],
        ),
        out_shape=[
            jax.ShapeDtypeStruct((count * rows, cols), F32),
            jax.ShapeDtypeStruct((total, cols), F32),
            jax.ShapeDtypeStruct((total, cols), F32),
            jax.ShapeDtypeStruct((width, cols), F32),
        ],
        name="attend_back",
    )(tiles, starts, *row_blocks, q, k, v, o, lse, weight)


def sum_parts(refs):
    total = refs[0][...].astype(F32)
    for ref in refs[1:]:
        total = total + ref[...].astype(F32)
    return total


def join_attention_kernel(parts, place, *refs):
    x_ref, rate_ref = refs[parts : parts + 2]
    low_ref, hidden_ref, branch_ref = refs[parts + 2 :]
    branch = sum_parts(refs[:parts])
    x = x_ref[...].astype(F32)
    hidden = rms_rows(x + rate_ref[0:1] * (rms_rows(branch) - x))
    branch_ref[...] = branch
    hidden_ref[...] = hidden
    low_ref[...] = hidden.astype(BF16)


def part_specs(parts, rows, width):
    return [
        pl.BlockSpec((rows, width), lambda i, p, last=a.shape[0] // rows: (last - SUB + i, 0))
        for a in parts
    ]


SUB = 4


def join_attention(parts, x, place, rates, share):
    width = x.shape[1]
    rows = share // SUB
    here = pl.BlockSpec((rows, width), lambda i, p: (i, 0))
    return pl.pallas_call(
        functools.partial(join_attention_kernel, len(parts)),
        grid_spec=pltpu.PrefetchScalarGridSpec(
            num_scalar_prefetch=1,
            grid=(SUB,),
            in_specs=part_specs(parts, rows, width)
            + [pl.BlockSpec((rows, width), lambda i, p: (p[0] * SUB + i, 0)), whole(rates.shape)],
            out_specs=[here] * 3,
        ),
        out_shape=[
            jax.ShapeDtypeStruct((share, width), BF16),
            jax.ShapeDtypeStruct((share, width), F32),
            jax.ShapeDtypeStruct((share, width), F32),
        ],
        name="join_attention",
    )(place, *parts, x, rates)


def mlp_kernel(blocks, *refs):
    row_refs = refs[:blocks]
    w_ref, down_ref, scale_ref = refs[blocks : blocks + 3]
    full_ref, up_ref, gate_ref, mixed_ref, send_ref, keep_ref = refs[blocks + 3 :]
    index = pl.program_id(0)
    half = blocks // 2
    rows = row_refs[0].shape[0]
    for side in range(2):

        @pl.when(index == side)
        def _(side=side):
            for block in range(half):
                full_ref[block * rows : (block + 1) * rows] = row_refs[side * half + block][...]

    x = full_ref[...]
    cols = w_ref.shape[2]
    step = 2 * BLOCK
    for col in range(0, cols, step):
        lanes = slice(col, col + step)
        up = mm(x, w_ref[0, :, lanes])
        gate = mm(x, w_ref[1, :, lanes])
        up_ref[:, lanes] = up.astype(BF16)
        gate_ref[:, lanes] = gate.astype(BF16)
        scaled = gate * scale_ref[1:2, lanes]
        mixed_ref[:, lanes] = (
            up * scale_ref[0:1, lanes] * (scaled * jax.nn.sigmoid(scaled))
        ).astype(BF16)
    part = mm(mixed_ref[...], down_ref[...]).astype(BF16)

    @pl.when(index == 0)
    def _():
        send_ref[...] = part

    @pl.when(index == 1)
    def _():
        keep_ref[...] = part


def mlp(row_blocks, weight, down, scale):
    rows, width = row_blocks[0].shape
    side = rows * len(row_blocks) // 2
    cols = weight.shape[2]
    at_step = lambda w: pl.BlockSpec((side, w), lambda i: (i, 0))
    return pl.pallas_call(
        functools.partial(mlp_kernel, len(row_blocks)),
        grid=(2,),
        in_specs=[whole(b.shape, True) for b in row_blocks]
        + [whole(weight.shape, True), whole(down.shape, True), whole(scale.shape)],
        out_specs=[at_step(width), at_step(cols), at_step(cols), at_step(cols)]
        + [whole((side, width))] * 2,
        out_shape=[jax.ShapeDtypeStruct((2 * side, width), BF16)]
        + [jax.ShapeDtypeStruct((2 * side, cols), BF16)] * 3
        + [jax.ShapeDtypeStruct((side, width), BF16)] * 2,
        name="mlp",
    )(*row_blocks, weight, down, scale)


def join_mlp_kernel(parts, *refs):
    hidden_ref, cot_ref, rate_ref = refs[parts : parts + 3]
    out_ref, low_ref, d_hidden_ref, rate_grad_ref = refs[parts + 3 :]
    branch = sum_parts(refs[:parts])
    hidden = hidden_ref[...]
    rate = rate_ref[1:2]
    factor = rms_factor(branch)
    normed = branch * factor
    gap = normed - hidden
    before = hidden + rate * gap
    factor_out = rms_factor(before)
    out = before * factor_out
    d_before = rms_back(out, factor_out, cot_ref[...].astype(F32))
    out_ref[...] = out
    d_hidden_ref[...] = (1.0 - rate) * d_before
    low_ref[...] = rms_back(normed, factor, rate * d_before).astype(BF16)

    @pl.when(pl.program_id(0) == 0)
    def _():
        rate_grad_ref[...] = jnp.zeros_like(rate_grad_ref)

    rate_grad_ref[...] += jnp.sum(d_before * gap, axis=0, keepdims=True)


def join_mlp(parts, hidden, cotangent, chunk, rates, share):
    width = hidden.shape[1]
    rows = share // SUB
    here = pl.BlockSpec((rows, width), lambda i, p: (i, 0))
    return pl.pallas_call(
        lambda p, *refs: join_mlp_kernel(len(parts), *refs),
        grid_spec=pltpu.PrefetchScalarGridSpec(
            num_scalar_prefetch=1,
            grid=(SUB,),
            in_specs=part_specs(parts, rows, width)
            + [
                here,
                pl.BlockSpec((rows, width), lambda i, p: (chunk * SUB + i, 0)),
                whole(rates.shape),
            ],
            out_specs=[here] * 3 + [whole((1, width))],
        ),
        out_shape=[
            jax.ShapeDtypeStruct((share, width), F32),
            jax.ShapeDtypeStruct((share, width), BF16),
            jax.ShapeDtypeStruct((share, width), F32),
            jax.ShapeDtypeStruct((1, width), F32),
        ],
        name="join_mlp",
    )(jnp.zeros((1,), jnp.int32), *parts, hidden, cotangent, rates)


def mlp_back_kernel(blocks, *refs):
    row_refs = refs[:blocks]
    up_ref, gate_ref, w_ref, down_ref, scale_ref = refs[blocks : blocks + 5]
    full_ref, d_up_ref, d_gate_ref, sums_ref, send_ref, keep_ref = refs[blocks + 5 :]
    index = pl.program_id(0)
    half = blocks // 2
    rows = row_refs[0].shape[0]
    for side in range(2):

        @pl.when(index == side)
        def _(side=side):
            for block in range(half):
                full_ref[block * rows : (block + 1) * rows] = row_refs[side * half + block][...]

    @pl.when(index == 0)
    def _():
        sums_ref[...] = jnp.zeros_like(sums_ref)

    d_rows = full_ref[...]
    cols = w_ref.shape[2]
    step = 2 * BLOCK
    for col in range(0, cols, step):
        lanes = slice(col, col + step)
        d_mixed = mm(d_rows, down_ref[lanes, :], NT)
        up_raw = up_ref[:, lanes].astype(F32)
        gate_raw = gate_ref[:, lanes].astype(F32)
        scale_up = scale_ref[0:1, lanes]
        scale_gate = scale_ref[1:2, lanes]
        gate = gate_raw * scale_gate
        sig = jax.nn.sigmoid(gate)
        d_up = d_mixed * (gate * sig)
        d_gate = d_mixed * (up_raw * scale_up) * (sig * (1.0 + gate * (1.0 - sig)))
        sums_ref[0:1, lanes] += jnp.sum(d_up * up_raw, axis=0, keepdims=True)
        sums_ref[1:2, lanes] += jnp.sum(d_gate * gate_raw, axis=0, keepdims=True)
        d_up_ref[:, lanes] = (d_up * scale_up).astype(BF16)
        d_gate_ref[:, lanes] = (d_gate * scale_gate).astype(BF16)
    part = (mm(d_up_ref[...], w_ref[0], NT) + mm(d_gate_ref[...], w_ref[1], NT)).astype(BF16)

    @pl.when(index == 0)
    def _():
        send_ref[...] = part

    @pl.when(index == 1)
    def _():
        keep_ref[...] = part


def mlp_back(row_blocks, up, gate, weight, down, scale):
    rows, width = row_blocks[0].shape
    side = rows * len(row_blocks) // 2
    cols = weight.shape[2]
    at_step = lambda w: pl.BlockSpec((side, w), lambda i: (i, 0))
    return pl.pallas_call(
        functools.partial(mlp_back_kernel, len(row_blocks)),
        grid=(2,),
        in_specs=[whole(b.shape, True) for b in row_blocks]
        + [
            at_step(cols),
            at_step(cols),
            whole(weight.shape, True),
            whole(down.shape, True),
            whole(scale.shape),
        ],
        out_specs=[at_step(width), at_step(cols), at_step(cols), whole(scale.shape)]
        + [whole((side, width))] * 2,
        out_shape=[jax.ShapeDtypeStruct((2 * side, width), BF16)]
        + [jax.ShapeDtypeStruct((2 * side, cols), BF16)] * 2
        + [jax.ShapeDtypeStruct(scale.shape, F32)]
        + [jax.ShapeDtypeStruct((side, width), BF16)] * 2,
        name="mlp_back",
    )(*row_blocks, up, gate, weight, down, scale)


def split_attention_kernel(parts, place, *refs):
    d_hidden_ref, hidden_ref, branch_ref, x_ref, rate_ref = refs[parts : parts + 5]
    low_ref, d_input_ref, rate_grad_ref = refs[parts + 5 :]
    d_hidden = sum_parts(refs[:parts]) + d_hidden_ref[...]
    hidden = hidden_ref[...]
    branch = branch_ref[...]
    x = x_ref[...].astype(F32)
    rate = rate_ref[0:1]
    factor = rms_factor(branch)
    normed = branch * factor
    gap = normed - x
    d_before = rms_back(hidden, rms_factor(x + rate * gap), d_hidden)
    d_input_ref[...] = (1.0 - rate) * d_before
    low_ref[...] = rms_back(normed, factor, rate * d_before).astype(BF16)

    @pl.when(pl.program_id(0) == 0)
    def _():
        rate_grad_ref[...] = jnp.zeros_like(rate_grad_ref)

    rate_grad_ref[...] += jnp.sum(d_before * gap, axis=0, keepdims=True)


def split_attention(parts, d_hidden, hidden, branch, x, place, rates, share):
    width = x.shape[1]
    rows = share // SUB
    here = pl.BlockSpec((rows, width), lambda i, p: (i, 0))
    return pl.pallas_call(
        functools.partial(split_attention_kernel, len(parts)),
        grid_spec=pltpu.PrefetchScalarGridSpec(
            num_scalar_prefetch=1,
            grid=(SUB,),
            in_specs=part_specs(parts, rows, width)
            + [here] * 3
            + [pl.BlockSpec((rows, width), lambda i, p: (p[0] * SUB + i, 0)), whole(rates.shape)],
            out_specs=[here] * 2 + [whole((1, width))],
        ),
        out_shape=[
            jax.ShapeDtypeStruct((share, width), BF16),
            jax.ShapeDtypeStruct((share, width), F32),
            jax.ShapeDtypeStruct((1, width), F32),
        ],
        name="split_attention",
    )(place, *parts, d_hidden, hidden, branch, x, rates)


def project_back_kernel(order, *refs):
    (
        x_ref,
        q_rot_ref,
        k_rot_ref,
        w_ref,
        gain_ref,
        near_ref,
        far_ref,
    ) = refs[:7]
    dq_refs = refs[7 : 7 + CHUNKS]
    dk_refs = refs[7 + CHUNKS : 7 + 2 * CHUNKS]
    dv_refs = refs[7 + 2 * CHUNKS : 7 + 3 * CHUNKS]
    send_ref, keep_ref, gain_grad_ref, grad_ref, acc = refs[7 + 3 * CHUNKS :]
    index = pl.program_id(0)
    count = pl.num_programs(0)

    @pl.when(index == 0)
    def _():
        gain_grad_ref[...] = jnp.zeros_like(gain_grad_ref)
        acc[...] = jnp.zeros_like(acc)

    tile = order[index]
    cosine, sine = angles(tile, near_ref, far_ref)
    ones = ones_block()
    cols = q_rot_ref.shape[1]
    chunk = index % CHUNKS
    dq = dq_refs[0][...]
    for other in range(1, CHUNKS):
        dq = jnp.where(chunk == other, dq_refs[other][...], dq)
    d_raw = []
    for used, rot_ref in ((dq, q_rot_ref), (sum_parts(dk_refs), k_rot_ref)):
        for pair in range(cols // LANES):
            lanes = slice(pair * LANES, (pair + 1) * LANES)
            turned = rot_ref[:, lanes]
            factor = lax.rsqrt(head_mean(turned * turned, ones) + 1e-06)
            normed = turned * factor
            d_used = used[:, lanes]
            gain_grad_ref[:, lanes] += jnp.sum(d_used * normed, axis=0, keepdims=True)
            d_normed = d_used * gain_ref[:, lanes]
            d_turned = factor * (d_normed - normed * head_mean(d_normed * normed, ones))
            d_raw.append((d_turned * cosine - half_turn(d_turned) * sine).astype(BF16))
    d_raw.append(sum_parts(dv_refs).astype(BF16))
    d_all = jnp.concatenate(d_raw, axis=1)
    part = mm(d_all[:, :cols], w_ref[0], NT)
    part = part + mm(d_all[:, cols : 2 * cols], w_ref[1], NT)
    part = (part + mm(d_all[:, 2 * cols :], w_ref[2], NT)).astype(BF16)
    acc[...] += mm(x_ref[...], d_all, TN)

    @pl.when(index < count // 2)
    def _():
        send_ref[...] = part

    @pl.when(index >= count // 2)
    def _():
        keep_ref[...] = part

    @pl.when(index == count - 1)
    def _():
        grad_ref[...] = acc[...].astype(BF16)


def project_back(x, q_rot, k_rot, weight, gains, near, far, dq, dk, dv, order, rows):
    total, width = x.shape
    cols = weight.shape[2]
    count = order.shape[0]
    half = count // 2
    at_tile = lambda w: pl.BlockSpec((rows, w), lambda i, t: (t[i], 0))
    return pl.pallas_call(
        project_back_kernel,
        grid_spec=pltpu.PrefetchScalarGridSpec(
            num_scalar_prefetch=1,
            grid=(count,),
            in_specs=[
                at_tile(width),
                at_tile(cols),
                at_tile(cols),
                whole(weight.shape, True),
                whole((1, cols)),
                whole(near.shape),
                whole(far.shape),
            ]
            + [pl.BlockSpec((rows, cols), lambda i, t: (i // CHUNKS, 0))] * CHUNKS
            + [at_tile(cols)] * (2 * CHUNKS),
            out_specs=[
                pl.BlockSpec((rows, width), lambda i, t: (jnp.minimum(i, half - 1), 0)),
                pl.BlockSpec((rows, width), lambda i, t: (jnp.maximum(i - half, 0), 0)),
                whole((1, cols)),
                whole((width, 3 * cols)),
            ],
            scratch_shapes=[pltpu.VMEM((width, 3 * cols), F32)],
        ),
        out_shape=[
            jax.ShapeDtypeStruct((half * rows, width), BF16),
            jax.ShapeDtypeStruct((half * rows, width), BF16),
            jax.ShapeDtypeStruct((1, cols), F32),
            jax.ShapeDtypeStruct((width, 3 * cols), BF16),
        ],
        name="project_back",
    )(order, x, q_rot, k_rot, weight, gains, near, far, *dq, *dk, *dv)


def outer_kernel(chunks, *refs):
    left_refs = refs[:chunks]
    right_refs = refs[chunks : 2 * chunks]
    out_ref = refs[2 * chunks]
    total = mm(left_refs[0][...], right_refs[0][...], TN)
    for left, right in zip(left_refs[1:], right_refs[1:], strict=True):
        total = total + mm(left[...], right[...], TN)
    out_ref[...] = total.astype(BF16)


def outer(left, right, step):
    rows, width = left[0].shape
    cols = right[0].shape[1]
    return pl.pallas_call(
        functools.partial(outer_kernel, len(left)),
        grid=(cols // step,),
        in_specs=[whole((rows, width), True)] * len(left)
        + [pl.BlockSpec((rows, step), lambda i: (0, i))] * len(right),
        out_specs=pl.BlockSpec((width, step), lambda i: (0, i)),
        out_shape=jax.ShapeDtypeStruct((width, cols), BF16),
        name="outer",
    )(*left, *right)


def two_parts(value):
    high = value.astype(BF16)
    return high, (value - high.astype(F32)).astype(BF16)


def step_kernel(g_ref, left_ref, right_ref, master_ref, grad_ref, stepped_ref, square_ref):
    owners, slots, piece, width = g_ref.shape
    for slot in range(slots):
        low = jnp.concatenate([g_ref[o, slot] for o in range(owners)], axis=0)
        grad_ref[slot] = low.astype(F32)
        high, rest = two_parts(left_ref[slot])
        turned = mm(high, low) + mm(rest, low)
        t_high, t_rest = two_parts(turned)
        r_high, r_rest = two_parts(right_ref[slot])
        direction = mm(t_high, r_high) + mm(t_high, r_rest) + mm(t_rest, r_high)
        stepped = master_ref[slot] - 0.3 * direction
        stepped_ref[slot] = stepped
        square_ref[slot : slot + 1] = jnp.sum(stepped * stepped, axis=0, keepdims=True)


def stats_kernel(g_ref, left_ref, right_ref, new_left_ref, new_right_ref):
    owners, slots, piece, width = g_ref.shape
    for slot in range(slots):
        low = jnp.concatenate([g_ref[o, slot] for o in range(owners)], axis=0)
        new_left_ref[slot] = 0.5 * left_ref[slot] + 0.5 * mm(low, low, NT)
        new_right_ref[slot] = 0.5 * right_ref[slot] + 0.5 * mm(low, low, TN)


def finish_kernel(stepped_ref, ema_ref, norm_ref, master_ref, new_ema_ref):
    slots = stepped_ref.shape[0]
    for slot in range(slots):
        master = stepped_ref[slot] * lax.rsqrt(norm_ref[slot : slot + 1] + 1e-06)
        master_ref[slot] = master
        new_ema_ref[slot] = 0.5 * ema_ref[slot] + 0.5 * master


def block_specs(count, slots):
    return pl.BlockSpec((slots, BLOCK, BLOCK), lambda i: (i, 0, 0))


def exchange(value, axis, pairs):
    return lax.ppermute(value, axis, pairs)


def shards(
    tokens,
    seq_lengths,
    qkv_weight,
    out_weight,
    up_gate_weight,
    down_weight,
    qk_scale,
    mlp_scale,
    eigen_rates,
    cotangent,
    block_order,
    master_blocks,
    ema_blocks,
    left_stats,
    right_stats,
    left_root,
    right_root,
):
    x_rows = tokens[0]
    total, width = x_rows.shape
    cols = qk_scale.shape[0]
    heads = lax.axis_size("head")
    owners = lax.axis_size("batch")
    ranks = heads // 2
    here = lax.axis_index("head")
    rank, core = here // 2, here % 2
    share = total // heads
    rows = share // CHUNKS
    tiles_all = total // rows

    core_swap = [(i, i ^ 1) for i in range(heads)]
    shift_up = [
        [(i, (i // 2 + s) % ranks * 2 + i % 2) for i in range(heads)] for s in range(ranks)
    ]
    shift_down = [
        [(i, (i // 2 - s) % ranks * 2 + i % 2) for i in range(heads)] for s in range(ranks)
    ]
    far_steps = list(range(1, ranks))
    ring = far_steps + [0]

    shares = jnp.stack(
        [(rank - s) % ranks * 2 + (core + d) % 2 for d in (1, 0) for s in ring]
    ).astype(jnp.int32)
    ends = jnp.cumsum(seq_lengths[0])

    def begin_of(row):
        segment = jnp.sum((row[:, None] >= ends[None, :]).astype(jnp.int32), axis=1)
        member = segment[:, None] == jnp.arange(ends.shape[0], dtype=jnp.int32)[None, :]
        return jnp.sum(jnp.where(member, (ends - seq_lengths[0])[None, :], 0), axis=1)

    tile_rows = jnp.arange(tiles_all, dtype=jnp.int32) * rows
    tile_begin = begin_of(tile_rows)
    lane = jnp.arange(LANES, dtype=jnp.int32) % (HEAD_DIM // 2)
    freq = 10000.0 ** (-lane.astype(F32) * 2.0 / HEAD_DIM)
    near_angle = jnp.arange(rows, dtype=F32)[:, None] * freq[None, :]
    far_angle = (tile_rows - tile_begin).astype(F32)[:, None] * freq[None, :]
    near = jnp.stack([jnp.cos(near_angle), jnp.sin(near_angle)])
    far = jnp.stack([jnp.cos(far_angle), jnp.sin(far_angle)])
    gains = qk_scale[None, :]
    rates = eigen_rates.T

    q, k, v, q_rot, k_rot = project(x_rows, qkv_weight, gains, near, far)

    def reduce_to_shares(send, keep, size):
        got = exchange(send, "head", core_swap)
        parts = [keep, got]
        if ranks > 1:
            away = (keep[: -size].astype(F32) + got[: -size].astype(F32)).astype(BF16)
            for n, s in enumerate(far_steps):
                parts.append(
                    exchange(away[n * size : (n + 1) * size], "head", shift_down[s])
                )
        return parts

    def gather_shares(own):
        mine = [exchange(own, "head", shift_up[s]) for s in far_steps] + [own]
        return [exchange(b, "head", core_swap) for b in mine] + mine

    places = [(here * CHUNKS + j).astype(jnp.int32)[None] for j in range(CHUNKS)]
    tiles = [shares * CHUNKS + j for j in range(CHUNKS)]
    starts = [begin_of(t * rows) for t in tiles]
    chunks = range(CHUNKS)
    fwd = [attend(q, k, v, out_weight, tiles[j], starts[j], rows) for j in chunks]
    attn_out = [f[0] for f in fwd]
    lse = [f[1] for f in fwd]
    joined = []
    for j in chunks:
        parts = reduce_to_shares(fwd[j][2], fwd[j][3], rows)
        joined.append(join_attention(parts, x_rows, places[j], rates, rows))
    ffn = [
        mlp(gather_shares(joined[j][0]), up_gate_weight, down_weight, mlp_scale) for j in chunks
    ]
    ends_fwd = []
    for j in chunks:
        parts = reduce_to_shares(ffn[j][4], ffn[j][5], rows)
        ends_fwd.append(join_mlp(parts, joined[j][1], cotangent[0], j, rates, rows))
    back = [
        mlp_back(
            gather_shares(ends_fwd[j][1]),
            ffn[j][1],
            ffn[j][2],
            up_gate_weight,
            down_weight,
            mlp_scale,
        )
        for j in chunks
    ]
    split = []
    for j in chunks:
        parts = reduce_to_shares(back[j][4], back[j][5], rows)
        split.append(
            split_attention(
                parts,
                ends_fwd[j][2],
                joined[j][1],
                joined[j][2],
                x_rows,
                places[j],
                rates,
                rows,
            )
        )
    hidden_full = [ffn[j][0] for j in chunks]
    d_mlp_rows = [back[j][0] for j in chunks]
    grad_up = outer(hidden_full, [back[j][1] for j in chunks], 2 * BLOCK)
    grad_gate = outer(hidden_full, [back[j][2] for j in chunks], 2 * BLOCK)
    grad_down = outer(d_mlp_rows, [ffn[j][3] for j in chunks], 2 * BLOCK)
    attn_back = [
        attend_back(
            gather_shares(split[j][0]),
            q,
            k,
            v,
            attn_out[j],
            lse[j],
            out_weight,
            tiles[j],
            starts[j],
            rows,
        )
        for j in chunks
    ]
    order = (shares[:, None] * CHUNKS + jnp.arange(CHUNKS, dtype=jnp.int32)[None, :]).reshape(-1)
    send, keep, gain_grad, grad_qkv = project_back(
        x_rows,
        q_rot,
        k_rot,
        qkv_weight,
        gains,
        near,
        far,
        [a[0] for a in attn_back],
        [a[1] for a in attn_back],
        [a[2] for a in attn_back],
        order,
        rows,
    )
    parts = reduce_to_shares(send, keep, share)
    d_input = jnp.concatenate([s[1] for s in split], axis=0)
    d_input = d_input + sum(p[-share:].astype(F32) for p in parts)

    def double(value, axis, size):
        step = 1
        while step < size:
            value = value + exchange(value, axis, [(i, i ^ step) for i in range(size)])
            step *= 2
        return value

    rate_grad = jnp.concatenate(
        [sum(s[2] for s in split), sum(e[3] for e in ends_fwd)], axis=0
    )
    rate_grad = double(rate_grad, "head", heads)
    scale_grad = sum(b[3] for b in back)
    small = double(
        jnp.concatenate([rate_grad.reshape(-1), scale_grad.reshape(-1)]), "batch", owners
    )
    gain_sum = double(gain_grad[0], "batch", owners)
    rate_sum = small[: 2 * width].reshape(2, width)
    scale_sum = small[2 * width :].reshape(mlp_scale.shape)

    row_blocks = width // BLOCK
    piece = BLOCK // owners

    def as_pieces(matrix):
        panels = matrix.shape[1] // BLOCK
        return (
            matrix.reshape(row_blocks, owners, piece, panels, BLOCK)
            .transpose(1, 3, 0, 2, 4)
            .reshape(owners, panels * row_blocks * piece, BLOCK)
        )

    def summed(matrix):
        return lax.psum_scatter(
            as_pieces(matrix), "batch", scatter_dimension=0, tiled=False
        ).reshape(-1, piece, BLOCK)

    grad_out = sum(a[3] for a in attn_back).astype(BF16)
    late = summed(jnp.concatenate([grad_qkv, grad_out], axis=1))
    early = summed(jnp.concatenate([grad_up, grad_gate, grad_down], axis=1))
    pieces = jnp.concatenate([late, early], axis=0)
    slot_order = block_order[0]
    ordered = jnp.take(pieces, slot_order, axis=0)
    per_owner = ordered.shape[0] // owners
    owned = lax.all_to_all(
        ordered.reshape(owners, per_owner, piece, BLOCK),
        "batch",
        split_axis=0,
        concat_axis=0,
        tiled=True,
    )
    slots = min(8, per_owner)
    if piece % 16:
        owned = owned.transpose(1, 0, 2, 3).reshape(1, per_owner, BLOCK, BLOCK)
    g_spec = pl.BlockSpec(
        (owned.shape[0], slots) + owned.shape[2:], lambda i: (0, i, 0, 0)
    )
    blk = pl.BlockSpec((slots, BLOCK, BLOCK), lambda i: (i, 0, 0))
    row = pl.BlockSpec((slots, BLOCK), lambda i: (i, 0))
    cube = jax.ShapeDtypeStruct((per_owner, BLOCK, BLOCK), F32)
    grid = (per_owner // slots,)
    owned_grad, stepped, column_sq = pl.pallas_call(
        step_kernel,
        grid=grid,
        in_specs=[g_spec, blk, blk, blk],
        out_specs=[blk, blk, row],
        out_shape=[cube, cube, jax.ShapeDtypeStruct((per_owner, BLOCK), F32)],
        name="step",
    )(owned, left_root[0], right_root[0], master_blocks[0])
    new_left, new_right = pl.pallas_call(
        stats_kernel,
        grid=grid,
        in_specs=[g_spec, blk, blk],
        out_specs=[blk, blk],
        out_shape=[cube, cube],
        name="stats",
    )(owned, left_stats[0], right_stats[0])
    panels = block_order.shape[1] // row_blocks
    my_blocks = lax.dynamic_slice_in_dim(
        slot_order, lax.axis_index("batch") * per_owner, per_owner, 0
    )
    member = (
        (my_blocks // row_blocks)[:, None] == jnp.arange(panels, dtype=jnp.int32)[None, :]
    ).astype(F32)
    precise = lax.Precision.HIGHEST
    totals = double(jnp.einsum("sp,sb->pb", member, column_sq, precision=precise), "batch", owners)
    norms = jnp.einsum("sp,pb->sb", member, totals, precision=precise)
    new_master, new_ema = pl.pallas_call(
        finish_kernel,
        grid=grid,
        in_specs=[blk, blk, row],
        out_specs=[blk, blk],
        out_shape=[cube, cube],
        name="finish",
    )(stepped, ema_blocks[0], norms)
    gain_step = 0.5 / math.sqrt(total * owners)
    width_share = width // heads
    rate_here = lax.dynamic_slice_in_dim(rate_sum, here * width_share, width_share, 1)
    rate_slice = lax.dynamic_slice_in_dim(rates, here * width_share, width_share, 1)
    mlp_scale_out = jnp.stack([scale_sum, mlp_scale - gain_step * scale_sum])
    new_gains = jnp.concatenate(
        [(qk_scale - gain_step * gain_sum)[None, :], rate_slice - gain_step * rate_here], axis=0
    )
    out_share = jnp.concatenate([e[0] for e in ends_fwd], axis=0)
    return (
        out_share[None],
        d_input[None],
        owned_grad[None],
        new_master[None],
        new_ema[None],
        new_left[None],
        new_right[None],
        gain_sum,
        mlp_scale_out,
        rate_here.T,
        new_gains,
    )


def solution(mesh):
    return jax.shard_map(
        shards,
        mesh=mesh,
        in_specs=(
            P("batch", None, None),
            P("batch", None),
            P(None, None, "head"),
            P("head", None),
            P(None, None, "head"),
            P("head", None),
            P("head"),
            P(None, "head"),
            P(),
            P("batch", "head", None),
            P("head", None),
            P("head", "batch", None, None),
            P("head", "batch", None, None),
            P("head", "batch", None, None),
            P("head", "batch", None, None),
            P("head", "batch", None, None),
            P("head", "batch", None, None),
        ),
        out_specs=(
            P("batch", "head", None),
            P("batch", "head", None),
            P("head", "batch", None, None),
            P("head", "batch", None, None),
            P("head", "batch", None, None),
            P("head", "batch", None, None),
            P("head", "batch", None, None),
            P("head"),
            P(None, None, "head"),
            P("head", None),
            P(None, "head"),
        ),
        check_vma=False,
    )
```

```python
import functools
import math

import jax
import jax.numpy as jnp
from jax import lax
from jax.experimental import pallas as pl
from jax.experimental.pallas import tpu as pltpu
from jax.sharding import PartitionSpec as P

HEAD_DIM = 64
BLOCK = 128
LANES = 128
CHUNKS = 2
F32 = jnp.float32
BF16 = jnp.bfloat16
NN = (((1,), (0,)), ((), ()))
NT = (((1,), (1,)), ((), ()))
TN = (((0,), (0,)), ((), ()))


def mm(a, b, dims=NN):
    return lax.dot_general(a, b, dims, preferred_element_type=F32)


def whole(shape, single=False):
    zeros = (0,) * len(shape)
    if single:
        return pl.BlockSpec(shape, lambda *_: zeros, pipeline_mode=pl.Buffered(1))
    return pl.BlockSpec(shape, lambda *_: zeros)


def launch(kernel, name, grid, ins, outs, scratch=(), prefetch=(), after=(), alias=0):
    first, count, extra = len(prefetch), len(ins), len(after)

    def body(*refs):
        kernel(*refs[: first + count], *refs[first + count + extra :])

    return pl.pallas_call(
        body,
        grid_spec=pltpu.PrefetchScalarGridSpec(
            num_scalar_prefetch=first,
            grid=grid,
            in_specs=[s for _, s in ins] + [pl.BlockSpec(memory_space=pl.ANY)] * extra,
            out_specs=[s for _, s in outs],
            scratch_shapes=list(scratch),
        ),
        out_shape=[o for o, _ in outs],
        input_output_aliases={first + count + n: n for n in range(alias)},
        name=name,
    )(*prefetch, *[a for a, _ in ins], *after)


def like(shape, dtype):
    return jax.ShapeDtypeStruct(shape, dtype)


def rms_rows(value):
    return value * lax.rsqrt(jnp.mean(value * value, axis=-1, keepdims=True) + 1e-06)


def rms_factor(value):
    return lax.rsqrt(jnp.mean(value * value, axis=-1, keepdims=True) + 1e-06)


def rms_back(normed, factor, gradient):
    return factor * (gradient - normed * jnp.mean(gradient * normed, axis=-1, keepdims=True))


def lane_ids():
    return lax.broadcasted_iota(jnp.int32, (1, LANES), 1)


def head_mean(value, ones_block):
    high = value.astype(BF16)
    rest = (value - high.astype(F32)).astype(BF16)
    return (mm(high, ones_block) + mm(rest, ones_block)) * (1.0 / HEAD_DIM)


def ones_block():
    row = lax.broadcasted_iota(jnp.int32, (LANES, LANES), 0) // HEAD_DIM
    col = lax.broadcasted_iota(jnp.int32, (LANES, LANES), 1) // HEAD_DIM
    return jnp.where(row == col, 1.0, 0.0).astype(BF16)


def half_turn(value):
    first = (lane_ids() & (HEAD_DIM - 1)) < HEAD_DIM // 2
    return jnp.where(
        first,
        pltpu.roll(value, LANES - HEAD_DIM // 2, 1),
        pltpu.roll(value, HEAD_DIM // 2, 1),
    )


def angles(tile, near_ref, far_ref):
    cos_r, sin_r = near_ref[0], near_ref[1]
    cos_0 = far_ref[0, pl.ds(tile, 1), :]
    sin_0 = far_ref[1, pl.ds(tile, 1), :]
    first = (lane_ids() & (HEAD_DIM - 1)) < HEAD_DIM // 2
    sine = sin_0 * cos_r + cos_0 * sin_r
    return cos_0 * cos_r - sin_0 * sin_r, jnp.where(first, -sine, sine)


def project_kernel(
    x_ref, w_ref, gain_ref, near_ref, far_ref, q_ref, k_ref, v_ref, q_rot_ref, k_rot_ref
):
    tile = pl.program_id(0)
    cosine, sine = angles(tile, near_ref, far_ref)
    ones = ones_block()
    x = x_ref[...]
    for index, used_ref, rot_ref in ((0, q_ref, q_rot_ref), (1, k_ref, k_rot_ref)):
        raw = mm(x, w_ref[index])
        for pair in range(raw.shape[1] // LANES):
            lanes = slice(pair * LANES, (pair + 1) * LANES)
            value = raw[:, lanes]
            turned = value * cosine + half_turn(value) * sine
            factor = lax.rsqrt(head_mean(turned * turned, ones) + 1e-06)
            rot_ref[:, lanes] = turned
            used_ref[:, lanes] = (turned * factor * gain_ref[:, lanes]).astype(BF16)
    v_ref[...] = mm(x, w_ref[2]).astype(BF16)


def project(x, weight, gains, near, far):
    rows, width = x.shape
    cols = weight.shape[2]
    tile = near.shape[1]
    by_row = lambda w: pl.BlockSpec((tile, w), lambda i: (i, 0))
    return pl.pallas_call(
        project_kernel,
        grid=(rows // tile,),
        in_specs=[
            by_row(width),
            whole(weight.shape, True),
            whole((1, cols)),
            whole(near.shape),
            whole(far.shape),
        ],
        out_specs=[by_row(cols)] * 5,
        out_shape=[jax.ShapeDtypeStruct((rows, cols), BF16)] * 3
        + [jax.ShapeDtypeStruct((rows, cols), F32)] * 2,
        name="project",
    )(x, weight, gains, near, far)


def key_tiles(first_row, start, wide, narrow, visit):
    full = first_row // wide

    def step(index, carry):
        visit(pl.multiple_of(index * wide, wide), wide, False)
        return carry

    lax.fori_loop(start // wide, full, step, 0)
    diagonal = (first_row // narrow) * narrow

    @pl.when(diagonal > full * wide)
    def _():
        visit(pl.multiple_of(full * wide, narrow), narrow, False)

    visit(pl.multiple_of(diagonal, narrow), narrow, True)


def attend_kernel(
    wide, tiles, starts, q_ref, k_ref, v_ref, w_ref, o_ref, lse_ref, part_ref, acc
):
    index = pl.program_id(0)
    rows = q_ref.shape[0]
    first_row = tiles[index] * rows
    start = starts[index]
    narrow = wide // 2
    low = lane_ids() < HEAD_DIM
    zero = jnp.zeros((), BF16)
    results = []
    for pair in range(q_ref.shape[1] // LANES):
        lanes = slice(pair * LANES, (pair + 1) * LANES)
        q = q_ref[:, lanes] * jnp.asarray(1.0 / math.sqrt(HEAD_DIM), BF16)
        q_both = jnp.concatenate([jnp.where(low, q, zero), jnp.where(low, zero, q)], axis=0)
        acc[...] = jnp.zeros_like(acc)

        def visit(key_0, size, masked):
            keys = pl.ds(key_0, size)
            weights = jnp.exp(mm(q_both, k_ref[keys, lanes], NT))
            if masked:
                row = lax.broadcasted_iota(jnp.int32, (2 * rows, size), 0)
                row = jnp.where(row < rows, row, row - rows) + first_row
                col = lax.broadcasted_iota(jnp.int32, (2 * rows, size), 1) + key_0
                weights = jnp.where((col <= row) & (col >= start), weights, 0.0)
            total = weights[:, :LANES]
            for part in range(1, size // LANES):
                total = total + weights[:, part * LANES : (part + 1) * LANES]
            acc[:, LANES:] += total
            acc[:, :LANES] += mm(weights.astype(BF16), v_ref[keys, lanes])

        key_tiles(first_row, start, wide, narrow, visit)
        total_a = jnp.sum(acc[:rows, LANES:], axis=1, keepdims=True)
        total_b = jnp.sum(acc[rows:, LANES:], axis=1, keepdims=True)
        summed = jnp.where(low, acc[:rows, :LANES], acc[rows:, :LANES])
        out = (summed / jnp.where(low, total_a, total_b)).astype(BF16)
        o_ref[:, lanes] = out
        lse_ref[:, lanes] = jnp.log(jnp.where(low, total_b, total_a))
        results.append(out)
    part_ref[...] = mm(jnp.concatenate(results, axis=1), w_ref[...]).astype(BF16)


def attend(q, k, v, weight, tiles, starts, rows, offset, places, after, alias=0):
    count = tiles.shape[0]
    cols = k.shape[1]
    width = weight.shape[1]
    at_place = pl.BlockSpec((rows, cols), lambda i, t, s: (i + offset, 0))
    return launch(
        functools.partial(attend_kernel, 4 * BLOCK),
        "attend",
        (count,),
        [
            (q, pl.BlockSpec((rows, cols), lambda i, t, s: (t[i], 0))),
            (k, whole(k.shape, True)),
            (v, whole(v.shape, True)),
            (weight, whole(weight.shape, True)),
        ],
        [
            (like((places * rows, cols), BF16), at_place),
            (like((places * rows, cols), F32), at_place),
            (like((count * rows, width), BF16), pl.BlockSpec((rows, width), lambda i, t, s: (i, 0))),
        ],
        scratch=[pltpu.VMEM((2 * rows, 2 * LANES), F32)],
        prefetch=(tiles, starts),
        after=after,
        alias=alias,
    )


def attend_back_kernel(blocks, wide, tiles, starts, *refs):
    row_refs = refs[:blocks]
    q_ref, k_ref, v_ref, o_ref, lse_ref, w_ref = refs[blocks : blocks + 6]
    dq_ref, dk_ref, dv_ref, rows_s, acc = refs[blocks + 6 :]
    index = pl.program_id(0)
    rows = q_ref.shape[0]
    narrow = wide // 2

    @pl.when(index == 0)
    def _():
        dk_ref[...] = jnp.zeros_like(dk_ref)
        dv_ref[...] = jnp.zeros_like(dv_ref)

    for block in range(blocks):

        @pl.when(index == block)
        def _(block=block):
            rows_s[...] = row_refs[block][...]

    first_row = tiles[index] * rows
    start = starts[index]
    low = lane_ids() < HEAD_DIM
    place = lane_ids() & (HEAD_DIM - 1)
    zero = jnp.zeros((), BF16)
    ones = jnp.where(place < 3, 1.0, 0.0).astype(BF16)

    def parts(value):
        high = value.astype(BF16).astype(F32)
        rest = value - high
        middle = rest.astype(BF16).astype(F32)
        picked = jnp.where(place == 1, middle, jnp.where(place == 2, rest - middle, 0.0))
        return jnp.where(place == 0, high, picked).astype(BF16)

    d_rows = rows_s[...]
    d_attn = mm(d_rows, w_ref[...], NT).astype(BF16)
    for pair in range(q_ref.shape[1] // LANES):
        lanes = slice(pair * LANES, (pair + 1) * LANES)
        q = q_ref[:, lanes] * jnp.asarray(1.0 / math.sqrt(HEAD_DIM), BF16)
        d_out = d_attn[:, lanes]
        minus_lse = parts(-lse_ref[:, lanes])
        product = d_out.astype(F32) * o_ref[:, lanes].astype(F32)
        sum_a = jnp.sum(jnp.where(low, product, 0.0), axis=1, keepdims=True)
        sum_b = jnp.sum(jnp.where(low, 0.0, product), axis=1, keepdims=True)
        minus_delta = parts(-jnp.where(low, sum_b, sum_a))
        q_ext = (jnp.where(low, q, minus_lse), jnp.where(low, minus_lse, q))
        d_ext = (jnp.where(low, d_out, minus_delta), jnp.where(low, minus_delta, d_out))
        q_both = jnp.concatenate([jnp.where(low, q, zero), jnp.where(low, zero, q)], axis=0)
        d_both = jnp.concatenate(
            [jnp.where(low, d_out, zero), jnp.where(low, zero, d_out)], axis=0
        )
        acc[...] = jnp.zeros_like(acc)

        def visit(key_0, size, masked):
            keys = pl.ds(key_0, size)
            k = k_ref[keys, lanes]
            v = v_ref[keys, lanes]
            k_ext = (jnp.where(low, k, ones), jnp.where(low, ones, k))
            v_ext = (jnp.where(low, v, ones), jnp.where(low, ones, v))
            if masked:
                col = lax.broadcasted_iota(jnp.int32, (size, rows), 1) + first_row
                row = lax.broadcasted_iota(jnp.int32, (size, rows), 0) + key_0
                allowed = (row <= col) & (row >= start)
            probs = []
            d_scores = []
            for head in range(2):
                prob = jnp.exp(mm(k_ext[head], q_ext[head], NT))
                if masked:
                    prob = jnp.where(allowed, prob, 0.0)
                d_score = prob * mm(v_ext[head], d_ext[head], NT)
                probs.append(prob.astype(BF16))
                d_scores.append(d_score.astype(BF16))
            dv_ref[keys, lanes] += mm(jnp.concatenate(probs, axis=1), d_both)
            dk_ref[keys, lanes] += mm(jnp.concatenate(d_scores, axis=1), q_both)
            k_both = jnp.concatenate([jnp.where(low, k, zero), jnp.where(low, zero, k)], axis=0)
            acc[...] += mm(jnp.concatenate(d_scores, axis=0), k_both, TN)

        key_tiles(first_row, start, wide, narrow, visit)
        dq_ref[:, lanes] = acc[...] * (1.0 / math.sqrt(HEAD_DIM))


def attend_back(row_blocks, q, k, v, o, lse, weight, tiles, starts, rows, pair, after):
    count = tiles.shape[0]
    total = k.shape[0]
    width = weight.shape[1]
    at_tile = pl.BlockSpec((rows, LANES), lambda i, t, s: (t[i], pair))
    at_step = pl.BlockSpec((rows, LANES), lambda i, t, s: (i, pair))
    column = pl.BlockSpec((total, LANES), lambda *_: (0, pair), pipeline_mode=pl.Buffered(1))
    return launch(
        functools.partial(attend_back_kernel, len(row_blocks), 4 * BLOCK),
        "attend_back",
        (count,),
        [(b, whole(b.shape, True)) for b in row_blocks]
        + [
            (q, at_tile),
            (k, column),
            (v, column),
            (o, at_step),
            (lse, at_step),
            (weight, pl.BlockSpec((LANES, width), lambda *_: (pair, 0))),
        ],
        [
            (like((count * rows, LANES), F32), pl.BlockSpec((rows, LANES), lambda i, *_: (i, 0))),
            (like((total, LANES), F32), whole((total, LANES))),
            (like((total, LANES), F32), whole((total, LANES))),
        ],
        scratch=[pltpu.VMEM((rows, width), BF16), pltpu.VMEM((rows, LANES), F32)],
        prefetch=(tiles, starts),
        after=after,
    )


def sum_parts(refs):
    total = refs[0][...].astype(F32)
    for ref in refs[1:]:
        total = total + ref[...].astype(F32)
    return total


def join_attention_kernel(parts, place, *refs):
    x_ref, rate_ref = refs[parts : parts + 2]
    low_ref, hidden_ref, branch_ref = refs[parts + 2 :]
    branch = sum_parts(refs[:parts])
    x = x_ref[...].astype(F32)
    hidden = rms_rows(x + rate_ref[0:1] * (rms_rows(branch) - x))
    branch_ref[...] = branch
    hidden_ref[...] = hidden
    low_ref[...] = hidden.astype(BF16)


def part_specs(parts, rows, width):
    return [
        pl.BlockSpec((rows, width), lambda i, *_, last=a.shape[0] // rows: (last - SUB + i, 0))
        for a in parts
    ]


SUB = 2


def join_attention(parts, x, place, rates, share, after):
    width = x.shape[1]
    rows = share // SUB
    here = pl.BlockSpec((rows, width), lambda i, p: (i, 0))
    return launch(
        functools.partial(join_attention_kernel, len(parts)),
        "join_attention",
        (SUB,),
        list(zip(parts, part_specs(parts, rows, width), strict=True))
        + [
            (x, pl.BlockSpec((rows, width), lambda i, p: (p[0] * SUB + i, 0))),
            (rates, whole(rates.shape)),
        ],
        [(like((share, width), d), here) for d in (BF16, F32, F32)],
        prefetch=(place,),
        after=after,
    )


def weight_tiles(weight, down, step, side):
    _, width, cols = weight.shape
    count = cols // step
    if side == 0:
        at = lambda t: jnp.minimum(t, count - 1)
    else:
        at = lambda t: jnp.maximum(t - count, 0)
    return [
        (weight, pl.BlockSpec((2, width, step), lambda t, *_: (0, 0, at(t)))),
        (down, pl.BlockSpec((step, width), lambda t, *_: (at(t), 0))),
    ]


def mlp_kernel(blocks, *refs):
    row_refs = refs[:blocks]
    sides = (refs[blocks : blocks + 2], refs[blocks + 2 : blocks + 4])
    scale_ref = refs[blocks + 4]
    up_ref, gate_ref, mixed_ref, away_ref, own_ref, x_s, acc = refs[blocks + 5 :]
    tile = pl.program_id(0)
    count = pl.num_programs(0)
    rows = row_refs[0].shape[0]

    @pl.when(tile == 0)
    def _():
        for block in range(blocks):
            x_s[block * rows : (block + 1) * rows] = row_refs[block][...]
        acc[...] = jnp.zeros_like(acc)

    def run(w_ref, down_ref):
        x = x_s[...]
        up = mm(x, w_ref[0])
        gate = mm(x, w_ref[1])
        up_ref[...] = up.astype(BF16)
        gate_ref[...] = gate.astype(BF16)
        scaled = gate * scale_ref[1:2]
        mixed = (up * scale_ref[0:1] * (scaled * jax.nn.sigmoid(scaled))).astype(BF16)
        mixed_ref[...] = mixed
        acc[...] += mm(mixed, down_ref[...])

    for side in range(2):

        @pl.when(tile // (count // 2) == side)
        def _(side=side):
            run(*sides[side])

    @pl.when(tile == count - 1)
    def _():
        last = (blocks - 1) * rows
        own_ref[...] = acc[last:]
        if blocks > 1:
            away_ref[...] = acc[:last].astype(BF16)


def mlp(row_blocks, weights, scales, step, after):
    rows, width = row_blocks[0].shape
    blocks = len(row_blocks)
    height = rows * blocks
    cols = 2 * weights[0][0].shape[2]
    at_tile = lambda h: pl.BlockSpec((h, step), lambda t: (0, t))
    far = max(blocks - 1, 1) * rows
    return launch(
        functools.partial(mlp_kernel, blocks),
        "mlp",
        (cols // step,),
        [(b, whole(b.shape, True)) for b in row_blocks]
        + weight_tiles(*weights[0], step, 0)
        + weight_tiles(*weights[1], step, 1)
        + [(scales, at_tile(2))],
        [(like((height, cols), BF16), at_tile(height))] * 3
        + [
            (like((far, width), BF16), whole((far, width))),
            (like((rows, width), F32), whole((rows, width))),
        ],
        scratch=[pltpu.VMEM((height, width), BF16), pltpu.VMEM((height, width), F32)],
        after=after,
    )


def join_mlp_kernel(parts, *refs):
    hidden_ref, cot_ref, rate_ref = refs[parts : parts + 3]
    out_ref, low_ref, d_hidden_ref, rate_grad_ref = refs[parts + 3 :]
    branch = sum_parts(refs[:parts])
    hidden = hidden_ref[...]
    rate = rate_ref[1:2]
    factor = rms_factor(branch)
    normed = branch * factor
    gap = normed - hidden
    before = hidden + rate * gap
    factor_out = rms_factor(before)
    out = before * factor_out
    d_before = rms_back(out, factor_out, cot_ref[...].astype(F32))
    out_ref[...] = out
    d_hidden_ref[...] = (1.0 - rate) * d_before
    low_ref[...] = rms_back(normed, factor, rate * d_before).astype(BF16)

    @pl.when(pl.program_id(0) == 0)
    def _():
        rate_grad_ref[...] = jnp.zeros_like(rate_grad_ref)

    rate_grad_ref[...] += jnp.sum(d_before * gap, axis=0, keepdims=True)


def join_mlp(parts, hidden, cotangent, chunk, rates, share, after):
    width = hidden.shape[1]
    rows = share // SUB
    here = pl.BlockSpec((rows, width), lambda i: (i, 0))
    return launch(
        functools.partial(join_mlp_kernel, len(parts)),
        "join_mlp",
        (SUB,),
        list(zip(parts, part_specs(parts, rows, width), strict=True))
        + [
            (hidden, here),
            (cotangent, pl.BlockSpec((rows, width), lambda i: (chunk * SUB + i, 0))),
            (rates, whole(rates.shape)),
        ],
        [(like((share, width), d), here) for d in (F32, BF16, F32)]
        + [(like((1, width), F32), whole((1, width)))],
        after=after,
    )


def mlp_back_kernel(blocks, *refs):
    row_refs = refs[:blocks]
    sides = (refs[blocks : blocks + 2], refs[blocks + 2 : blocks + 4])
    scale_ref, up_ref, gate_ref = refs[blocks + 4 : blocks + 7]
    d_up_ref, d_gate_ref, sums_ref, away_ref, own_ref, x_s, acc = refs[blocks + 7 :]
    tile = pl.program_id(0)
    count = pl.num_programs(0)
    rows = row_refs[0].shape[0]

    @pl.when(tile == 0)
    def _():
        for block in range(blocks):
            x_s[block * rows : (block + 1) * rows] = row_refs[block][...]
        acc[...] = jnp.zeros_like(acc)

    def run(w_ref, down_ref):
        d_mixed = mm(x_s[...], down_ref[...], NT)
        up_raw = up_ref[...].astype(F32)
        gate_raw = gate_ref[...].astype(F32)
        scale_up = scale_ref[0:1]
        scale_gate = scale_ref[1:2]
        gate = gate_raw * scale_gate
        sig = jax.nn.sigmoid(gate)
        d_up = d_mixed * (gate * sig)
        d_gate = d_mixed * (up_raw * scale_up) * (sig * (1.0 + gate * (1.0 - sig)))
        sums_ref[0:1] = jnp.sum(d_up * up_raw, axis=0, keepdims=True)
        sums_ref[1:2] = jnp.sum(d_gate * gate_raw, axis=0, keepdims=True)
        d_up = (d_up * scale_up).astype(BF16)
        d_gate = (d_gate * scale_gate).astype(BF16)
        d_up_ref[...] = d_up
        d_gate_ref[...] = d_gate
        acc[...] += mm(d_up, w_ref[0], NT) + mm(d_gate, w_ref[1], NT)

    for side in range(2):

        @pl.when(tile // (count // 2) == side)
        def _(side=side):
            run(*sides[side])

    @pl.when(tile == count - 1)
    def _():
        last = (blocks - 1) * rows
        own_ref[...] = acc[last:]
        if blocks > 1:
            away_ref[...] = acc[:last].astype(BF16)


def mlp_back(row_blocks, up, gate, weights, scales, step, after):
    rows, width = row_blocks[0].shape
    blocks = len(row_blocks)
    height = rows * blocks
    cols = 2 * weights[0][0].shape[2]
    at_tile = lambda h: pl.BlockSpec((h, step), lambda t: (0, t))
    far = max(blocks - 1, 1) * rows
    return launch(
        functools.partial(mlp_back_kernel, blocks),
        "mlp_back",
        (cols // step,),
        [(b, whole(b.shape, True)) for b in row_blocks]
        + weight_tiles(*weights[0], step, 0)
        + weight_tiles(*weights[1], step, 1)
        + [(scales, at_tile(2)), (up, at_tile(height)), (gate, at_tile(height))],
        [(like((height, cols), BF16), at_tile(height))] * 2
        + [
            (like((2, cols), F32), at_tile(2)),
            (like((far, width), BF16), whole((far, width))),
            (like((rows, width), F32), whole((rows, width))),
        ],
        scratch=[pltpu.VMEM((height, width), BF16), pltpu.VMEM((height, width), F32)],
        after=after,
    )


def split_attention_kernel(parts, place, *refs):
    d_hidden_ref, hidden_ref, branch_ref, x_ref, rate_ref = refs[parts : parts + 5]
    low_ref, d_input_ref, rate_grad_ref = refs[parts + 5 :]
    d_hidden = sum_parts(refs[:parts]) + d_hidden_ref[...]
    hidden = hidden_ref[...]
    branch = branch_ref[...]
    x = x_ref[...].astype(F32)
    rate = rate_ref[0:1]
    factor = rms_factor(branch)
    normed = branch * factor
    gap = normed - x
    d_before = rms_back(hidden, rms_factor(x + rate * gap), d_hidden)
    d_input_ref[...] = (1.0 - rate) * d_before
    low_ref[...] = rms_back(normed, factor, rate * d_before).astype(BF16)

    @pl.when(pl.program_id(0) == 0)
    def _():
        rate_grad_ref[...] = jnp.zeros_like(rate_grad_ref)

    rate_grad_ref[...] += jnp.sum(d_before * gap, axis=0, keepdims=True)


def split_attention(parts, d_hidden, hidden, branch, x, place, rates, share, after):
    width = x.shape[1]
    rows = share // SUB
    here = pl.BlockSpec((rows, width), lambda i, p: (i, 0))
    return launch(
        functools.partial(split_attention_kernel, len(parts)),
        "split_attention",
        (SUB,),
        list(zip(parts, part_specs(parts, rows, width), strict=True))
        + [(d_hidden, here), (hidden, here), (branch, here)]
        + [
            (x, pl.BlockSpec((rows, width), lambda i, p: (p[0] * SUB + i, 0))),
            (rates, whole(rates.shape)),
        ],
        [(like((share, width), d), here) for d in (BF16, F32)]
        + [(like((1, width), F32), whole((1, width)))],
        prefetch=(place,),
        after=after,
    )


def project_back_kernel(order, x_here, *refs):
    (
        x_ref,
        q_rot_ref,
        k_rot_ref,
        w_ref,
        gain_ref,
        near_ref,
        far_ref,
    ) = refs[:7]
    pairs = q_rot_ref.shape[1] // LANES
    d_refs = refs[7 : 7 + 3 * CHUNKS * pairs]
    part = lambda which, pair: [
        d_refs[(which * CHUNKS + chunk) * pairs + pair] for chunk in range(CHUNKS)
    ]
    send_ref, keep_ref, gain_grad_ref = refs[7 + 3 * CHUNKS * pairs : 10 + 3 * CHUNKS * pairs]
    grad_refs = refs[10 + 3 * CHUNKS * pairs : -1]
    acc = refs[-1]
    index = pl.program_id(0)
    count = pl.num_programs(0)

    @pl.when(index == 0)
    def _():
        gain_grad_ref[...] = jnp.zeros_like(gain_grad_ref)
        acc[...] = jnp.zeros_like(acc)

    tile = order[index]
    cosine, sine = angles(tile, near_ref, far_ref)
    ones = ones_block()
    cols = q_rot_ref.shape[1]
    chunk = index % CHUNKS
    d_raw = []
    for which, rot_ref in ((0, q_rot_ref), (1, k_rot_ref)):
        for pair in range(pairs):
            lanes = slice(pair * LANES, (pair + 1) * LANES)
            if which == 0:
                d_used = part(0, pair)[0][...]
                for other in range(1, CHUNKS):
                    d_used = jnp.where(chunk == other, part(0, pair)[other][...], d_used)
            else:
                d_used = sum_parts(part(1, pair))
            turned = rot_ref[:, lanes]
            factor = lax.rsqrt(head_mean(turned * turned, ones) + 1e-06)
            normed = turned * factor
            gain_grad_ref[:, lanes] += jnp.sum(d_used * normed, axis=0, keepdims=True)
            d_normed = d_used * gain_ref[:, lanes]
            d_turned = factor * (d_normed - normed * head_mean(d_normed * normed, ones))
            d_raw.append((d_turned * cosine - half_turn(d_turned) * sine).astype(BF16))
    d_raw += [sum_parts(part(2, pair)).astype(BF16) for pair in range(pairs)]
    d_all = jnp.concatenate(d_raw, axis=1)
    d_x = mm(d_all[:, :cols], w_ref[0], NT)
    d_x = d_x + mm(d_all[:, cols : 2 * cols], w_ref[1], NT)
    d_x = (d_x + mm(d_all[:, 2 * cols :], w_ref[2], NT)).astype(BF16)
    acc[...] += mm(x_ref[...], d_all, TN)

    @pl.when(index < count // 2)
    def _():
        send_ref[...] = d_x

    @pl.when(index >= count // 2)
    def _():
        keep_ref[...] = d_x

    @pl.when(index == count - 1)
    def _():
        total = acc[...].astype(BF16)
        if len(grad_refs) == 1:
            grad_refs[0][...] = total
        else:
            store_pieces(total, x_here[0], *grad_refs)


def project_back(
    x, q_rot, k_rot, weight, gains, near, far, parts, order, rows, place, levels, after
):
    total, width = x.shape
    cols = weight.shape[2]
    count = order.shape[0]
    half = count // 2
    at_tile = lambda w: pl.BlockSpec((rows, w), lambda i, t, *_: (t[i], 0))
    if levels:
        shape = (levels, 3 * cols // BLOCK * (width // BLOCK), BLOCK // (2 * levels), BLOCK)
        grads = [(like(shape, BF16), whole(shape))] * 2
    else:
        grads = [(like((width, 3 * cols), BF16), whole((width, 3 * cols)))]
    return launch(
        project_back_kernel,
        "project_back",
        (count,),
        [
            (x, at_tile(width)),
            (q_rot, at_tile(cols)),
            (k_rot, at_tile(cols)),
            (weight, whole(weight.shape, True)),
            (gains, whole((1, cols))),
            (near, whole(near.shape)),
            (far, whole(far.shape)),
        ]
        + [
            (a, pl.BlockSpec((rows, LANES), lambda i, *_: (i // CHUNKS, 0)))
            for chunk in parts
            for a in chunk[0]
        ]
        + [
            (a, pl.BlockSpec((rows, LANES), lambda i, t, *_: (t[i], 0)))
            for which in (1, 2)
            for chunk in parts
            for a in chunk[which]
        ],
        [
            (
                like((half * rows, width), BF16),
                pl.BlockSpec((rows, width), lambda i, *_: (jnp.minimum(i, half - 1), 0)),
            ),
            (
                like((half * rows, width), BF16),
                pl.BlockSpec((rows, width), lambda i, *_: (jnp.maximum(i - half, 0), 0)),
            ),
            (like((1, cols), F32), whole((1, cols))),
        ]
        + grads,
        scratch=[pltpu.VMEM((width, 3 * cols), F32)],
        prefetch=(order, place),
        after=after,
    )


def outer_kernel(lefts, rights, has_more, pieces, *refs):
    if pieces:
        place, refs = refs[0], refs[1:]
    left_refs = refs[:lefts]
    right_refs = refs[lefts : lefts + rights]
    more_refs = refs[lefts + rights : lefts + rights + has_more]
    out_refs = refs[lefts + rights + has_more : -1]
    turned = refs[-1]
    rows = left_refs[0].shape[0]

    @pl.when(pl.program_id(0) == 0)
    def _():
        for block in range(lefts):
            turned[:, block * rows : (block + 1) * rows] = left_refs[block][...].T

    high = right_refs[0].shape[0]
    total = mm(turned[:, :high], right_refs[0][...])
    for n in range(1, rights):
        total = total + mm(turned[:, n * high : (n + 1) * high], right_refs[n][...])
    for more in more_refs:
        total = total + more[...].astype(F32)
    total = total.astype(BF16)
    if not pieces:
        out_refs[0][...] = total
        return
    store_pieces(total, place[0], *out_refs)


def store_pieces(total, x_here, *outs):
    joint = len(outs) == 1
    levels, piece = outs[0].shape[0], outs[0].shape[-2]
    tall, wide = total.shape
    row_blocks = tall // BLOCK
    for panel in range(wide // BLOCK):
        for block in range(row_blocks):
            value = total[block * BLOCK : (block + 1) * BLOCK, panel * BLOCK : (panel + 1) * BLOCK]
            for level in range(levels):
                even = value[2 * level * piece : (2 * level + 1) * piece]
                odd = value[(2 * level + 1) * piece : (2 * level + 2) * piece]
                place = panel * row_blocks + block
                for side in range(2):
                    chosen = jnp.where(x_here == side, even, odd)
                    if joint:
                        outs[0][level, side, place] = chosen
                    else:
                        outs[side][level, place] = chosen


def outer(left, right, side, sides, step, more=(), place=None, levels=0, joint=False, after=()):
    rows, width = left[0].shape
    cols = right[0].shape[1] // sides
    step = min(step, cols)
    tiles = cols // step
    ins = (
        [(a, whole(a.shape, True)) for a in left]
        + [
            (a, pl.BlockSpec((a.shape[0], step), lambda i, *_: (0, side * tiles + i)))
            for a in right
        ]
        + [(a, pl.BlockSpec((width, step), lambda i, *_: (0, i))) for a in more]
    )
    if not levels:
        outs = [(like((width, cols), BF16), pl.BlockSpec((width, step), lambda i: (0, i)))]
    else:
        piece = BLOCK // (2 * levels)
        held = step // BLOCK * (width // BLOCK)
        if joint:
            outs = [
                (
                    like((levels, 2, held * tiles, piece, BLOCK), BF16),
                    pl.BlockSpec((levels, 2, held, piece, BLOCK), lambda i, p: (0, 0, i, 0, 0)),
                )
            ]
        else:
            outs = [
                (
                    like((levels, held * tiles, piece, BLOCK), BF16),
                    pl.BlockSpec((levels, held, piece, BLOCK), lambda i, p: (0, i, 0, 0)),
                )
            ] * 2
    return launch(
        functools.partial(outer_kernel, len(left), len(right), len(more), levels > 0),
        "outer",
        (tiles,),
        ins,
        outs,
        scratch=[pltpu.VMEM((width, rows * len(left)), BF16)],
        prefetch=(place,) if levels else (),
        after=after,
    )


def two_parts(value):
    high = value.astype(BF16)
    return high, (value - high.astype(F32)).astype(BF16)


def step_kernel(g_ref, left_ref, right_ref, master_ref, grad_ref, stepped_ref, square_ref):
    owners, slots, piece, width = g_ref.shape
    for slot in range(slots):
        low = jnp.concatenate([g_ref[o, slot] for o in range(owners)], axis=0)
        grad_ref[slot] = low.astype(F32)
        high, rest = two_parts(left_ref[slot])
        turned = mm(high, low) + mm(rest, low)
        t_high, t_rest = two_parts(turned)
        r_high, r_rest = two_parts(right_ref[slot])
        direction = mm(t_high, r_high) + mm(t_high, r_rest) + mm(t_rest, r_high)
        stepped = master_ref[slot] - 0.3 * direction
        stepped_ref[slot] = stepped
        square_ref[slot : slot + 1] = jnp.sum(stepped * stepped, axis=0, keepdims=True)


def stats_kernel(g_ref, left_ref, right_ref, new_left_ref, new_right_ref):
    owners, slots, piece, width = g_ref.shape
    for slot in range(slots):
        low = jnp.concatenate([g_ref[o, slot] for o in range(owners)], axis=0)
        new_left_ref[slot] = 0.5 * left_ref[slot] + 0.5 * mm(low, low, NT)
        new_right_ref[slot] = 0.5 * right_ref[slot] + 0.5 * mm(low, low, TN)


def finish_kernel(stepped_ref, ema_ref, norm_ref, master_ref, new_ema_ref):
    slots = stepped_ref.shape[0]
    for slot in range(slots):
        master = stepped_ref[slot] * lax.rsqrt(norm_ref[slot : slot + 1] + 1e-06)
        master_ref[slot] = master
        new_ema_ref[slot] = 0.5 * ema_ref[slot] + 0.5 * master


def block_specs(count, slots):
    return pl.BlockSpec((slots, BLOCK, BLOCK), lambda i: (i, 0, 0))


def exchange(value, axis, pairs):
    return lax.ppermute(value, axis, pairs)


def shards(
    tokens,
    seq_lengths,
    qkv_weight,
    out_weight,
    up_gate_weight,
    down_weight,
    qk_scale,
    mlp_scale,
    eigen_rates,
    cotangent,
    block_order,
    master_blocks,
    ema_blocks,
    left_stats,
    right_stats,
    left_root,
    right_root,
):
    x_rows = tokens[0]
    total, width = x_rows.shape
    cols = qk_scale.shape[0]
    heads = lax.axis_size("head")
    owners = lax.axis_size("batch")
    ranks = heads // 2
    here = lax.axis_index("head")
    rank, core = here // 2, here % 2
    share = total // heads
    rows = share // CHUNKS
    tiles_all = total // rows

    core_swap = [(i, i ^ 1) for i in range(heads)]
    shift_up = [
        [(i, (i // 2 + s) % ranks * 2 + i % 2) for i in range(heads)] for s in range(ranks)
    ]
    shift_down = [
        [(i, (i // 2 - s) % ranks * 2 + i % 2) for i in range(heads)] for s in range(ranks)
    ]
    far_steps = list(range(1, ranks))
    ring = far_steps + [0]

    shares = jnp.stack(
        [(rank - s) % ranks * 2 + (core + d) % 2 for d in (1, 0) for s in ring]
    ).astype(jnp.int32)
    ends = jnp.cumsum(seq_lengths[0])

    def begin_of(row):
        segment = jnp.sum((row[:, None] >= ends[None, :]).astype(jnp.int32), axis=1)
        member = segment[:, None] == jnp.arange(ends.shape[0], dtype=jnp.int32)[None, :]
        return jnp.sum(jnp.where(member, (ends - seq_lengths[0])[None, :], 0), axis=1)

    tile_rows = jnp.arange(tiles_all, dtype=jnp.int32) * rows
    tile_begin = begin_of(tile_rows)
    lane = jnp.arange(LANES, dtype=jnp.int32) % (HEAD_DIM // 2)
    freq = 10000.0 ** (-lane.astype(F32) * 2.0 / HEAD_DIM)
    near_angle = jnp.arange(rows, dtype=F32)[:, None] * freq[None, :]
    far_angle = (tile_rows - tile_begin).astype(F32)[:, None] * freq[None, :]
    near = jnp.stack([jnp.cos(near_angle), jnp.sin(near_angle)])
    far = jnp.stack([jnp.cos(far_angle), jnp.sin(far_angle)])
    gains = qk_scale[None, :]
    rates = eigen_rates.T

    q, k, v, q_rot, k_rot = project(x_rows, qkv_weight, gains, near, far)
    weights = [
        (up_gate_weight, down_weight),
        (exchange(up_gate_weight, "head", core_swap), exchange(down_weight, "head", core_swap)),
    ]
    scales = jnp.concatenate([mlp_scale, exchange(mlp_scale, "head", core_swap)], axis=1)

    def from_partner(send, keep, size):
        got = exchange(send, "head", core_swap)
        if ranks == 1:
            return keep[:size], [keep, got]
        away = (keep[:-size].astype(F32) + got[:-size].astype(F32)).astype(BF16)
        return away, [keep, got] + from_ranks(away, size)

    def from_ranks(away, size):
        return [
            exchange(away[n * size : (n + 1) * size], "head", shift_down[s])
            for n, s in enumerate(far_steps)
        ]

    def gather_ranks(own):
        return [exchange(own, "head", shift_up[s]) for s in far_steps] + [own]

    def gather_shares(own):
        mine = gather_ranks(own)
        return [exchange(b, "head", core_swap) for b in mine] + mine

    places = [(here * CHUNKS + j).astype(jnp.int32)[None] for j in range(CHUNKS)]
    tiles = [shares * CHUNKS + j for j in range(CHUNKS)]
    starts = [begin_of(t * rows) for t in tiles]
    chunks = range(CHUNKS)
    tile = 2 * BLOCK

    attn_out, lse, parts = [], [], []
    last = ()
    for j in chunks:
        half = heads // 2
        first = attend(
            q, k, v, out_weight, tiles[j][:half], starts[j][:half], rows, 0, heads, last
        )
        second = attend(
            q,
            k,
            v,
            out_weight,
            tiles[j][half:],
            starts[j][half:],
            rows,
            half,
            heads,
            (first[0], first[1]),
            2,
        )
        away, got = from_partner(first[2], second[2], rows)
        attn_out.append(second[0])
        lse.append(second[1])
        parts.append(got)
        last = (away,)
    joined = []
    for j in chunks:
        joined.append(join_attention(parts[j], x_rows, places[j], rates, rows, last))
        last = (joined[j][0],)
    hidden = [gather_ranks(joined[j][0]) for j in chunks]
    ffn = []
    for j in chunks:
        ffn.append(mlp(hidden[j], weights, scales, tile, last))
        last = (ffn[j][4],)
    ends_fwd = []
    for j in chunks:
        parts = [ffn[j][4]] + from_ranks(ffn[j][3], rows)
        ends_fwd.append(
            join_mlp(parts, joined[j][1], cotangent[0], j, rates, rows, last)
        )
        last = (ends_fwd[j][1],)
    d_rows = [gather_ranks(ends_fwd[j][1]) for j in chunks]
    back = []
    for j in chunks:
        back.append(mlp_back(d_rows[j], ffn[j][0], ffn[j][1], weights, scales, tile, last))
        last = (back[j][4],)

    row_blocks = width // BLOCK
    piece = BLOCK // owners
    across = ranks
    levels = owners // across
    z_here, x_here = lax.axis_index("batch") // across, lax.axis_index("batch") % across
    direct = levels if piece % 16 == 0 and across == 2 else 0
    x_place = x_here.astype(jnp.int32)[None]
    left_hidden = [b for h in hidden for b in h]
    left_down = [b for d in d_rows for b in d]
    rights = {
        "down": (left_down, [f[2] for f in ffn]),
        "up": (left_hidden, [b[0] for b in back]),
        "gate": (left_hidden, [b[1] for b in back]),
    }

    def partner_part(name, after):
        out = outer(*rights[name], 1, 2, tile, after=after)[0]
        return out, exchange(out, "head", core_swap)

    def own_part(name, more, joint, after):
        return outer(
            *rights[name],
            0,
            2,
            tile,
            more=(more,),
            place=x_place,
            levels=direct,
            joint=joint,
            after=after,
        )

    def as_pieces(matrix):
        panels = matrix.shape[1] // BLOCK
        return (
            matrix.reshape(row_blocks, levels, across, piece, panels, BLOCK)
            .transpose(1, 2, 4, 0, 3, 5)
            .reshape(levels, across, panels * row_blocks * piece, BLOCK)
        )

    def from_this_x(pieces):
        return [
            lax.dynamic_index_in_dim(pieces, (x_here + s) % across, 1, keepdims=False)
            for s in range(across)
        ]

    def hold(value, anchor):
        return value if anchor is None else lax.optimization_barrier((value, anchor))[0]

    def over_x(pieces, anchor=None):
        total = pieces[0].astype(F32)
        for s in range(1, across):
            pairs = [
                (i, i // across * across + (i % across + s) % across) for i in range(owners)
            ]
            total = total + hold(exchange(pieces[s], "batch", pairs), anchor).astype(F32)
        return total.astype(BF16)

    def over_z(pieces, anchors=()):
        pick = lambda n: lax.dynamic_index_in_dim(
            pieces, jnp.clip(n, 0, levels - 1), 0, keepdims=False
        ).astype(F32)
        rising = falling = None
        for turn in range(1, levels):
            up = pick(z_here + levels - turn)
            down = pick(z_here - levels + turn)
            if turn > 1:
                up = up + rising.astype(F32)
                down = down + falling.astype(F32)
            rising = exchange(
                up.astype(BF16),
                "batch",
                [
                    (z * across + x, (z + 1) * across + x)
                    for z in range(min(turn, levels - 1))
                    for x in range(across)
                ],
            )
            falling = exchange(
                down.astype(BF16),
                "batch",
                [
                    (z * across + x, (z - 1) * across + x)
                    for z in range(max(levels - turn, 1), levels)
                    for x in range(across)
                ],
            )
            if turn <= len(anchors):
                rising, falling = hold((rising, falling), anchors[turn - 1])
        total = pick(z_here)
        if levels > 1:
            total = total + rising.astype(F32) + falling.astype(F32)
        return total.astype(BF16)

    split = []
    partner = {}
    for j in chunks:
        parts = [back[j][4]] + from_ranks(back[j][3], rows)
        split.append(
            split_attention(
                parts,
                ends_fwd[j][2],
                joined[j][1],
                joined[j][2],
                x_rows,
                places[j],
                rates,
                rows,
                last,
            )
        )
        last = (split[j][0],)
        if j == 0:
            out, partner["down"] = partner_part("down", last)
            last = (out,)
    for name in ("up", "gate"):
        out, partner[name] = partner_part(name, last)
        last = (out,)
    flat = lambda a: a.reshape(a.shape[:-3] + (-1, BLOCK))
    own = {}
    outer_marks = []
    for name in ("down", "up", "gate"):
        own[name] = own_part(name, partner[name], name == "down", last)
        last = (own[name][0],)
        outer_marks.append(own[name][0])
    d_attn_rows = [gather_shares(split[j][0]) for j in chunks]
    own["out"] = outer(
        [b for d in d_attn_rows for b in d],
        attn_out,
        0,
        1,
        tile,
        place=x_place,
        levels=direct,
        after=last,
    )
    last = (own["out"][0],)
    attn_back = []
    marks = []
    for j in chunks:
        pairs_back = []
        for pair in range(cols // LANES):
            pairs_back.append(
                attend_back(
                    d_attn_rows[j],
                    q,
                    k,
                    v,
                    attn_out[j],
                    lse[j],
                    out_weight,
                    tiles[j],
                    starts[j],
                    rows,
                    pair,
                    last,
                )
            )
            last = (pairs_back[-1][0],)
            marks.append(last[0])
        attn_back.append([[p[n] for p in pairs_back] for n in range(3)])

    def double(value, axis, size, anchors=()):
        step = 1
        turn = 0
        while step < size:
            got = exchange(value, axis, [(i, i ^ step) for i in range(size)])
            value = value + hold(got, anchors[turn] if turn < len(anchors) else None)
            step *= 2
            turn += 1
        return value

    rate_grad = double(
        jnp.concatenate([sum(s[2] for s in split), sum(e[3] for e in ends_fwd)], axis=0),
        "head",
        heads,
        outer_marks,
    )
    both = sum(b[2] for b in back)
    scale_cols = mlp_scale.shape[1]
    scale_grad = both[:, :scale_cols] + exchange(both[:, scale_cols:], "head", core_swap)
    small = double(
        jnp.concatenate([rate_grad.reshape(-1), scale_grad.reshape(-1)]).reshape(-1, LANES),
        "batch",
        owners,
        marks,
    )
    order = (shares[:, None] * CHUNKS + jnp.arange(CHUNKS, dtype=jnp.int32)[None, :]).reshape(-1)
    send, keep, gain_grad, *late = project_back(
        x_rows,
        q_rot,
        k_rot,
        qkv_weight,
        gains,
        near,
        far,
        attn_back,
        order,
        rows,
        x_place,
        direct,
        (small,),
    )

    def sides(outs):
        return [flat(o) for o in outs] if direct else from_this_x(as_pieces(outs[0]))

    if direct:
        down = list(over_z(flat(own["down"][0]), marks))
    else:
        down = over_z(jnp.stack(from_this_x(as_pieces(own["down"][0])), axis=1), marks)
    down = over_x(down, gain_grad)
    early = jnp.concatenate(
        [over_x(sides(own[name]), marks[-1]) for name in ("out", "up", "gate")], axis=1
    )
    early = over_z(early, (gain_grad,))
    late = over_z(over_x(sides(late)))
    _, parts = from_partner(send, keep, share)
    d_input = jnp.concatenate([s[1] for s in split], axis=0)
    d_input = d_input + sum(p[-share:].astype(F32) for p in parts)
    small = small.reshape(-1)
    rate_sum = small[: 2 * width].reshape(2, width)
    scale_sum = small[2 * width :].reshape(mlp_scale.shape)
    pieces = jnp.concatenate([late, early, down], axis=0).reshape(-1, piece, BLOCK)
    slot_order = block_order[0]
    ordered = jnp.take(pieces, slot_order, axis=0, mode="clip")
    per_owner = ordered.shape[0] // owners
    owned = lax.all_to_all(
        ordered.reshape(owners, per_owner, piece, BLOCK),
        "batch",
        split_axis=0,
        concat_axis=0,
        tiled=True,
    )
    slots = min(8, per_owner)
    if piece % 16:
        owned = owned.transpose(1, 0, 2, 3).reshape(1, per_owner, BLOCK, BLOCK)
    g_spec = pl.BlockSpec(
        (owned.shape[0], slots) + owned.shape[2:], lambda i: (0, i, 0, 0)
    )
    blk = pl.BlockSpec((slots, BLOCK, BLOCK), lambda i: (i, 0, 0))
    row = pl.BlockSpec((slots, BLOCK), lambda i: (i, 0))
    cube = jax.ShapeDtypeStruct((per_owner, BLOCK, BLOCK), F32)
    grid = (per_owner // slots,)
    owned_grad, stepped, column_sq = pl.pallas_call(
        step_kernel,
        grid=grid,
        in_specs=[g_spec, blk, blk, blk],
        out_specs=[blk, blk, row],
        out_shape=[cube, cube, jax.ShapeDtypeStruct((per_owner, BLOCK), F32)],
        name="step",
    )(owned, left_root[0], right_root[0], master_blocks[0])
    new_left, new_right = pl.pallas_call(
        stats_kernel,
        grid=grid,
        in_specs=[g_spec, blk, blk],
        out_specs=[blk, blk],
        out_shape=[cube, cube],
        name="stats",
    )(owned, left_stats[0], right_stats[0])
    panels = block_order.shape[1] // row_blocks
    my_blocks = lax.dynamic_slice_in_dim(
        slot_order, lax.axis_index("batch") * per_owner, per_owner, 0
    )
    member = (
        (my_blocks // row_blocks)[:, None] == jnp.arange(panels, dtype=jnp.int32)[None, :]
    ).astype(F32)
    precise = lax.Precision.HIGHEST
    sums = jnp.concatenate(
        [
            jnp.einsum("sp,sb->pb", member, column_sq, precision=precise),
            gain_grad.reshape(-1, LANES),
        ],
        axis=0,
    )
    sums = double(sums, "batch", owners)
    totals = sums[:panels]
    gain_sum = sums[panels:].reshape(-1)
    norms = jnp.einsum("sp,pb->sb", member, totals, precision=precise)
    new_master, new_ema = pl.pallas_call(
        finish_kernel,
        grid=grid,
        in_specs=[blk, blk, row],
        out_specs=[blk, blk],
        out_shape=[cube, cube],
        name="finish",
    )(stepped, ema_blocks[0], norms)
    gain_step = 0.5 / math.sqrt(total * owners)
    width_share = width // heads
    rate_here = lax.dynamic_slice_in_dim(rate_sum, here * width_share, width_share, 1)
    rate_slice = lax.dynamic_slice_in_dim(rates, here * width_share, width_share, 1)
    mlp_scale_out = jnp.stack([scale_sum, mlp_scale - gain_step * scale_sum])
    new_gains = jnp.concatenate(
        [(qk_scale - gain_step * gain_sum)[None, :], rate_slice - gain_step * rate_here], axis=0
    )
    out_share = jnp.concatenate([e[0] for e in ends_fwd], axis=0)
    return (
        out_share[None],
        d_input[None],
        owned_grad[None],
        new_master[None],
        new_ema[None],
        new_left[None],
        new_right[None],
        gain_sum,
        mlp_scale_out,
        rate_here.T,
        new_gains,
    )


def solution(mesh):
    return jax.shard_map(
        shards,
        mesh=mesh,
        in_specs=(
            P("batch", None, None),
            P("batch", None),
            P(None, None, "head"),
            P("head", None),
            P(None, None, "head"),
            P("head", None),
            P("head"),
            P(None, "head"),
            P(),
            P("batch", "head", None),
            P("head", None),
            P("head", "batch", None, None),
            P("head", "batch", None, None),
            P("head", "batch", None, None),
            P("head", "batch", None, None),
            P("head", "batch", None, None),
            P("head", "batch", None, None),
        ),
        out_specs=(
            P("batch", "head", None),
            P("batch", "head", None),
            P("head", "batch", None, None),
            P("head", "batch", None, None),
            P("head", "batch", None, None),
            P("head", "batch", None, None),
            P("head", "batch", None, None),
            P("head"),
            P(None, None, "head"),
            P("head", None),
            P(None, "head"),
        ),
        check_vma=False,
    )
```

```python
import functools
import math

import jax
import jax.numpy as jnp
from jax import lax
from jax.experimental import pallas as pl
from jax.experimental.pallas import tpu as pltpu
from jax.sharding import PartitionSpec as P

HEAD_DIM = 64
BLOCK = 128
LANES = 128
CHUNKS = 2
F32 = jnp.float32
BF16 = jnp.bfloat16
NN = (((1,), (0,)), ((), ()))
NT = (((1,), (1,)), ((), ()))
TN = (((0,), (0,)), ((), ()))
COST = pl.CostEstimate(flops=10**10, transcendentals=0, bytes_accessed=10**7)


def mm(a, b, dims=NN):
    return lax.dot_general(a, b, dims, preferred_element_type=F32)


def whole(shape, single=False):
    zeros = (0,) * len(shape)
    if single:
        return pl.BlockSpec(shape, lambda *_: zeros, pipeline_mode=pl.Buffered(1))
    return pl.BlockSpec(shape, lambda *_: zeros)


def launch(kernel, name, grid, ins, outs, scratch=(), prefetch=(), after=(), alias=0):
    first, count, extra = len(prefetch), len(ins), len(after)

    def body(*refs):
        kernel(*refs[: first + count], *refs[first + count + extra :])

    return pl.pallas_call(
        body,
        grid_spec=pltpu.PrefetchScalarGridSpec(
            num_scalar_prefetch=first,
            grid=grid,
            in_specs=[s for _, s in ins] + [pl.BlockSpec(memory_space=pl.ANY)] * extra,
            out_specs=[s for _, s in outs],
            scratch_shapes=list(scratch),
        ),
        out_shape=[o for o, _ in outs],
        input_output_aliases={first + count + n: n for n in range(alias)},
        name=name,
        cost_estimate=COST,
    )(*prefetch, *[a for a, _ in ins], *after)


def like(shape, dtype):
    return jax.ShapeDtypeStruct(shape, dtype)


def rms_rows(value):
    return value * lax.rsqrt(jnp.mean(value * value, axis=-1, keepdims=True) + 1e-06)


def rms_factor(value):
    return lax.rsqrt(jnp.mean(value * value, axis=-1, keepdims=True) + 1e-06)


def rms_back(normed, factor, gradient):
    return factor * (gradient - normed * jnp.mean(gradient * normed, axis=-1, keepdims=True))


def lane_ids():
    return lax.broadcasted_iota(jnp.int32, (1, LANES), 1)


def head_mean(value, ones_block):
    high = value.astype(BF16)
    rest = (value - high.astype(F32)).astype(BF16)
    return (mm(high, ones_block) + mm(rest, ones_block)) * (1.0 / HEAD_DIM)


def ones_block():
    row = lax.broadcasted_iota(jnp.int32, (LANES, LANES), 0) // HEAD_DIM
    col = lax.broadcasted_iota(jnp.int32, (LANES, LANES), 1) // HEAD_DIM
    return jnp.where(row == col, 1.0, 0.0).astype(BF16)


def half_turn(value):
    first = (lane_ids() & (HEAD_DIM - 1)) < HEAD_DIM // 2
    return jnp.where(
        first,
        pltpu.roll(value, LANES - HEAD_DIM // 2, 1),
        pltpu.roll(value, HEAD_DIM // 2, 1),
    )


def angles(tile, near_ref, far_ref):
    cos_r, sin_r = near_ref[0], near_ref[1]
    cos_0 = far_ref[0, pl.ds(tile, 1), :]
    sin_0 = far_ref[1, pl.ds(tile, 1), :]
    first = (lane_ids() & (HEAD_DIM - 1)) < HEAD_DIM // 2
    sine = sin_0 * cos_r + cos_0 * sin_r
    return cos_0 * cos_r - sin_0 * sin_r, jnp.where(first, -sine, sine)


def project_kernel(
    x_ref, w_ref, gain_ref, near_ref, far_ref, q_ref, k_ref, v_ref, q_rot_ref, k_rot_ref
):
    tile = pl.program_id(0)
    cosine, sine = angles(tile, near_ref, far_ref)
    ones = ones_block()
    x = x_ref[...]
    for index, used_ref, rot_ref in ((0, q_ref, q_rot_ref), (1, k_ref, k_rot_ref)):
        raw = mm(x, w_ref[index])
        for pair in range(raw.shape[1] // LANES):
            lanes = slice(pair * LANES, (pair + 1) * LANES)
            value = raw[:, lanes]
            turned = value * cosine + half_turn(value) * sine
            factor = lax.rsqrt(head_mean(turned * turned, ones) + 1e-06)
            rot_ref[:, lanes] = turned
            used_ref[:, lanes] = (turned * factor * gain_ref[:, lanes]).astype(BF16)
    v_ref[...] = mm(x, w_ref[2]).astype(BF16)


def project(x, weight, gains, near, far):
    rows, width = x.shape
    cols = weight.shape[2]
    tile = near.shape[1]
    by_row = lambda w: pl.BlockSpec((tile, w), lambda i: (i, 0))
    return pl.pallas_call(
        project_kernel,
        grid=(rows // tile,),
        in_specs=[
            by_row(width),
            whole(weight.shape, True),
            whole((1, cols)),
            whole(near.shape),
            whole(far.shape),
        ],
        out_specs=[by_row(cols)] * 5,
        out_shape=[jax.ShapeDtypeStruct((rows, cols), BF16)] * 3
        + [jax.ShapeDtypeStruct((rows, cols), F32)] * 2,
        name="project",
        cost_estimate=COST,
    )(x, weight, gains, near, far)


def key_tiles(first_row, start, wide, narrow, visit):
    full = first_row // wide

    def step(index, carry):
        visit(pl.multiple_of(index * wide, wide), wide, False)
        return carry

    lax.fori_loop(start // wide, full, step, 0)
    diagonal = (first_row // narrow) * narrow

    @pl.when(diagonal > full * wide)
    def _():
        visit(pl.multiple_of(full * wide, narrow), narrow, False)

    visit(pl.multiple_of(diagonal, narrow), narrow, True)


def attend_kernel(
    wide, tiles, starts, q_ref, k_ref, v_ref, w_ref, o_ref, lse_ref, part_ref, acc
):
    index = pl.program_id(0)
    rows = q_ref.shape[0]
    first_row = tiles[index] * rows
    start = starts[index]
    narrow = wide // 2
    low = lane_ids() < HEAD_DIM
    zero = jnp.zeros((), BF16)
    results = []
    for pair in range(q_ref.shape[1] // LANES):
        lanes = slice(pair * LANES, (pair + 1) * LANES)
        q = q_ref[:, lanes] * jnp.asarray(1.0 / math.sqrt(HEAD_DIM), BF16)
        q_both = jnp.concatenate([jnp.where(low, q, zero), jnp.where(low, zero, q)], axis=0)
        acc[...] = jnp.zeros_like(acc)

        def visit(key_0, size, masked):
            keys = pl.ds(key_0, size)
            weights = jnp.exp(mm(q_both, k_ref[keys, lanes], NT))
            if masked:
                row = lax.broadcasted_iota(jnp.int32, (2 * rows, size), 0)
                row = jnp.where(row < rows, row, row - rows) + first_row
                col = lax.broadcasted_iota(jnp.int32, (2 * rows, size), 1) + key_0
                weights = jnp.where((col <= row) & (col >= start), weights, 0.0)
            total = weights[:, :LANES]
            for part in range(1, size // LANES):
                total = total + weights[:, part * LANES : (part + 1) * LANES]
            acc[:, LANES:] += total
            acc[:, :LANES] += mm(weights.astype(BF16), v_ref[keys, lanes])

        key_tiles(first_row, start, wide, narrow, visit)
        total_a = jnp.sum(acc[:rows, LANES:], axis=1, keepdims=True)
        total_b = jnp.sum(acc[rows:, LANES:], axis=1, keepdims=True)
        summed = jnp.where(low, acc[:rows, :LANES], acc[rows:, :LANES])
        out = (summed / jnp.where(low, total_a, total_b)).astype(BF16)
        o_ref[:, lanes] = out
        lse_ref[:, lanes] = jnp.log(jnp.where(low, total_b, total_a))
        results.append(out)
    part_ref[...] = mm(jnp.concatenate(results, axis=1), w_ref[...]).astype(BF16)


def attend(q, k, v, weight, tiles, starts, rows, offset, places, after, alias=0):
    count = tiles.shape[0]
    cols = k.shape[1]
    width = weight.shape[1]
    at_place = pl.BlockSpec((rows, cols), lambda i, t, s: (i + offset, 0))
    return launch(
        functools.partial(attend_kernel, 4 * BLOCK),
        "attend",
        (count,),
        [
            (q, pl.BlockSpec((rows, cols), lambda i, t, s: (t[i], 0))),
            (k, whole(k.shape, True)),
            (v, whole(v.shape, True)),
            (weight, whole(weight.shape, True)),
        ],
        [
            (like((places * rows, cols), BF16), at_place),
            (like((places * rows, cols), F32), at_place),
            (like((count * rows, width), BF16), pl.BlockSpec((rows, width), lambda i, t, s: (i, 0))),
        ],
        scratch=[pltpu.VMEM((2 * rows, 2 * LANES), F32)],
        prefetch=(tiles, starts),
        after=after,
        alias=alias,
    )


def attend_back_kernel(blocks, wide, tiles, starts, *refs):
    row_refs = refs[:blocks]
    q_ref, k_ref, v_ref, o_ref, lse_ref, w_ref = refs[blocks : blocks + 6]
    dq_ref, dk_ref, dv_ref, rows_s, acc = refs[blocks + 6 :]
    index = pl.program_id(0)
    rows = q_ref.shape[0]
    narrow = wide // 2

    @pl.when(index == 0)
    def _():
        dk_ref[...] = jnp.zeros_like(dk_ref)
        dv_ref[...] = jnp.zeros_like(dv_ref)

    for block in range(blocks):

        @pl.when(index == block)
        def _(block=block):
            rows_s[...] = row_refs[block][...]

    first_row = tiles[index] * rows
    start = starts[index]
    low = lane_ids() < HEAD_DIM
    place = lane_ids() & (HEAD_DIM - 1)
    zero = jnp.zeros((), BF16)
    ones = jnp.where(place < 3, 1.0, 0.0).astype(BF16)

    def parts(value):
        high = value.astype(BF16).astype(F32)
        rest = value - high
        middle = rest.astype(BF16).astype(F32)
        picked = jnp.where(place == 1, middle, jnp.where(place == 2, rest - middle, 0.0))
        return jnp.where(place == 0, high, picked).astype(BF16)

    d_rows = rows_s[...]
    d_attn = mm(d_rows, w_ref[...], NT).astype(BF16)
    for pair in range(q_ref.shape[1] // LANES):
        lanes = slice(pair * LANES, (pair + 1) * LANES)
        q = q_ref[:, lanes] * jnp.asarray(1.0 / math.sqrt(HEAD_DIM), BF16)
        d_out = d_attn[:, lanes]
        minus_lse = parts(-lse_ref[:, lanes])
        product = d_out.astype(F32) * o_ref[:, lanes].astype(F32)
        sum_a = jnp.sum(jnp.where(low, product, 0.0), axis=1, keepdims=True)
        sum_b = jnp.sum(jnp.where(low, 0.0, product), axis=1, keepdims=True)
        minus_delta = parts(-jnp.where(low, sum_b, sum_a))
        q_ext = (jnp.where(low, q, minus_lse), jnp.where(low, minus_lse, q))
        d_ext = (jnp.where(low, d_out, minus_delta), jnp.where(low, minus_delta, d_out))
        q_both = jnp.concatenate([jnp.where(low, q, zero), jnp.where(low, zero, q)], axis=0)
        d_both = jnp.concatenate(
            [jnp.where(low, d_out, zero), jnp.where(low, zero, d_out)], axis=0
        )
        acc[...] = jnp.zeros_like(acc)

        def visit(key_0, size, masked):
            keys = pl.ds(key_0, size)
            k = k_ref[keys, lanes]
            v = v_ref[keys, lanes]
            k_ext = (jnp.where(low, k, ones), jnp.where(low, ones, k))
            v_ext = (jnp.where(low, v, ones), jnp.where(low, ones, v))
            if masked:
                col = lax.broadcasted_iota(jnp.int32, (size, rows), 1) + first_row
                row = lax.broadcasted_iota(jnp.int32, (size, rows), 0) + key_0
                allowed = (row <= col) & (row >= start)
            probs = []
            d_scores = []
            for head in range(2):
                prob = jnp.exp(mm(k_ext[head], q_ext[head], NT))
                if masked:
                    prob = jnp.where(allowed, prob, 0.0)
                d_score = prob * mm(v_ext[head], d_ext[head], NT)
                probs.append(prob.astype(BF16))
                d_scores.append(d_score.astype(BF16))
            dv_ref[keys, lanes] += mm(jnp.concatenate(probs, axis=1), d_both)
            dk_ref[keys, lanes] += mm(jnp.concatenate(d_scores, axis=1), q_both)
            k_both = jnp.concatenate([jnp.where(low, k, zero), jnp.where(low, zero, k)], axis=0)
            acc[...] += mm(jnp.concatenate(d_scores, axis=0), k_both, TN)

        key_tiles(first_row, start, wide, narrow, visit)
        dq_ref[:, lanes] = acc[...] * (1.0 / math.sqrt(HEAD_DIM))


def attend_back(row_blocks, q, k, v, o, lse, weight, tiles, starts, rows, pair, after):
    count = tiles.shape[0]
    total = k.shape[0]
    width = weight.shape[1]
    at_tile = pl.BlockSpec((rows, LANES), lambda i, t, s: (t[i], pair))
    at_step = pl.BlockSpec((rows, LANES), lambda i, t, s: (i, pair))
    column = pl.BlockSpec((total, LANES), lambda *_: (0, pair), pipeline_mode=pl.Buffered(1))
    return launch(
        functools.partial(attend_back_kernel, len(row_blocks), 4 * BLOCK),
        "attend_back",
        (count,),
        [(b, whole(b.shape, True)) for b in row_blocks]
        + [
            (q, at_tile),
            (k, column),
            (v, column),
            (o, at_step),
            (lse, at_step),
            (weight, pl.BlockSpec((LANES, width), lambda *_: (pair, 0))),
        ],
        [
            (like((count * rows, LANES), F32), pl.BlockSpec((rows, LANES), lambda i, *_: (i, 0))),
            (like((total, LANES), F32), whole((total, LANES))),
            (like((total, LANES), F32), whole((total, LANES))),
        ],
        scratch=[pltpu.VMEM((rows, width), BF16), pltpu.VMEM((rows, LANES), F32)],
        prefetch=(tiles, starts),
        after=after,
    )


def sum_parts(refs):
    total = refs[0][...].astype(F32)
    for ref in refs[1:]:
        total = total + ref[...].astype(F32)
    return total


def join_attention_kernel(parts, place, *refs):
    x_ref, rate_ref = refs[parts : parts + 2]
    low_ref, hidden_ref, branch_ref = refs[parts + 2 :]
    branch = sum_parts(refs[:parts])
    x = x_ref[...].astype(F32)
    hidden = rms_rows(x + rate_ref[0:1] * (rms_rows(branch) - x))
    branch_ref[...] = branch
    hidden_ref[...] = hidden
    low_ref[...] = hidden.astype(BF16)


def part_specs(parts, rows, width):
    return [
        pl.BlockSpec((rows, width), lambda i, *_, last=a.shape[0] // rows: (last - SUB + i, 0))
        for a in parts
    ]


SUB = 2


def join_attention(parts, x, place, rates, share, after):
    width = x.shape[1]
    rows = share // SUB
    here = pl.BlockSpec((rows, width), lambda i, p: (i, 0))
    return launch(
        functools.partial(join_attention_kernel, len(parts)),
        "join_attention",
        (SUB,),
        list(zip(parts, part_specs(parts, rows, width), strict=True))
        + [
            (x, pl.BlockSpec((rows, width), lambda i, p: (p[0] * SUB + i, 0))),
            (rates, whole(rates.shape)),
        ],
        [(like((share, width), d), here) for d in (BF16, F32, F32)],
        prefetch=(place,),
        after=after,
    )


def weight_tiles(weight, down, step, side):
    _, width, cols = weight.shape
    count = cols // step
    if side == 0:
        at = lambda t: jnp.minimum(t, count - 1)
    else:
        at = lambda t: jnp.maximum(t - count, 0)
    return [
        (weight, pl.BlockSpec((2, width, step), lambda t, *_: (0, 0, at(t)))),
        (down, pl.BlockSpec((step, width), lambda t, *_: (at(t), 0))),
    ]


def mlp_kernel(blocks, *refs):
    row_refs = refs[:blocks]
    sides = (refs[blocks : blocks + 2], refs[blocks + 2 : blocks + 4])
    scale_ref = refs[blocks + 4]
    up_ref, gate_ref, mixed_ref, away_ref, own_ref, x_s, acc = refs[blocks + 5 :]
    tile = pl.program_id(0)
    count = pl.num_programs(0)
    rows = row_refs[0].shape[0]

    @pl.when(tile == 0)
    def _():
        for block in range(blocks):
            x_s[block * rows : (block + 1) * rows] = row_refs[block][...]
        acc[...] = jnp.zeros_like(acc)

    def run(w_ref, down_ref):
        x = x_s[...]
        up = mm(x, w_ref[0])
        gate = mm(x, w_ref[1])
        up_ref[...] = up.astype(BF16)
        gate_ref[...] = gate.astype(BF16)
        scaled = gate * scale_ref[1:2]
        mixed = (up * scale_ref[0:1] * (scaled * jax.nn.sigmoid(scaled))).astype(BF16)
        mixed_ref[...] = mixed
        acc[...] += mm(mixed, down_ref[...])

    for side in range(2):

        @pl.when(tile // (count // 2) == side)
        def _(side=side):
            run(*sides[side])

    @pl.when(tile == count - 1)
    def _():
        last = (blocks - 1) * rows
        own_ref[...] = acc[last:]
        if blocks > 1:
            away_ref[...] = acc[:last].astype(BF16)


def mlp(row_blocks, weights, scales, step, after):
    rows, width = row_blocks[0].shape
    blocks = len(row_blocks)
    height = rows * blocks
    cols = 2 * weights[0][0].shape[2]
    at_tile = lambda h: pl.BlockSpec((h, step), lambda t: (0, t))
    far = max(blocks - 1, 1) * rows
    return launch(
        functools.partial(mlp_kernel, blocks),
        "mlp",
        (cols // step,),
        [(b, whole(b.shape, True)) for b in row_blocks]
        + weight_tiles(*weights[0], step, 0)
        + weight_tiles(*weights[1], step, 1)
        + [(scales, at_tile(2))],
        [(like((height, cols), BF16), at_tile(height))] * 3
        + [
            (like((far, width), BF16), whole((far, width))),
            (like((rows, width), F32), whole((rows, width))),
        ],
        scratch=[pltpu.VMEM((height, width), BF16), pltpu.VMEM((height, width), F32)],
        after=after,
    )


def join_mlp_kernel(parts, *refs):
    hidden_ref, cot_ref, rate_ref = refs[parts : parts + 3]
    out_ref, low_ref, d_hidden_ref, rate_grad_ref = refs[parts + 3 :]
    branch = sum_parts(refs[:parts])
    hidden = hidden_ref[...]
    rate = rate_ref[1:2]
    factor = rms_factor(branch)
    normed = branch * factor
    gap = normed - hidden
    before = hidden + rate * gap
    factor_out = rms_factor(before)
    out = before * factor_out
    d_before = rms_back(out, factor_out, cot_ref[...].astype(F32))
    out_ref[...] = out
    d_hidden_ref[...] = (1.0 - rate) * d_before
    low_ref[...] = rms_back(normed, factor, rate * d_before).astype(BF16)

    @pl.when(pl.program_id(0) == 0)
    def _():
        rate_grad_ref[...] = jnp.zeros_like(rate_grad_ref)

    rate_grad_ref[...] += jnp.sum(d_before * gap, axis=0, keepdims=True)


def join_mlp(parts, hidden, cotangent, chunk, rates, share, after):
    width = hidden.shape[1]
    rows = share // SUB
    here = pl.BlockSpec((rows, width), lambda i: (i, 0))
    return launch(
        functools.partial(join_mlp_kernel, len(parts)),
        "join_mlp",
        (SUB,),
        list(zip(parts, part_specs(parts, rows, width), strict=True))
        + [
            (hidden, here),
            (cotangent, pl.BlockSpec((rows, width), lambda i: (chunk * SUB + i, 0))),
            (rates, whole(rates.shape)),
        ],
        [(like((share, width), d), here) for d in (F32, BF16, F32)]
        + [(like((1, width), F32), whole((1, width)))],
        after=after,
    )


def mlp_back_kernel(blocks, *refs):
    row_refs = refs[:blocks]
    sides = (refs[blocks : blocks + 2], refs[blocks + 2 : blocks + 4])
    scale_ref, up_ref, gate_ref = refs[blocks + 4 : blocks + 7]
    d_up_ref, d_gate_ref, sums_ref, away_ref, own_ref, x_s, acc = refs[blocks + 7 :]
    tile = pl.program_id(0)
    count = pl.num_programs(0)
    rows = row_refs[0].shape[0]

    @pl.when(tile == 0)
    def _():
        for block in range(blocks):
            x_s[block * rows : (block + 1) * rows] = row_refs[block][...]
        acc[...] = jnp.zeros_like(acc)

    def run(w_ref, down_ref):
        d_mixed = mm(x_s[...], down_ref[...], NT)
        up_raw = up_ref[...].astype(F32)
        gate_raw = gate_ref[...].astype(F32)
        scale_up = scale_ref[0:1]
        scale_gate = scale_ref[1:2]
        gate = gate_raw * scale_gate
        sig = jax.nn.sigmoid(gate)
        d_up = d_mixed * (gate * sig)
        d_gate = d_mixed * (up_raw * scale_up) * (sig * (1.0 + gate * (1.0 - sig)))
        sums_ref[0:1] = jnp.sum(d_up * up_raw, axis=0, keepdims=True)
        sums_ref[1:2] = jnp.sum(d_gate * gate_raw, axis=0, keepdims=True)
        d_up = (d_up * scale_up).astype(BF16)
        d_gate = (d_gate * scale_gate).astype(BF16)
        d_up_ref[...] = d_up
        d_gate_ref[...] = d_gate
        acc[...] += mm(d_up, w_ref[0], NT) + mm(d_gate, w_ref[1], NT)

    for side in range(2):

        @pl.when(tile // (count // 2) == side)
        def _(side=side):
            run(*sides[side])

    @pl.when(tile == count - 1)
    def _():
        last = (blocks - 1) * rows
        own_ref[...] = acc[last:]
        if blocks > 1:
            away_ref[...] = acc[:last].astype(BF16)


def mlp_back(row_blocks, up, gate, weights, scales, step, after):
    rows, width = row_blocks[0].shape
    blocks = len(row_blocks)
    height = rows * blocks
    cols = 2 * weights[0][0].shape[2]
    at_tile = lambda h: pl.BlockSpec((h, step), lambda t: (0, t))
    far = max(blocks - 1, 1) * rows
    return launch(
        functools.partial(mlp_back_kernel, blocks),
        "mlp_back",
        (cols // step,),
        [(b, whole(b.shape, True)) for b in row_blocks]
        + weight_tiles(*weights[0], step, 0)
        + weight_tiles(*weights[1], step, 1)
        + [(scales, at_tile(2)), (up, at_tile(height)), (gate, at_tile(height))],
        [(like((height, cols), BF16), at_tile(height))] * 2
        + [
            (like((2, cols), F32), at_tile(2)),
            (like((far, width), BF16), whole((far, width))),
            (like((rows, width), F32), whole((rows, width))),
        ],
        scratch=[pltpu.VMEM((height, width), BF16), pltpu.VMEM((height, width), F32)],
        after=after,
    )


def split_attention_kernel(parts, place, *refs):
    d_hidden_ref, hidden_ref, branch_ref, x_ref, rate_ref = refs[parts : parts + 5]
    low_ref, d_input_ref, rate_grad_ref = refs[parts + 5 :]
    d_hidden = sum_parts(refs[:parts]) + d_hidden_ref[...]
    hidden = hidden_ref[...]
    branch = branch_ref[...]
    x = x_ref[...].astype(F32)
    rate = rate_ref[0:1]
    factor = rms_factor(branch)
    normed = branch * factor
    gap = normed - x
    d_before = rms_back(hidden, rms_factor(x + rate * gap), d_hidden)
    d_input_ref[...] = (1.0 - rate) * d_before
    low_ref[...] = rms_back(normed, factor, rate * d_before).astype(BF16)

    @pl.when(pl.program_id(0) == 0)
    def _():
        rate_grad_ref[...] = jnp.zeros_like(rate_grad_ref)

    rate_grad_ref[...] += jnp.sum(d_before * gap, axis=0, keepdims=True)


def split_attention(parts, d_hidden, hidden, branch, x, place, rates, share, after):
    width = x.shape[1]
    rows = share // SUB
    here = pl.BlockSpec((rows, width), lambda i, p: (i, 0))
    return launch(
        functools.partial(split_attention_kernel, len(parts)),
        "split_attention",
        (SUB,),
        list(zip(parts, part_specs(parts, rows, width), strict=True))
        + [(d_hidden, here), (hidden, here), (branch, here)]
        + [
            (x, pl.BlockSpec((rows, width), lambda i, p: (p[0] * SUB + i, 0))),
            (rates, whole(rates.shape)),
        ],
        [(like((share, width), d), here) for d in (BF16, F32)]
        + [(like((1, width), F32), whole((1, width)))],
        prefetch=(place,),
        after=after,
    )


def project_back_kernel(order, x_here, *refs):
    x_ref, q_rot_ref, k_rot_ref, gain_ref, near_ref, far_ref = refs[:6]
    d_refs = refs[6 : 6 + 3 * CHUNKS]
    part = lambda which: d_refs[which * CHUNKS : (which + 1) * CHUNKS]
    raw_ref, gain_grad_ref = refs[6 + 3 * CHUNKS : 8 + 3 * CHUNKS]
    grad_refs = refs[8 + 3 * CHUNKS : -1]
    acc = refs[-1]
    index = pl.program_id(0)
    count = pl.num_programs(0)

    @pl.when(index == 0)
    def _():
        gain_grad_ref[...] = jnp.zeros_like(gain_grad_ref)
        acc[...] = jnp.zeros_like(acc)

    cosine, sine = angles(order[index], near_ref, far_ref)
    ones = ones_block()
    chunk = index % CHUNKS
    d_raw = []
    for which, rot_ref in ((0, q_rot_ref), (1, k_rot_ref)):
        if which == 0:
            d_used = part(0)[0][...]
            for other in range(1, CHUNKS):
                d_used = jnp.where(chunk == other, part(0)[other][...], d_used)
        else:
            d_used = sum_parts(part(1))
        turned = rot_ref[...]
        factor = lax.rsqrt(head_mean(turned * turned, ones) + 1e-06)
        normed = turned * factor
        gain_grad_ref[...] += jnp.sum(d_used * normed, axis=0, keepdims=True)
        d_normed = d_used * gain_ref[...]
        d_turned = factor * (d_normed - normed * head_mean(d_normed * normed, ones))
        d_raw.append((d_turned * cosine - half_turn(d_turned) * sine).astype(BF16))
    d_raw.append(sum_parts(part(2)).astype(BF16))
    d_all = jnp.concatenate(d_raw, axis=1)
    raw_ref[...] = d_all
    acc[...] += mm(d_all, x_ref[...], TN)

    @pl.when(index == count - 1)
    def _():
        total = acc[...].T.astype(BF16)
        if len(grad_refs) == 1:
            grad_refs[0][...] = total
        else:
            store_pieces(total, x_here[0], *grad_refs)


def project_back(x, q_rot, k_rot, gains, near, far, parts, order, rows, pair, place, levels, after):
    total, width = x.shape
    count = order.shape[0]
    wide = 3 * LANES
    at_tile = lambda w, n: pl.BlockSpec((rows, w), lambda i, t, *_: (t[i], n))
    if levels:
        shape = (levels, 3 * (width // BLOCK), BLOCK // (2 * levels), BLOCK)
        grads = [(like(shape, BF16), whole(shape))] * 2
    else:
        grads = [(like((width, wide), BF16), whole((width, wide)))]
    return launch(
        project_back_kernel,
        "project_back",
        (count,),
        [
            (x, at_tile(width, 0)),
            (q_rot, at_tile(LANES, pair)),
            (k_rot, at_tile(LANES, pair)),
            (gains, pl.BlockSpec((1, LANES), lambda *_: (0, pair))),
            (near, whole(near.shape)),
            (far, whole(far.shape)),
        ]
        + [
            (chunk[0], pl.BlockSpec((rows, LANES), lambda i, *_: (i // CHUNKS, 0)))
            for chunk in parts
        ]
        + [(chunk[which], at_tile(LANES, 0)) for which in (1, 2) for chunk in parts],
        [
            (like((total, wide), BF16), at_tile(wide, 0)),
            (like((1, LANES), F32), whole((1, LANES))),
        ]
        + grads,
        scratch=[pltpu.VMEM((wide, width), F32)],
        prefetch=(order, place),
        after=after,
    )


def input_back_kernel(pairs, order, *refs):
    raw_refs = refs[:pairs]
    w_ref, send_ref, keep_ref = refs[pairs : pairs + 3]
    index = pl.program_id(0)
    count = pl.num_programs(0)
    d_x = None
    for which in range(3):
        lanes = slice(which * LANES, (which + 1) * LANES)
        d_all = jnp.concatenate([r[:, lanes] for r in raw_refs], axis=1)
        product = mm(d_all, w_ref[which], NT)
        d_x = product if d_x is None else d_x + product
    d_x = d_x.astype(BF16)

    @pl.when(index < count // 2)
    def _():
        send_ref[...] = d_x

    @pl.when(index >= count // 2)
    def _():
        keep_ref[...] = d_x


def input_back(raws, weight, order, rows, after):
    count = order.shape[0]
    half = count // 2
    width = weight.shape[1]
    out = like((half * rows, width), BF16)
    return launch(
        functools.partial(input_back_kernel, len(raws)),
        "input_back",
        (count,),
        [(r, pl.BlockSpec((rows, r.shape[1]), lambda i, t: (t[i], 0))) for r in raws]
        + [(weight, whole(weight.shape, True))],
        [
            (out, pl.BlockSpec((rows, width), lambda i, *_: (jnp.minimum(i, half - 1), 0))),
            (out, pl.BlockSpec((rows, width), lambda i, *_: (jnp.maximum(i - half, 0), 0))),
        ],
        prefetch=(order,),
        after=after,
    )


def join_x_kernel(place, mine_ref, got_ref, *out_refs):
    levels = len(out_refs)
    for step in range(levels):
        level = (place[0] + step) % levels
        both = mine_ref[level].astype(F32) + got_ref[level].astype(F32)
        out_refs[step][...] = both.astype(BF16)


def join_x(mine, got, z_place, after):
    levels, height, width = mine.shape
    return launch(
        join_x_kernel,
        "join_x",
        (1,),
        [(mine, whole(mine.shape)), (got, whole(got.shape))],
        [(like((height, width), BF16), whole((height, width)))] * levels,
        prefetch=(z_place,),
        after=after,
    )


def order_kernel(counts, order, *refs):
    groups = []
    at = 0
    for n in counts:
        groups.append(refs[at : at + n])
        at += n
    out_ref, held = refs[at:]
    row = 0
    for group in groups:
        total = sum_parts(group)
        height = total.shape[0]
        held[row : row + height] = total.astype(BF16)
        row += height
    slots, piece, _ = out_ref.shape

    def move(slot, carry):
        start = pl.multiple_of(order[slot] * piece, piece)
        out_ref[slot] = held[pl.ds(start, piece)]
        return carry

    lax.fori_loop(0, slots, move, 0, unroll=8)


def order_pieces(groups, order, piece, after):
    arrays = [a for g in groups for a in g]
    slots = order.shape[0]
    shape = (slots, piece, BLOCK)
    return launch(
        functools.partial(order_kernel, [len(g) for g in groups]),
        "order_pieces",
        (1,),
        [(a, whole(a.shape)) for a in arrays],
        [(like(shape, BF16), whole(shape))],
        scratch=[pltpu.VMEM((slots * piece, BLOCK), BF16)],
        prefetch=(order,),
        after=after,
    )[0]


def outer_kernel(lefts, rights, has_more, pieces, *refs):
    if pieces:
        place, refs = refs[0], refs[1:]
    left_refs = refs[:lefts]
    right_refs = refs[lefts : lefts + rights]
    more_refs = refs[lefts + rights : lefts + rights + has_more]
    out_refs = refs[lefts + rights + has_more : -1]
    turned = refs[-1]
    rows = left_refs[0].shape[0]

    @pl.when(pl.program_id(0) == 0)
    def _():
        for block in range(lefts):
            turned[:, block * rows : (block + 1) * rows] = left_refs[block][...].T

    high = right_refs[0].shape[0]
    total = mm(turned[:, :high], right_refs[0][...])
    for n in range(1, rights):
        total = total + mm(turned[:, n * high : (n + 1) * high], right_refs[n][...])
    for more in more_refs:
        total = total + more[...].astype(F32)
    total = total.astype(BF16)
    if not pieces:
        out_refs[0][...] = total
        return
    store_pieces(total, place[0], *out_refs)


def store_pieces(total, x_here, *outs):
    levels, piece = outs[0].shape[0], outs[0].shape[-2]
    tall, wide = total.shape
    row_blocks = tall // BLOCK
    for panel in range(wide // BLOCK):
        for block in range(row_blocks):
            value = total[block * BLOCK : (block + 1) * BLOCK, panel * BLOCK : (panel + 1) * BLOCK]
            for level in range(levels):
                even = value[2 * level * piece : (2 * level + 1) * piece]
                odd = value[(2 * level + 1) * piece : (2 * level + 2) * piece]
                place = panel * row_blocks + block
                for side in range(2):
                    chosen = jnp.where(x_here == side, even, odd)
                    outs[side][level, place] = chosen


def outer(left, right, side, sides, step, more=(), place=None, levels=0, after=()):
    rows, width = left[0].shape
    cols = right[0].shape[1] // sides
    step = min(step, cols)
    tiles = cols // step
    ins = (
        [(a, whole(a.shape, True)) for a in left]
        + [
            (a, pl.BlockSpec((a.shape[0], step), lambda i, *_: (0, side * tiles + i)))
            for a in right
        ]
        + [(a, pl.BlockSpec((width, step), lambda i, *_: (0, i))) for a in more]
    )
    if not levels:
        outs = [(like((width, cols), BF16), pl.BlockSpec((width, step), lambda i: (0, i)))]
    else:
        piece = BLOCK // (2 * levels)
        held = step // BLOCK * (width // BLOCK)
        outs = [
            (
                like((levels, held * tiles, piece, BLOCK), BF16),
                pl.BlockSpec((levels, held, piece, BLOCK), lambda i, p: (0, i, 0, 0)),
            )
        ] * 2
    return launch(
        functools.partial(outer_kernel, len(left), len(right), len(more), levels > 0),
        "outer",
        (tiles,),
        ins,
        outs,
        scratch=[pltpu.VMEM((width, rows * len(left)), BF16)],
        prefetch=(place,) if levels else (),
        after=after,
    )


def two_parts(value):
    high = value.astype(BF16)
    return high, (value - high.astype(F32)).astype(BF16)


def step_kernel(g_ref, left_ref, right_ref, master_ref, grad_ref, stepped_ref, square_ref):
    owners, slots, piece, width = g_ref.shape
    for slot in range(slots):
        low = jnp.concatenate([g_ref[o, slot] for o in range(owners)], axis=0)
        grad_ref[slot] = low.astype(F32)
        high, rest = two_parts(left_ref[slot])
        turned = mm(high, low) + mm(rest, low)
        t_high, t_rest = two_parts(turned)
        r_high, r_rest = two_parts(right_ref[slot])
        direction = mm(t_high, r_high) + mm(t_high, r_rest) + mm(t_rest, r_high)
        stepped = master_ref[slot] - 0.3 * direction
        stepped_ref[slot] = stepped
        square_ref[slot : slot + 1] = jnp.sum(stepped * stepped, axis=0, keepdims=True)


def stats_kernel(g_ref, left_ref, right_ref, new_left_ref, new_right_ref):
    owners, slots, piece, width = g_ref.shape
    for slot in range(slots):
        low = jnp.concatenate([g_ref[o, slot] for o in range(owners)], axis=0)
        new_left_ref[slot] = 0.5 * left_ref[slot] + 0.5 * mm(low, low, NT)
        new_right_ref[slot] = 0.5 * right_ref[slot] + 0.5 * mm(low, low, TN)


def finish_kernel(stepped_ref, ema_ref, norm_ref, master_ref, new_ema_ref):
    slots = stepped_ref.shape[0]
    for slot in range(slots):
        master = stepped_ref[slot] * lax.rsqrt(norm_ref[slot : slot + 1] + 1e-06)
        master_ref[slot] = master
        new_ema_ref[slot] = 0.5 * ema_ref[slot] + 0.5 * master


def block_specs(count, slots):
    return pl.BlockSpec((slots, BLOCK, BLOCK), lambda i: (i, 0, 0))


def exchange(value, axis, pairs):
    return lax.ppermute(value, axis, pairs)


def shards(
    tokens,
    seq_lengths,
    qkv_weight,
    out_weight,
    up_gate_weight,
    down_weight,
    qk_scale,
    mlp_scale,
    eigen_rates,
    cotangent,
    block_order,
    master_blocks,
    ema_blocks,
    left_stats,
    right_stats,
    left_root,
    right_root,
):
    x_rows = tokens[0]
    total, width = x_rows.shape
    cols = qk_scale.shape[0]
    heads = lax.axis_size("head")
    owners = lax.axis_size("batch")
    ranks = heads // 2
    here = lax.axis_index("head")
    rank, core = here // 2, here % 2
    share = total // heads
    rows = share // CHUNKS
    tiles_all = total // rows

    core_swap = [(i, i ^ 1) for i in range(heads)]
    shift_up = [
        [(i, (i // 2 + s) % ranks * 2 + i % 2) for i in range(heads)] for s in range(ranks)
    ]
    shift_down = [
        [(i, (i // 2 - s) % ranks * 2 + i % 2) for i in range(heads)] for s in range(ranks)
    ]
    far_steps = list(range(1, ranks))
    ring = far_steps + [0]

    shares = jnp.stack(
        [(rank - s) % ranks * 2 + (core + d) % 2 for d in (1, 0) for s in ring]
    ).astype(jnp.int32)
    ends = jnp.cumsum(seq_lengths[0])

    def begin_of(row):
        segment = jnp.sum((row[:, None] >= ends[None, :]).astype(jnp.int32), axis=1)
        member = segment[:, None] == jnp.arange(ends.shape[0], dtype=jnp.int32)[None, :]
        return jnp.sum(jnp.where(member, (ends - seq_lengths[0])[None, :], 0), axis=1)

    tile_rows = jnp.arange(tiles_all, dtype=jnp.int32) * rows
    tile_begin = begin_of(tile_rows)
    lane = jnp.arange(LANES, dtype=jnp.int32) % (HEAD_DIM // 2)
    freq = 10000.0 ** (-lane.astype(F32) * 2.0 / HEAD_DIM)
    near_angle = jnp.arange(rows, dtype=F32)[:, None] * freq[None, :]
    far_angle = (tile_rows - tile_begin).astype(F32)[:, None] * freq[None, :]
    near = jnp.stack([jnp.cos(near_angle), jnp.sin(near_angle)])
    far = jnp.stack([jnp.cos(far_angle), jnp.sin(far_angle)])
    gains = qk_scale[None, :]
    rates = eigen_rates.T

    q, k, v, q_rot, k_rot = project(x_rows, qkv_weight, gains, near, far)
    weights = [
        (up_gate_weight, down_weight),
        (exchange(up_gate_weight, "head", core_swap), exchange(down_weight, "head", core_swap)),
    ]
    scales = jnp.concatenate([mlp_scale, exchange(mlp_scale, "head", core_swap)], axis=1)

    def from_partner(send, keep, size):
        got = exchange(send, "head", core_swap)
        if ranks == 1:
            return keep[:size], [keep, got]
        away = (keep[:-size].astype(F32) + got[:-size].astype(F32)).astype(BF16)
        return away, [keep, got] + from_ranks(away, size)

    def from_ranks(away, size):
        return [
            exchange(away[n * size : (n + 1) * size], "head", shift_down[s])
            for n, s in enumerate(far_steps)
        ]

    def gather_ranks(own):
        return [exchange(own, "head", shift_up[s]) for s in far_steps] + [own]

    def gather_shares(own):
        mine = gather_ranks(own)
        return [exchange(b, "head", core_swap) for b in mine] + mine

    places = [(here * CHUNKS + j).astype(jnp.int32)[None] for j in range(CHUNKS)]
    tiles = [shares * CHUNKS + j for j in range(CHUNKS)]
    starts = [begin_of(t * rows) for t in tiles]
    chunks = range(CHUNKS)
    tile = 2 * BLOCK

    attn_out, lse, parts = [], [], []
    last = ()
    for j in chunks:
        half = heads // 2
        first = attend(
            q, k, v, out_weight, tiles[j][:half], starts[j][:half], rows, 0, heads, last
        )
        second = attend(
            q,
            k,
            v,
            out_weight,
            tiles[j][half:],
            starts[j][half:],
            rows,
            half,
            heads,
            (first[0], first[1]),
            2,
        )
        away, got = from_partner(first[2], second[2], rows)
        attn_out.append(second[0])
        lse.append(second[1])
        parts.append(got)
        last = (away,)
    joined = []
    for j in chunks:
        joined.append(join_attention(parts[j], x_rows, places[j], rates, rows, last))
        last = (joined[j][0],)
    hidden = [gather_ranks(joined[j][0]) for j in chunks]
    ffn = []
    for j in chunks:
        ffn.append(mlp(hidden[j], weights, scales, tile, last))
        last = (ffn[j][4],)
    ends_fwd = []
    for j in chunks:
        parts = [ffn[j][4]] + from_ranks(ffn[j][3], rows)
        ends_fwd.append(
            join_mlp(parts, joined[j][1], cotangent[0], j, rates, rows, last)
        )
        last = (ends_fwd[j][1],)
    d_rows = [gather_ranks(ends_fwd[j][1]) for j in chunks]
    back = []
    for j in chunks:
        back.append(mlp_back(d_rows[j], ffn[j][0], ffn[j][1], weights, scales, tile, last))
        last = (back[j][4],)

    row_blocks = width // BLOCK
    piece = BLOCK // owners
    across = ranks
    levels = owners // across
    z_here, x_here = lax.axis_index("batch") // across, lax.axis_index("batch") % across
    direct = levels if piece % 16 == 0 and across == 2 else 0
    x_place = x_here.astype(jnp.int32)[None]
    left_hidden = [b for h in hidden for b in h]
    left_down = [b for d in d_rows for b in d]
    rights = {
        "down": (left_down, [f[2] for f in ffn]),
        "up": (left_hidden, [b[0] for b in back]),
        "gate": (left_hidden, [b[1] for b in back]),
    }

    def partner_part(name, after):
        out = outer(*rights[name], 1, 2, tile, after=after)[0]
        return out, exchange(out, "head", core_swap)

    def own_part(name, more, after):
        return outer(
            *rights[name],
            0,
            2,
            tile,
            more=(more,),
            place=x_place,
            levels=direct,
            after=after,
        )

    def as_pieces(matrix):
        panels = matrix.shape[1] // BLOCK
        return (
            matrix.reshape(row_blocks, levels, across, piece, panels, BLOCK)
            .transpose(1, 2, 4, 0, 3, 5)
            .reshape(levels, across, panels * row_blocks * piece, BLOCK)
        )

    def from_this_x(pieces):
        return [
            lax.dynamic_index_in_dim(pieces, (x_here + s) % across, 1, keepdims=False)
            for s in range(across)
        ]

    def hold(value, anchor):
        return value if anchor is None else lax.optimization_barrier((value, anchor))[0]

    x_step = lambda s: [
        (i, i // across * across + (i % across + s) % across) for i in range(owners)
    ]
    z_step = lambda s: [
        (i, (i // across + s) % levels * across + i % across) for i in range(owners)
    ]
    z_place = z_here.astype(jnp.int32)[None]

    def over_z(parts):
        return [parts[0]] + [
            exchange(parts[s], "batch", z_step(s)) for s in range(1, levels)
        ]

    def plain_x(pieces):
        total = pieces[0].astype(F32)
        for s in range(1, across):
            total = total + exchange(pieces[s], "batch", x_step(s)).astype(F32)
        total = total.astype(BF16)
        return [
            lax.dynamic_index_in_dim(total, (z_here + s) % levels, 0, keepdims=False)
            for s in range(levels)
        ]

    def start_x(outs):
        if direct:
            mine, other = [flat(o) for o in outs]
            return mine, exchange(other, "batch", x_step(1))
        return from_this_x(as_pieces(outs[0]))

    def finish_x(started, after):
        if direct:
            sums = join_x(*started, z_place, after)
        else:
            sums = plain_x(started)
        return over_z(sums)

    split = []
    partner = {}
    for j in chunks:
        parts = [back[j][4]] + from_ranks(back[j][3], rows)
        split.append(
            split_attention(
                parts,
                ends_fwd[j][2],
                joined[j][1],
                joined[j][2],
                x_rows,
                places[j],
                rates,
                rows,
                last,
            )
        )
        last = (split[j][0],)
        if j == 0:
            out, partner["down"] = partner_part("down", last)
            last = (out,)
    for name in ("up", "gate"):
        out, partner[name] = partner_part(name, last)
        last = (out,)
    flat = lambda a: a.reshape(a.shape[:-3] + (-1, BLOCK))
    started = {}
    for name in ("down", "up", "gate"):
        outs = own_part(name, partner[name], last)
        last = (outs[0],)
        started[name] = start_x(outs)
    d_attn_rows = [gather_shares(split[j][0]) for j in chunks]
    outs = outer(
        [b for d in d_attn_rows for b in d],
        attn_out,
        0,
        1,
        tile,
        place=x_place,
        levels=direct,
        after=last,
    )
    last = (outs[0],)
    started["out"] = start_x(outs)
    order = (shares[:, None] * CHUNKS + jnp.arange(CHUNKS, dtype=jnp.int32)[None, :]).reshape(-1)
    waiting = ["down", "up", "gate", "out"]
    moved = {}

    def next_x(after):
        name = waiting.pop(0)
        moved[name] = finish_x(started[name], after)
        return (moved[name][0],)

    raws, gain_parts, late = [], [], []
    pairs_all = cols // LANES
    marks = []
    for pair in range(pairs_all):
        pair_back = []
        for j in chunks:
            pair_back.append(
                attend_back(
                    d_attn_rows[j],
                    q,
                    k,
                    v,
                    attn_out[j],
                    lse[j],
                    out_weight,
                    tiles[j],
                    starts[j],
                    rows,
                    pair,
                    last,
                )
            )
            last = (pair_back[-1][0],)
            marks.append(last[0])
            if waiting:
                last = next_x(last)
        raw, gain_part, *outs = project_back(
            x_rows,
            q_rot,
            k_rot,
            gains,
            near,
            far,
            pair_back,
            order,
            rows,
            pair,
            x_place,
            direct,
            last,
        )
        last = (raw,)
        raws.append(raw)
        gain_parts.append(gain_part)
        late.append(start_x(outs))
        if pair < pairs_all - 1:
            waiting.append(pair)
            started[pair] = late[pair]
    while len(waiting):
        last = next_x(last)
    send, keep = input_back(raws, qkv_weight, order, rows, last)
    gain_grad = jnp.concatenate(gain_parts, axis=1)
    moved[pairs_all - 1] = finish_x(late[-1], (keep,))

    def double(value, axis, size, anchors=()):
        step = 1
        turn = 0
        while step < size:
            got = exchange(value, axis, [(i, i ^ step) for i in range(size)])
            value = value + hold(got, anchors[turn] if turn < len(anchors) else None)
            step *= 2
            turn += 1
        return value

    rate_grad = double(
        jnp.concatenate([sum(s[2] for s in split), sum(e[3] for e in ends_fwd)], axis=0),
        "head",
        heads,
        marks,
    )
    both = sum(b[2] for b in back)
    scale_cols = mlp_scale.shape[1]
    scale_grad = both[:, :scale_cols] + exchange(both[:, scale_cols:], "head", core_swap)

    _, parts = from_partner(send, keep, share)
    d_input = jnp.concatenate([s[1] for s in split], axis=0)
    slot_order = block_order[0]
    panel, rest = slot_order // row_blocks, slot_order % row_blocks
    early_panel = panel % pairs_all * 3 + panel // pairs_all
    place_of = jnp.where(panel < 3 * pairs_all, early_panel, panel) * row_blocks + rest
    groups = [moved[n] for n in list(range(pairs_all)) + ["out", "up", "gate", "down"]]
    if direct:
        ordered = order_pieces(groups, place_of, piece, ())
    else:
        sums = [sum(a.astype(F32) for a in g).astype(BF16) for g in groups]
        pieces = jnp.concatenate(sums, axis=0).reshape(-1, piece, BLOCK)
        ordered = jnp.take(pieces, place_of, axis=0, mode="clip")
    per_owner = slot_order.shape[0] // owners
    owned = lax.all_to_all(
        ordered.reshape(owners, per_owner, piece, BLOCK),
        "batch",
        split_axis=0,
        concat_axis=0,
        tiled=True,
    )
    slots = min(8, per_owner)
    if piece % 16:
        owned = owned.transpose(1, 0, 2, 3).reshape(1, per_owner, BLOCK, BLOCK)
    g_spec = pl.BlockSpec(
        (owned.shape[0], slots) + owned.shape[2:], lambda i: (0, i, 0, 0)
    )
    blk = pl.BlockSpec((slots, BLOCK, BLOCK), lambda i: (i, 0, 0))
    row = pl.BlockSpec((slots, BLOCK), lambda i: (i, 0))
    cube = jax.ShapeDtypeStruct((per_owner, BLOCK, BLOCK), F32)
    grid = (per_owner // slots,)
    owned_grad, stepped, column_sq = pl.pallas_call(
        step_kernel,
        grid=grid,
        in_specs=[g_spec, blk, blk, blk],
        out_specs=[blk, blk, row],
        out_shape=[cube, cube, jax.ShapeDtypeStruct((per_owner, BLOCK), F32)],
        name="step",
        cost_estimate=COST,
    )(owned, left_root[0], right_root[0], master_blocks[0])
    new_left, new_right = launch(
        stats_kernel,
        "stats",
        grid,
        [(owned, g_spec), (left_stats[0], blk), (right_stats[0], blk)],
        [(cube, blk), (cube, blk)],
        after=(column_sq,),
    )
    panels = block_order.shape[1] // row_blocks
    my_blocks = lax.dynamic_slice_in_dim(
        slot_order, lax.axis_index("batch") * per_owner, per_owner, 0
    )
    member = (
        (my_blocks // row_blocks)[:, None] == jnp.arange(panels, dtype=jnp.int32)[None, :]
    ).astype(F32)
    precise = lax.Precision.HIGHEST
    sums = jnp.concatenate(
        [jnp.einsum("sp,sb->pb", member, column_sq, precision=precise)]
        + [a.reshape(-1, LANES) for a in (gain_grad, rate_grad, scale_grad)],
        axis=0,
    )
    sums = double(sums, "batch", owners, (new_left,))
    totals = sums[:panels]
    small = sums[panels:].reshape(-1)
    gain_sum = small[:cols]
    rate_sum = small[cols : cols + 2 * width].reshape(2, width)
    scale_sum = small[cols + 2 * width :].reshape(mlp_scale.shape)
    d_input = d_input + sum(p[-share:].astype(F32) for p in parts)
    norms = jnp.einsum("sp,pb->sb", member, totals, precision=precise)
    new_master, new_ema = pl.pallas_call(
        finish_kernel,
        grid=grid,
        in_specs=[blk, blk, row],
        out_specs=[blk, blk],
        out_shape=[cube, cube],
        name="finish",
    )(stepped, ema_blocks[0], norms)
    gain_step = 0.5 / math.sqrt(total * owners)
    width_share = width // heads
    rate_here = lax.dynamic_slice_in_dim(rate_sum, here * width_share, width_share, 1)
    rate_slice = lax.dynamic_slice_in_dim(rates, here * width_share, width_share, 1)
    mlp_scale_out = jnp.stack([scale_sum, mlp_scale - gain_step * scale_sum])
    new_gains = jnp.concatenate(
        [(qk_scale - gain_step * gain_sum)[None, :], rate_slice - gain_step * rate_here], axis=0
    )
    out_share = jnp.concatenate([e[0] for e in ends_fwd], axis=0)
    return (
        out_share[None],
        d_input[None],
        owned_grad[None],
        new_master[None],
        new_ema[None],
        new_left[None],
        new_right[None],
        gain_sum,
        mlp_scale_out,
        rate_here.T,
        new_gains,
    )


def solution(mesh):
    return jax.shard_map(
        shards,
        mesh=mesh,
        in_specs=(
            P("batch", None, None),
            P("batch", None),
            P(None, None, "head"),
            P("head", None),
            P(None, None, "head"),
            P("head", None),
            P("head"),
            P(None, "head"),
            P(),
            P("batch", "head", None),
            P("head", None),
            P("head", "batch", None, None),
            P("head", "batch", None, None),
            P("head", "batch", None, None),
            P("head", "batch", None, None),
            P("head", "batch", None, None),
            P("head", "batch", None, None),
        ),
        out_specs=(
            P("batch", "head", None),
            P("batch", "head", None),
            P("head", "batch", None, None),
            P("head", "batch", None, None),
            P("head", "batch", None, None),
            P("head", "batch", None, None),
            P("head", "batch", None, None),
            P("head"),
            P(None, None, "head"),
            P("head", None),
            P(None, "head"),
        ),
        check_vma=False,
    )
```

```python
import functools
import math

import jax
import jax.numpy as jnp
from jax import lax
from jax.experimental import pallas as pl
from jax.experimental.pallas import tpu as pltpu
from jax.sharding import PartitionSpec as P

HEAD_DIM = 64
BLOCK = 128
LANES = 128
CHUNKS = 2
F32 = jnp.float32
BF16 = jnp.bfloat16
NN = (((1,), (0,)), ((), ()))
NT = (((1,), (1,)), ((), ()))
TN = (((0,), (0,)), ((), ()))
COST = pl.CostEstimate(flops=10**10, transcendentals=0, bytes_accessed=10**7)


def mm(a, b, dims=NN):
    return lax.dot_general(a, b, dims, preferred_element_type=F32)


def whole(shape, single=False):
    zeros = (0,) * len(shape)
    if single:
        return pl.BlockSpec(shape, lambda *_: zeros, pipeline_mode=pl.Buffered(1))
    return pl.BlockSpec(shape, lambda *_: zeros)


def launch(kernel, name, grid, ins, outs, scratch=(), prefetch=(), after=(), alias=0):
    first, count, extra = len(prefetch), len(ins), len(after)

    def body(*refs):
        kernel(*refs[: first + count], *refs[first + count + extra :])

    return pl.pallas_call(
        body,
        grid_spec=pltpu.PrefetchScalarGridSpec(
            num_scalar_prefetch=first,
            grid=grid,
            in_specs=[s for _, s in ins] + [pl.BlockSpec(memory_space=pl.ANY)] * extra,
            out_specs=[s for _, s in outs],
            scratch_shapes=list(scratch),
        ),
        out_shape=[o for o, _ in outs],
        input_output_aliases={first + count + n: n for n in range(alias)},
        name=name,
        cost_estimate=COST,
    )(*prefetch, *[a for a, _ in ins], *after)


def like(shape, dtype):
    return jax.ShapeDtypeStruct(shape, dtype)


def rms_rows(value):
    return value * lax.rsqrt(jnp.mean(value * value, axis=-1, keepdims=True) + 1e-06)


def rms_factor(value):
    return lax.rsqrt(jnp.mean(value * value, axis=-1, keepdims=True) + 1e-06)


def rms_back(normed, factor, gradient):
    return factor * (gradient - normed * jnp.mean(gradient * normed, axis=-1, keepdims=True))


def lane_ids():
    return lax.broadcasted_iota(jnp.int32, (1, LANES), 1)


def head_mean(value, ones_block):
    high = value.astype(BF16)
    rest = (value - high.astype(F32)).astype(BF16)
    return (mm(high, ones_block) + mm(rest, ones_block)) * (1.0 / HEAD_DIM)


def ones_block():
    row = lax.broadcasted_iota(jnp.int32, (LANES, LANES), 0) // HEAD_DIM
    col = lax.broadcasted_iota(jnp.int32, (LANES, LANES), 1) // HEAD_DIM
    return jnp.where(row == col, 1.0, 0.0).astype(BF16)


def half_turn(value):
    first = (lane_ids() & (HEAD_DIM - 1)) < HEAD_DIM // 2
    return jnp.where(
        first,
        pltpu.roll(value, LANES - HEAD_DIM // 2, 1),
        pltpu.roll(value, HEAD_DIM // 2, 1),
    )


def angles(tile, near_ref, far_ref):
    cos_r, sin_r = near_ref[0], near_ref[1]
    cos_0 = far_ref[0, pl.ds(tile, 1), :]
    sin_0 = far_ref[1, pl.ds(tile, 1), :]
    first = (lane_ids() & (HEAD_DIM - 1)) < HEAD_DIM // 2
    sine = sin_0 * cos_r + cos_0 * sin_r
    return cos_0 * cos_r - sin_0 * sin_r, jnp.where(first, -sine, sine)


def project_kernel(
    x_ref, w_ref, gain_ref, near_ref, far_ref, q_ref, k_ref, v_ref, q_rot_ref, k_rot_ref
):
    tile = pl.program_id(0)
    cosine, sine = angles(tile, near_ref, far_ref)
    ones = ones_block()
    x = x_ref[...]
    for index, used_ref, rot_ref in ((0, q_ref, q_rot_ref), (1, k_ref, k_rot_ref)):
        raw = mm(x, w_ref[index])
        for pair in range(raw.shape[1] // LANES):
            lanes = slice(pair * LANES, (pair + 1) * LANES)
            value = raw[:, lanes]
            turned = value * cosine + half_turn(value) * sine
            factor = lax.rsqrt(head_mean(turned * turned, ones) + 1e-06)
            rot_ref[:, lanes] = turned
            used_ref[:, lanes] = (turned * factor * gain_ref[:, lanes]).astype(BF16)
    v_ref[...] = mm(x, w_ref[2]).astype(BF16)


def project(x, weight, gains, near, far):
    rows, width = x.shape
    cols = weight.shape[2]
    tile = near.shape[1]
    by_row = lambda w: pl.BlockSpec((tile, w), lambda i: (i, 0))
    return pl.pallas_call(
        project_kernel,
        grid=(rows // tile,),
        in_specs=[
            by_row(width),
            whole(weight.shape, True),
            whole((1, cols)),
            whole(near.shape),
            whole(far.shape),
        ],
        out_specs=[by_row(cols)] * 5,
        out_shape=[jax.ShapeDtypeStruct((rows, cols), BF16)] * 3
        + [jax.ShapeDtypeStruct((rows, cols), F32)] * 2,
        name="project",
        cost_estimate=COST,
    )(x, weight, gains, near, far)


def key_tiles(first_row, start, wide, narrow, visit):
    full = first_row // wide

    def step(index, carry):
        visit(pl.multiple_of(index * wide, wide), wide, False)
        return carry

    lax.fori_loop(start // wide, full, step, 0)
    diagonal = (first_row // narrow) * narrow

    @pl.when(diagonal > full * wide)
    def _():
        visit(pl.multiple_of(full * wide, narrow), narrow, False)

    visit(pl.multiple_of(diagonal, narrow), narrow, True)


def attend_kernel(
    wide, tiles, starts, q_ref, k_ref, v_ref, w_ref, o_ref, lse_ref, part_ref, acc
):
    index = pl.program_id(0)
    rows = q_ref.shape[0]
    first_row = tiles[index] * rows
    start = starts[index]
    narrow = wide // 2
    low = lane_ids() < HEAD_DIM
    zero = jnp.zeros((), BF16)
    results = []
    for pair in range(q_ref.shape[1] // LANES):
        lanes = slice(pair * LANES, (pair + 1) * LANES)
        q = q_ref[:, lanes] * jnp.asarray(1.0 / math.sqrt(HEAD_DIM), BF16)
        q_both = jnp.concatenate([jnp.where(low, q, zero), jnp.where(low, zero, q)], axis=0)
        acc[...] = jnp.zeros_like(acc)

        def visit(key_0, size, masked):
            keys = pl.ds(key_0, size)
            weights = jnp.exp(mm(q_both, k_ref[keys, lanes], NT))
            if masked:
                row = lax.broadcasted_iota(jnp.int32, (2 * rows, size), 0)
                row = jnp.where(row < rows, row, row - rows) + first_row
                col = lax.broadcasted_iota(jnp.int32, (2 * rows, size), 1) + key_0
                weights = jnp.where((col <= row) & (col >= start), weights, 0.0)
            total = weights[:, :LANES]
            for part in range(1, size // LANES):
                total = total + weights[:, part * LANES : (part + 1) * LANES]
            acc[:, LANES:] += total
            acc[:, :LANES] += mm(weights.astype(BF16), v_ref[keys, lanes])

        key_tiles(first_row, start, wide, narrow, visit)
        total_a = jnp.sum(acc[:rows, LANES:], axis=1, keepdims=True)
        total_b = jnp.sum(acc[rows:, LANES:], axis=1, keepdims=True)
        summed = jnp.where(low, acc[:rows, :LANES], acc[rows:, :LANES])
        out = (summed / jnp.where(low, total_a, total_b)).astype(BF16)
        o_ref[:, lanes] = out
        lse_ref[:, lanes] = jnp.log(jnp.where(low, total_b, total_a))
        results.append(out)
    part_ref[...] = mm(jnp.concatenate(results, axis=1), w_ref[...]).astype(BF16)


def attend(q, k, v, weight, tiles, starts, rows, offset, places, after, alias=0):
    count = tiles.shape[0]
    cols = k.shape[1]
    width = weight.shape[1]
    at_place = pl.BlockSpec((rows, cols), lambda i, t, s: (i + offset, 0))
    return launch(
        functools.partial(attend_kernel, 4 * BLOCK),
        "attend",
        (count,),
        [
            (q, pl.BlockSpec((rows, cols), lambda i, t, s: (t[i], 0))),
            (k, whole(k.shape, True)),
            (v, whole(v.shape, True)),
            (weight, whole(weight.shape, True)),
        ],
        [
            (like((places * rows, cols), BF16), at_place),
            (like((places * rows, cols), F32), at_place),
            (like((count * rows, width), BF16), pl.BlockSpec((rows, width), lambda i, t, s: (i, 0))),
        ],
        scratch=[pltpu.VMEM((2 * rows, 2 * LANES), F32)],
        prefetch=(tiles, starts),
        after=after,
        alias=alias,
    )


def attend_back_kernel(blocks, wide, tiles, starts, *refs):
    row_refs = refs[:blocks]
    q_ref, k_ref, v_ref, o_ref, lse_ref, w_ref = refs[blocks : blocks + 6]
    dq_ref, dk_ref, dv_ref, rows_s, acc = refs[blocks + 6 :]
    index = pl.program_id(0)
    rows = q_ref.shape[0]
    narrow = wide // 2

    @pl.when(index == 0)
    def _():
        dk_ref[...] = jnp.zeros_like(dk_ref)
        dv_ref[...] = jnp.zeros_like(dv_ref)

    for block in range(blocks):

        @pl.when(index == block)
        def _(block=block):
            rows_s[...] = row_refs[block][...]

    first_row = tiles[index] * rows
    start = starts[index]
    low = lane_ids() < HEAD_DIM
    place = lane_ids() & (HEAD_DIM - 1)
    zero = jnp.zeros((), BF16)
    ones = jnp.where(place < 3, 1.0, 0.0).astype(BF16)

    def parts(value):
        high = value.astype(BF16).astype(F32)
        rest = value - high
        middle = rest.astype(BF16).astype(F32)
        picked = jnp.where(place == 1, middle, jnp.where(place == 2, rest - middle, 0.0))
        return jnp.where(place == 0, high, picked).astype(BF16)

    d_rows = rows_s[...]
    d_attn = mm(d_rows, w_ref[...], NT).astype(BF16)
    for pair in range(q_ref.shape[1] // LANES):
        lanes = slice(pair * LANES, (pair + 1) * LANES)
        q = q_ref[:, lanes] * jnp.asarray(1.0 / math.sqrt(HEAD_DIM), BF16)
        d_out = d_attn[:, lanes]
        minus_lse = parts(-lse_ref[:, lanes])
        product = d_out.astype(F32) * o_ref[:, lanes].astype(F32)
        sum_a = jnp.sum(jnp.where(low, product, 0.0), axis=1, keepdims=True)
        sum_b = jnp.sum(jnp.where(low, 0.0, product), axis=1, keepdims=True)
        minus_delta = parts(-jnp.where(low, sum_b, sum_a))
        q_ext = (jnp.where(low, q, minus_lse), jnp.where(low, minus_lse, q))
        d_ext = (jnp.where(low, d_out, minus_delta), jnp.where(low, minus_delta, d_out))
        q_both = jnp.concatenate([jnp.where(low, q, zero), jnp.where(low, zero, q)], axis=0)
        d_both = jnp.concatenate(
            [jnp.where(low, d_out, zero), jnp.where(low, zero, d_out)], axis=0
        )
        acc[...] = jnp.zeros_like(acc)

        def visit(key_0, size, masked):
            keys = pl.ds(key_0, size)
            k = k_ref[keys, lanes]
            v = v_ref[keys, lanes]
            k_ext = (jnp.where(low, k, ones), jnp.where(low, ones, k))
            v_ext = (jnp.where(low, v, ones), jnp.where(low, ones, v))
            if masked:
                col = lax.broadcasted_iota(jnp.int32, (size, rows), 1) + first_row
                row = lax.broadcasted_iota(jnp.int32, (size, rows), 0) + key_0
                allowed = (row <= col) & (row >= start)
            probs = []
            d_scores = []
            for head in range(2):
                prob = jnp.exp(mm(k_ext[head], q_ext[head], NT))
                if masked:
                    prob = jnp.where(allowed, prob, 0.0)
                d_score = prob * mm(v_ext[head], d_ext[head], NT)
                probs.append(prob.astype(BF16))
                d_scores.append(d_score.astype(BF16))
            dv_ref[keys, lanes] += mm(jnp.concatenate(probs, axis=1), d_both)
            dk_ref[keys, lanes] += mm(jnp.concatenate(d_scores, axis=1), q_both)
            k_both = jnp.concatenate([jnp.where(low, k, zero), jnp.where(low, zero, k)], axis=0)
            acc[...] += mm(jnp.concatenate(d_scores, axis=0), k_both, TN)

        key_tiles(first_row, start, wide, narrow, visit)
        dq_ref[:, lanes] = acc[...] * (1.0 / math.sqrt(HEAD_DIM))


def attend_back(row_blocks, q, k, v, o, lse, weight, tiles, starts, rows, pair, after):
    count = tiles.shape[0]
    total = k.shape[0]
    width = weight.shape[1]
    at_tile = pl.BlockSpec((rows, LANES), lambda i, t, s: (t[i], pair))
    at_step = pl.BlockSpec((rows, LANES), lambda i, t, s: (i, pair))
    column = pl.BlockSpec((total, LANES), lambda *_: (0, pair), pipeline_mode=pl.Buffered(1))
    return launch(
        functools.partial(attend_back_kernel, len(row_blocks), 4 * BLOCK),
        "attend_back",
        (count,),
        [(b, whole(b.shape, True)) for b in row_blocks]
        + [
            (q, at_tile),
            (k, column),
            (v, column),
            (o, at_step),
            (lse, at_step),
            (weight, pl.BlockSpec((LANES, width), lambda *_: (pair, 0))),
        ],
        [
            (like((count * rows, LANES), F32), pl.BlockSpec((rows, LANES), lambda i, *_: (i, 0))),
            (like((total, LANES), F32), whole((total, LANES))),
            (like((total, LANES), F32), whole((total, LANES))),
        ],
        scratch=[pltpu.VMEM((rows, width), BF16), pltpu.VMEM((rows, LANES), F32)],
        prefetch=(tiles, starts),
        after=after,
    )


def sum_parts(refs):
    total = refs[0][...].astype(F32)
    for ref in refs[1:]:
        total = total + ref[...].astype(F32)
    return total


def join_attention_kernel(parts, place, *refs):
    x_ref, rate_ref = refs[parts : parts + 2]
    low_ref, hidden_ref, branch_ref = refs[parts + 2 :]
    branch = sum_parts(refs[:parts])
    x = x_ref[...].astype(F32)
    hidden = rms_rows(x + rate_ref[0:1] * (rms_rows(branch) - x))
    branch_ref[...] = branch
    hidden_ref[...] = hidden
    low_ref[...] = hidden.astype(BF16)


def part_specs(parts, rows, width):
    return [
        pl.BlockSpec((rows, width), lambda i, *_, last=a.shape[0] // rows: (last - SUB + i, 0))
        for a in parts
    ]


SUB = 2


def join_attention(parts, x, place, rates, share, after):
    width = x.shape[1]
    rows = share // SUB
    here = pl.BlockSpec((rows, width), lambda i, p: (i, 0))
    return launch(
        functools.partial(join_attention_kernel, len(parts)),
        "join_attention",
        (SUB,),
        list(zip(parts, part_specs(parts, rows, width), strict=True))
        + [
            (x, pl.BlockSpec((rows, width), lambda i, p: (p[0] * SUB + i, 0))),
            (rates, whole(rates.shape)),
        ],
        [(like((share, width), d), here) for d in (BF16, F32, F32)],
        prefetch=(place,),
        after=after,
    )


def weight_tiles(weight, down, step, side):
    _, width, cols = weight.shape
    count = cols // step
    if side == 0:
        at = lambda t: jnp.minimum(t, count - 1)
    else:
        at = lambda t: jnp.maximum(t - count, 0)
    return [
        (weight, pl.BlockSpec((2, width, step), lambda t, *_: (0, 0, at(t)))),
        (down, pl.BlockSpec((step, width), lambda t, *_: (at(t), 0))),
    ]


def mlp_kernel(blocks, *refs):
    row_refs = refs[:blocks]
    sides = (refs[blocks : blocks + 2], refs[blocks + 2 : blocks + 4])
    scale_ref = refs[blocks + 4]
    up_ref, gate_ref, mixed_ref, away_ref, own_ref, x_s, acc = refs[blocks + 5 :]
    tile = pl.program_id(0)
    count = pl.num_programs(0)
    rows = row_refs[0].shape[0]

    @pl.when(tile == 0)
    def _():
        for block in range(blocks):
            x_s[block * rows : (block + 1) * rows] = row_refs[block][...]
        acc[...] = jnp.zeros_like(acc)

    def run(w_ref, down_ref):
        x = x_s[...]
        up = mm(x, w_ref[0])
        gate = mm(x, w_ref[1])
        up_ref[...] = up.astype(BF16)
        gate_ref[...] = gate.astype(BF16)
        scaled = gate * scale_ref[1:2]
        mixed = (up * scale_ref[0:1] * (scaled * jax.nn.sigmoid(scaled))).astype(BF16)
        mixed_ref[...] = mixed
        acc[...] += mm(mixed, down_ref[...])

    for side in range(2):

        @pl.when(tile // (count // 2) == side)
        def _(side=side):
            run(*sides[side])

    @pl.when(tile == count - 1)
    def _():
        last = (blocks - 1) * rows
        own_ref[...] = acc[last:]
        if blocks > 1:
            away_ref[...] = acc[:last].astype(BF16)


def mlp(row_blocks, weights, scales, step, after):
    rows, width = row_blocks[0].shape
    blocks = len(row_blocks)
    height = rows * blocks
    cols = 2 * weights[0][0].shape[2]
    at_tile = lambda h: pl.BlockSpec((h, step), lambda t: (0, t))
    far = max(blocks - 1, 1) * rows
    return launch(
        functools.partial(mlp_kernel, blocks),
        "mlp",
        (cols // step,),
        [(b, whole(b.shape, True)) for b in row_blocks]
        + weight_tiles(*weights[0], step, 0)
        + weight_tiles(*weights[1], step, 1)
        + [(scales, at_tile(2))],
        [(like((height, cols), BF16), at_tile(height))] * 3
        + [
            (like((far, width), BF16), whole((far, width))),
            (like((rows, width), F32), whole((rows, width))),
        ],
        scratch=[pltpu.VMEM((height, width), BF16), pltpu.VMEM((height, width), F32)],
        after=after,
    )


def join_mlp_kernel(parts, *refs):
    hidden_ref, cot_ref, rate_ref = refs[parts : parts + 3]
    out_ref, low_ref, d_hidden_ref, rate_grad_ref = refs[parts + 3 :]
    branch = sum_parts(refs[:parts])
    hidden = hidden_ref[...]
    rate = rate_ref[1:2]
    factor = rms_factor(branch)
    normed = branch * factor
    gap = normed - hidden
    before = hidden + rate * gap
    factor_out = rms_factor(before)
    out = before * factor_out
    d_before = rms_back(out, factor_out, cot_ref[...].astype(F32))
    out_ref[...] = out
    d_hidden_ref[...] = (1.0 - rate) * d_before
    low_ref[...] = rms_back(normed, factor, rate * d_before).astype(BF16)

    @pl.when(pl.program_id(0) == 0)
    def _():
        rate_grad_ref[...] = jnp.zeros_like(rate_grad_ref)

    rate_grad_ref[...] += jnp.sum(d_before * gap, axis=0, keepdims=True)


def join_mlp(parts, hidden, cotangent, chunk, rates, share, after):
    width = hidden.shape[1]
    rows = share // SUB
    here = pl.BlockSpec((rows, width), lambda i: (i, 0))
    return launch(
        functools.partial(join_mlp_kernel, len(parts)),
        "join_mlp",
        (SUB,),
        list(zip(parts, part_specs(parts, rows, width), strict=True))
        + [
            (hidden, here),
            (cotangent, pl.BlockSpec((rows, width), lambda i: (chunk * SUB + i, 0))),
            (rates, whole(rates.shape)),
        ],
        [(like((share, width), d), here) for d in (F32, BF16, F32)]
        + [(like((1, width), F32), whole((1, width)))],
        after=after,
    )


def mlp_back_kernel(blocks, *refs):
    row_refs = refs[:blocks]
    sides = (refs[blocks : blocks + 2], refs[blocks + 2 : blocks + 4])
    scale_ref, up_ref, gate_ref = refs[blocks + 4 : blocks + 7]
    d_up_ref, d_gate_ref, sums_ref, away_ref, own_ref, x_s, acc = refs[blocks + 7 :]
    tile = pl.program_id(0)
    count = pl.num_programs(0)
    rows = row_refs[0].shape[0]

    @pl.when(tile == 0)
    def _():
        for block in range(blocks):
            x_s[block * rows : (block + 1) * rows] = row_refs[block][...]
        acc[...] = jnp.zeros_like(acc)

    def run(w_ref, down_ref):
        d_mixed = mm(x_s[...], down_ref[...], NT)
        up_raw = up_ref[...].astype(F32)
        gate_raw = gate_ref[...].astype(F32)
        scale_up = scale_ref[0:1]
        scale_gate = scale_ref[1:2]
        gate = gate_raw * scale_gate
        sig = jax.nn.sigmoid(gate)
        d_up = d_mixed * (gate * sig)
        d_gate = d_mixed * (up_raw * scale_up) * (sig * (1.0 + gate * (1.0 - sig)))
        sums_ref[0:1] = jnp.sum(d_up * up_raw, axis=0, keepdims=True)
        sums_ref[1:2] = jnp.sum(d_gate * gate_raw, axis=0, keepdims=True)
        d_up = (d_up * scale_up).astype(BF16)
        d_gate = (d_gate * scale_gate).astype(BF16)
        d_up_ref[...] = d_up
        d_gate_ref[...] = d_gate
        acc[...] += mm(d_up, w_ref[0], NT) + mm(d_gate, w_ref[1], NT)

    for side in range(2):

        @pl.when(tile // (count // 2) == side)
        def _(side=side):
            run(*sides[side])

    @pl.when(tile == count - 1)
    def _():
        last = (blocks - 1) * rows
        own_ref[...] = acc[last:]
        if blocks > 1:
            away_ref[...] = acc[:last].astype(BF16)


def mlp_back(row_blocks, up, gate, weights, scales, step, after):
    rows, width = row_blocks[0].shape
    blocks = len(row_blocks)
    height = rows * blocks
    cols = 2 * weights[0][0].shape[2]
    at_tile = lambda h: pl.BlockSpec((h, step), lambda t: (0, t))
    far = max(blocks - 1, 1) * rows
    return launch(
        functools.partial(mlp_back_kernel, blocks),
        "mlp_back",
        (cols // step,),
        [(b, whole(b.shape, True)) for b in row_blocks]
        + weight_tiles(*weights[0], step, 0)
        + weight_tiles(*weights[1], step, 1)
        + [(scales, at_tile(2)), (up, at_tile(height)), (gate, at_tile(height))],
        [(like((height, cols), BF16), at_tile(height))] * 2
        + [
            (like((2, cols), F32), at_tile(2)),
            (like((far, width), BF16), whole((far, width))),
            (like((rows, width), F32), whole((rows, width))),
        ],
        scratch=[pltpu.VMEM((height, width), BF16), pltpu.VMEM((height, width), F32)],
        after=after,
    )


def split_attention_kernel(parts, place, *refs):
    d_hidden_ref, hidden_ref, branch_ref, x_ref, rate_ref = refs[parts : parts + 5]
    low_ref, d_input_ref, rate_grad_ref = refs[parts + 5 :]
    d_hidden = sum_parts(refs[:parts]) + d_hidden_ref[...]
    hidden = hidden_ref[...]
    branch = branch_ref[...]
    x = x_ref[...].astype(F32)
    rate = rate_ref[0:1]
    factor = rms_factor(branch)
    normed = branch * factor
    gap = normed - x
    d_before = rms_back(hidden, rms_factor(x + rate * gap), d_hidden)
    d_input_ref[...] = (1.0 - rate) * d_before
    low_ref[...] = rms_back(normed, factor, rate * d_before).astype(BF16)

    @pl.when(pl.program_id(0) == 0)
    def _():
        rate_grad_ref[...] = jnp.zeros_like(rate_grad_ref)

    rate_grad_ref[...] += jnp.sum(d_before * gap, axis=0, keepdims=True)


def split_attention(parts, d_hidden, hidden, branch, x, place, rates, share, after):
    width = x.shape[1]
    rows = share // SUB
    here = pl.BlockSpec((rows, width), lambda i, p: (i, 0))
    return launch(
        functools.partial(split_attention_kernel, len(parts)),
        "split_attention",
        (SUB,),
        list(zip(parts, part_specs(parts, rows, width), strict=True))
        + [(d_hidden, here), (hidden, here), (branch, here)]
        + [
            (x, pl.BlockSpec((rows, width), lambda i, p: (p[0] * SUB + i, 0))),
            (rates, whole(rates.shape)),
        ],
        [(like((share, width), d), here) for d in (BF16, F32)]
        + [(like((1, width), F32), whole((1, width)))],
        prefetch=(place,),
        after=after,
    )


def project_back_kernel(order, x_here, *refs):
    x_ref, q_rot_ref, k_rot_ref, gain_ref, near_ref, far_ref = refs[:6]
    d_refs = refs[6 : 6 + 3 * CHUNKS]
    part = lambda which: d_refs[which * CHUNKS : (which + 1) * CHUNKS]
    raw_ref, gain_grad_ref = refs[6 + 3 * CHUNKS : 8 + 3 * CHUNKS]
    grad_refs = refs[8 + 3 * CHUNKS : -2]
    acc, held = refs[-2:]
    index = pl.program_id(0)
    count = pl.num_programs(0)

    @pl.when(index == 0)
    def _():
        gain_grad_ref[...] = jnp.zeros_like(gain_grad_ref)
        acc[...] = jnp.zeros_like(acc)

    cosine, sine = angles(order[index], near_ref, far_ref)
    ones = ones_block()
    chunk = index % CHUNKS
    d_raw = []
    for which, rot_ref in ((0, q_rot_ref), (1, k_rot_ref)):
        if which == 0:
            d_used = part(0)[0][...]
            for other in range(1, CHUNKS):
                d_used = jnp.where(chunk == other, part(0)[other][...], d_used)
        else:
            d_used = sum_parts(part(1))
        turned = rot_ref[...]
        factor = lax.rsqrt(head_mean(turned * turned, ones) + 1e-06)
        normed = turned * factor
        gain_grad_ref[...] += jnp.sum(d_used * normed, axis=0, keepdims=True)
        d_normed = d_used * gain_ref[...]
        d_turned = factor * (d_normed - normed * head_mean(d_normed * normed, ones))
        d_raw.append((d_turned * cosine - half_turn(d_turned) * sine).astype(BF16))
    d_raw.append(sum_parts(part(2)).astype(BF16))
    d_all = jnp.concatenate(d_raw, axis=1)
    raw_ref[...] = d_all
    acc[...] += mm(d_all, x_ref[...], TN)

    @pl.when(index == count - 1)
    def _():
        held[...] = acc[...].T.astype(BF16)
        if len(grad_refs) == 1:
            grad_refs[0][...] = held[...]
        else:
            store_pieces(held, x_here[0], *grad_refs)


def project_back(x, q_rot, k_rot, gains, near, far, parts, order, rows, pair, place, levels, after):
    total, width = x.shape
    count = order.shape[0]
    wide = 3 * LANES
    at_tile = lambda w, n: pl.BlockSpec((rows, w), lambda i, t, *_: (t[i], n))
    if levels:
        shape = (levels, 3 * (width // BLOCK), BLOCK // (2 * levels), BLOCK)
        grads = [(like(shape, BF16), whole(shape))] * 2
    else:
        grads = [(like((width, wide), BF16), whole((width, wide)))]
    return launch(
        project_back_kernel,
        "project_back",
        (count,),
        [
            (x, at_tile(width, 0)),
            (q_rot, at_tile(LANES, pair)),
            (k_rot, at_tile(LANES, pair)),
            (gains, pl.BlockSpec((1, LANES), lambda *_: (0, pair))),
            (near, whole(near.shape)),
            (far, whole(far.shape)),
        ]
        + [
            (chunk[0], pl.BlockSpec((rows, LANES), lambda i, *_: (i // CHUNKS, 0)))
            for chunk in parts
        ]
        + [(chunk[which], at_tile(LANES, 0)) for which in (1, 2) for chunk in parts],
        [
            (like((total, wide), BF16), at_tile(wide, 0)),
            (like((1, LANES), F32), whole((1, LANES))),
        ]
        + grads,
        scratch=[pltpu.VMEM((wide, width), F32), pltpu.VMEM((width, wide), BF16)],
        prefetch=(order, place),
        after=after,
    )


def input_back_kernel(pairs, order, *refs):
    raw_refs = refs[:pairs]
    w_ref, send_ref, keep_ref = refs[pairs : pairs + 3]
    index = pl.program_id(0)
    count = pl.num_programs(0)
    d_x = None
    for which in range(3):
        lanes = slice(which * LANES, (which + 1) * LANES)
        d_all = jnp.concatenate([r[:, lanes] for r in raw_refs], axis=1)
        product = mm(d_all, w_ref[which], NT)
        d_x = product if d_x is None else d_x + product
    d_x = d_x.astype(BF16)

    @pl.when(index < count // 2)
    def _():
        send_ref[...] = d_x

    @pl.when(index >= count // 2)
    def _():
        keep_ref[...] = d_x


def input_back(raws, weight, order, rows, after):
    count = order.shape[0]
    half = count // 2
    width = weight.shape[1]
    out = like((half * rows, width), BF16)
    return launch(
        functools.partial(input_back_kernel, len(raws)),
        "input_back",
        (count,),
        [(r, pl.BlockSpec((rows, r.shape[1]), lambda i, t: (t[i], 0))) for r in raws]
        + [(weight, whole(weight.shape, True))],
        [
            (out, pl.BlockSpec((rows, width), lambda i, *_: (jnp.minimum(i, half - 1), 0))),
            (out, pl.BlockSpec((rows, width), lambda i, *_: (jnp.maximum(i - half, 0), 0))),
        ],
        prefetch=(order,),
        after=after,
    )


def join_x_kernel(units, place, *refs):
    out_refs = refs[2 * units :]
    levels = len(out_refs)
    for step in range(levels):
        level = (place[0] + step) % levels
        row = 0
        for unit in range(units):
            mine_ref, got_ref = refs[2 * unit : 2 * unit + 2]
            both = mine_ref[level].astype(F32) + got_ref[level].astype(F32)
            height = both.shape[0]
            out_refs[step][row : row + height] = both.astype(BF16)
            row += height


def join_x(units, z_place, after):
    levels, _, width = units[0][0].shape
    height = sum(u[0].shape[1] for u in units)
    arrays = [a for u in units for a in u]
    return launch(
        functools.partial(join_x_kernel, len(units)),
        "join_x",
        (1,),
        [(a, whole(a.shape)) for a in arrays],
        [(like((height, width), BF16), whole((height, width)))] * levels,
        prefetch=(z_place,),
        after=after,
    )


def join_partner_kernel(keep_ref, got_ref, out_ref):
    out_ref[...] = (keep_ref[...].astype(F32) + got_ref[...].astype(F32)).astype(BF16)


def join_partner(keep, got, size, after):
    width = keep.shape[1]
    away = keep.shape[0] - size
    block = pl.BlockSpec((size // 2, width), lambda i: (i, 0))
    return launch(
        join_partner_kernel,
        "join_partner",
        (away // (size // 2),),
        [(keep, block), (got, block)],
        [(like((away, width), BF16), block)],
        after=after,
    )[0]


def sum_input_kernel(parts, *refs):
    straight = refs[parts : parts + CHUNKS]
    out_ref = refs[-1]
    chunk = pl.program_id(0)
    value = straight[0][...]
    for other in range(1, CHUNKS):
        value = jnp.where(chunk == other, straight[other][...], value)
    out_ref[...] = value + sum_parts(refs[:parts])


def sum_input(parts, straight, rows, after):
    width = straight[0].shape[1]
    last = lambda a: a.shape[0] // rows - CHUNKS
    return launch(
        functools.partial(sum_input_kernel, len(parts)),
        "sum_input",
        (CHUNKS,),
        [
            (a, pl.BlockSpec((rows, width), lambda i, first=last(a): (first + i, 0)))
            for a in parts
        ]
        + [(a, whole(a.shape)) for a in straight],
        [
            (
                like((CHUNKS * rows, width), F32),
                pl.BlockSpec((rows, width), lambda i: (i, 0)),
            )
        ],
        after=after,
    )[0]


def order_kernel(counts, order, *refs):
    groups = []
    at = 0
    for n in counts:
        groups.append(refs[at : at + n])
        at += n
    out_ref, held = refs[at:]
    row = 0
    for group in groups:
        total = sum_parts(group)
        height = total.shape[0]
        held[row : row + height] = total.astype(BF16)
        row += height
    slots, piece, _ = out_ref.shape

    def move(slot, carry):
        start = pl.multiple_of(order[slot] * piece, piece)
        out_ref[slot] = held[pl.ds(start, piece)]
        return carry

    lax.fori_loop(0, slots, move, 0, unroll=8)


def order_pieces(groups, order, piece, after):
    arrays = [a for g in groups for a in g]
    slots = order.shape[0]
    shape = (slots, piece, BLOCK)
    return launch(
        functools.partial(order_kernel, [len(g) for g in groups]),
        "order_pieces",
        (1,),
        [(a, whole(a.shape)) for a in arrays],
        [(like(shape, BF16), whole(shape))],
        scratch=[pltpu.VMEM((slots * piece, BLOCK), BF16)],
        prefetch=(order,),
        after=after,
    )[0]


def outer_kernel(lefts, groups, rights, has_more, pieces, *refs):
    if pieces:
        place, refs = refs[0], refs[1:]
    left_refs = refs[:lefts]
    right_refs = refs[lefts : lefts + groups * rights]
    more_refs = refs[lefts + groups * rights : lefts + groups * rights + has_more]
    out_refs = refs[lefts + groups * rights + has_more : -2]
    turned, held = refs[-2:]
    rows = left_refs[0].shape[0]
    index = pl.program_id(0)

    @pl.when(index == 0)
    def _():
        for block in range(lefts):
            turned[:, block * rows : (block + 1) * rows] = left_refs[block][...].T

    def run(used):
        high = used[0].shape[0]
        total = mm(turned[:, :high], used[0][...])
        for n in range(1, rights):
            total = total + mm(turned[:, n * high : (n + 1) * high], used[n][...])
        for more in more_refs:
            total = total + more[...].astype(F32)
        if pieces:
            held[...] = total.astype(BF16)
        else:
            out_refs[0][...] = total.astype(BF16)

    if groups == 1:
        run(right_refs)
    else:
        for group in range(groups):

            @pl.when(index // (pl.num_programs(0) // groups) == group)
            def _(group=group):
                run(right_refs[group * rights : (group + 1) * rights])

    if pieces:
        store_pieces(held, place[0], *out_refs)


def store_pieces(held, x_here, *outs):
    levels, piece = outs[0].shape[0], outs[0].shape[-2]
    tall, wide = held.shape
    row_blocks = tall // BLOCK
    for side in range(2):
        shift = pl.multiple_of((x_here + side) % 2 * piece, piece)
        for panel in range(wide // BLOCK):
            lanes = slice(panel * BLOCK, (panel + 1) * BLOCK)
            for block in range(row_blocks):
                for level in range(levels):
                    start = block * BLOCK + 2 * level * piece
                    outs[side][level, panel * row_blocks + block] = held[
                        pl.ds(shift + start, piece), lanes
                    ]


def outer(left, groups, side, sides, step, more=(), place=None, levels=0, after=()):
    rows, width = left[0].shape
    cols = groups[0][0].shape[1] // sides
    step = min(step, cols)
    tiles = cols // step
    count = tiles * len(groups)

    def columns(array, group):
        if len(groups) == 1:
            at = lambda i, *_: (0, side * tiles + i)
        else:
            at = lambda i, *_: (0, side * tiles + jnp.clip(i - group * tiles, 0, tiles - 1))
        return array, pl.BlockSpec((array.shape[0], step), at)

    ins = (
        [(a, whole(a.shape, True)) for a in left]
        + [columns(a, n) for n, group in enumerate(groups) for a in group]
        + [(a, pl.BlockSpec((width, step), lambda i, *_: (0, i))) for a in more]
    )
    if not levels:
        outs = [
            (like((width, cols * len(groups)), BF16), pl.BlockSpec((width, step), lambda i: (0, i)))
        ]
    else:
        piece = BLOCK // (2 * levels)
        held = step // BLOCK * (width // BLOCK)
        outs = [
            (
                like((levels, held * count, piece, BLOCK), BF16),
                pl.BlockSpec((levels, held, piece, BLOCK), lambda i, p: (0, i, 0, 0)),
            )
        ] * 2
    return launch(
        functools.partial(
            outer_kernel, len(left), len(groups), len(groups[0]), len(more), levels > 0
        ),
        "outer",
        (count,),
        ins,
        outs,
        scratch=[pltpu.VMEM((width, rows * len(left)), BF16), pltpu.VMEM((width, step), BF16)],
        prefetch=(place,) if levels else (),
        after=after,
    )


def two_parts(value):
    high = value.astype(BF16)
    return high, (value - high.astype(F32)).astype(BF16)


def step_kernel(g_ref, left_ref, right_ref, master_ref, grad_ref, stepped_ref, square_ref):
    owners, slots, piece, width = g_ref.shape
    for slot in range(slots):
        low = jnp.concatenate([g_ref[o, slot] for o in range(owners)], axis=0)
        grad_ref[slot] = low.astype(F32)
        high, rest = two_parts(left_ref[slot])
        turned = mm(high, low) + mm(rest, low)
        t_high, t_rest = two_parts(turned)
        r_high, r_rest = two_parts(right_ref[slot])
        direction = mm(t_high, r_high) + mm(t_high, r_rest) + mm(t_rest, r_high)
        stepped = master_ref[slot] - 0.3 * direction
        stepped_ref[slot] = stepped
        square_ref[slot : slot + 1] = jnp.sum(stepped * stepped, axis=0, keepdims=True)


def stats_kernel(g_ref, left_ref, right_ref, new_left_ref, new_right_ref):
    owners, slots, piece, width = g_ref.shape
    for slot in range(slots):
        low = jnp.concatenate([g_ref[o, slot] for o in range(owners)], axis=0)
        new_left_ref[slot] = 0.5 * left_ref[slot] + 0.5 * mm(low, low, NT)
        new_right_ref[slot] = 0.5 * right_ref[slot] + 0.5 * mm(low, low, TN)


def finish_kernel(stepped_ref, ema_ref, norm_ref, master_ref, new_ema_ref):
    slots = stepped_ref.shape[0]
    for slot in range(slots):
        master = stepped_ref[slot] * lax.rsqrt(norm_ref[slot : slot + 1] + 1e-06)
        master_ref[slot] = master
        new_ema_ref[slot] = 0.5 * ema_ref[slot] + 0.5 * master


def block_specs(count, slots):
    return pl.BlockSpec((slots, BLOCK, BLOCK), lambda i: (i, 0, 0))


def exchange(value, axis, pairs):
    return lax.ppermute(value, axis, pairs)


def shards(
    tokens,
    seq_lengths,
    qkv_weight,
    out_weight,
    up_gate_weight,
    down_weight,
    qk_scale,
    mlp_scale,
    eigen_rates,
    cotangent,
    block_order,
    master_blocks,
    ema_blocks,
    left_stats,
    right_stats,
    left_root,
    right_root,
):
    x_rows = tokens[0]
    total, width = x_rows.shape
    cols = qk_scale.shape[0]
    heads = lax.axis_size("head")
    owners = lax.axis_size("batch")
    ranks = heads // 2
    here = lax.axis_index("head")
    rank, core = here // 2, here % 2
    share = total // heads
    rows = share // CHUNKS
    tiles_all = total // rows

    core_swap = [(i, i ^ 1) for i in range(heads)]
    shift_up = [
        [(i, (i // 2 + s) % ranks * 2 + i % 2) for i in range(heads)] for s in range(ranks)
    ]
    shift_down = [
        [(i, (i // 2 - s) % ranks * 2 + i % 2) for i in range(heads)] for s in range(ranks)
    ]
    far_steps = list(range(1, ranks))
    ring = far_steps + [0]

    shares = jnp.stack(
        [(rank - s) % ranks * 2 + (core + d) % 2 for d in (1, 0) for s in ring]
    ).astype(jnp.int32)
    ends = jnp.cumsum(seq_lengths[0])

    def begin_of(row):
        segment = jnp.sum((row[:, None] >= ends[None, :]).astype(jnp.int32), axis=1)
        member = segment[:, None] == jnp.arange(ends.shape[0], dtype=jnp.int32)[None, :]
        return jnp.sum(jnp.where(member, (ends - seq_lengths[0])[None, :], 0), axis=1)

    tile_rows = jnp.arange(tiles_all, dtype=jnp.int32) * rows
    tile_begin = begin_of(tile_rows)
    lane = jnp.arange(LANES, dtype=jnp.int32) % (HEAD_DIM // 2)
    freq = 10000.0 ** (-lane.astype(F32) * 2.0 / HEAD_DIM)
    near_angle = jnp.arange(rows, dtype=F32)[:, None] * freq[None, :]
    far_angle = (tile_rows - tile_begin).astype(F32)[:, None] * freq[None, :]
    near = jnp.stack([jnp.cos(near_angle), jnp.sin(near_angle)])
    far = jnp.stack([jnp.cos(far_angle), jnp.sin(far_angle)])
    gains = qk_scale[None, :]
    rates = eigen_rates.T

    q, k, v, q_rot, k_rot = project(x_rows, qkv_weight, gains, near, far)
    weights = [
        (up_gate_weight, down_weight),
        (exchange(up_gate_weight, "head", core_swap), exchange(down_weight, "head", core_swap)),
    ]
    scales = jnp.concatenate([mlp_scale, exchange(mlp_scale, "head", core_swap)], axis=1)

    def from_partner(send, keep, size):
        got = exchange(send, "head", core_swap)
        if ranks == 1:
            return keep[:size], [keep, got]
        away = (keep[:-size].astype(F32) + got[:-size].astype(F32)).astype(BF16)
        return away, [keep, got] + from_ranks(away, size)

    def from_ranks(away, size):
        return [
            exchange(away[n * size : (n + 1) * size], "head", shift_down[s])
            for n, s in enumerate(far_steps)
        ]

    def gather_ranks(own):
        return [exchange(own, "head", shift_up[s]) for s in far_steps] + [own]

    def gather_shares(own):
        mine = gather_ranks(own)
        return [exchange(b, "head", core_swap) for b in mine] + mine

    places = [(here * CHUNKS + j).astype(jnp.int32)[None] for j in range(CHUNKS)]
    tiles = [shares * CHUNKS + j for j in range(CHUNKS)]
    starts = [begin_of(t * rows) for t in tiles]
    chunks = range(CHUNKS)
    tile = 2 * BLOCK

    attn_out, lse, parts = [], [], []
    last = ()
    for j in chunks:
        half = heads // 2
        first = attend(
            q, k, v, out_weight, tiles[j][:half], starts[j][:half], rows, 0, heads, last
        )
        second = attend(
            q,
            k,
            v,
            out_weight,
            tiles[j][half:],
            starts[j][half:],
            rows,
            half,
            heads,
            (first[0], first[1]),
            2,
        )
        away, got = from_partner(first[2], second[2], rows)
        attn_out.append(second[0])
        lse.append(second[1])
        parts.append(got)
        last = (away,)
    joined = []
    for j in chunks:
        joined.append(join_attention(parts[j], x_rows, places[j], rates, rows, last))
        last = (joined[j][0],)
    hidden = [gather_ranks(joined[j][0]) for j in chunks]
    ffn = []
    for j in chunks:
        ffn.append(mlp(hidden[j], weights, scales, tile, last))
        last = (ffn[j][4],)
    ends_fwd = []
    for j in chunks:
        parts = [ffn[j][4]] + from_ranks(ffn[j][3], rows)
        ends_fwd.append(
            join_mlp(parts, joined[j][1], cotangent[0], j, rates, rows, last)
        )
        last = (ends_fwd[j][1],)
    d_rows = [gather_ranks(ends_fwd[j][1]) for j in chunks]
    back = []
    for j in chunks:
        back.append(mlp_back(d_rows[j], ffn[j][0], ffn[j][1], weights, scales, tile, last))
        last = (back[j][4],)

    row_blocks = width // BLOCK
    piece = BLOCK // owners
    across = ranks
    levels = owners // across
    z_here, x_here = lax.axis_index("batch") // across, lax.axis_index("batch") % across
    direct = levels if piece % 16 == 0 and across == 2 else 0
    x_place = x_here.astype(jnp.int32)[None]
    left_hidden = [b for h in hidden for b in h]
    left_down = [b for d in d_rows for b in d]
    rights = {
        "down": (left_down, [[f[2] for f in ffn]]),
        "up_gate": (left_hidden, [[b[0] for b in back], [b[1] for b in back]]),
    }

    def partner_part(name, after):
        out = outer(*rights[name], 1, 2, tile, after=after)[0]
        return out, exchange(out, "head", core_swap)

    def own_part(name, more, after):
        return outer(
            *rights[name], 0, 2, tile, more=(more,), place=x_place, levels=direct, after=after
        )

    def as_pieces(matrix):
        panels = matrix.shape[1] // BLOCK
        return (
            matrix.reshape(row_blocks, levels, across, piece, panels, BLOCK)
            .transpose(1, 2, 4, 0, 3, 5)
            .reshape(levels, across, panels * row_blocks * piece, BLOCK)
        )

    def from_this_x(pieces):
        return [
            lax.dynamic_index_in_dim(pieces, (x_here + s) % across, 1, keepdims=False)
            for s in range(across)
        ]

    def hold(value, anchor):
        return value if anchor is None else lax.optimization_barrier((value, anchor))[0]

    x_step = lambda s: [
        (i, i // across * across + (i % across + s) % across) for i in range(owners)
    ]
    z_step = lambda s: [
        (i, (i // across + s) % levels * across + i % across) for i in range(owners)
    ]
    z_place = z_here.astype(jnp.int32)[None]

    def over_z(parts):
        return [parts[0]] + [
            exchange(parts[s], "batch", z_step(s)) for s in range(1, levels)
        ]

    def plain_x(pieces):
        total = pieces[0].astype(F32)
        for s in range(1, across):
            total = total + exchange(pieces[s], "batch", x_step(s)).astype(F32)
        total = total.astype(BF16)
        return [
            lax.dynamic_index_in_dim(total, (z_here + s) % levels, 0, keepdims=False)
            for s in range(levels)
        ]

    def start_x(outs):
        if direct:
            mine, other = [flat(o) for o in outs]
            return mine, exchange(other, "batch", x_step(1))
        return from_this_x(as_pieces(outs[0]))

    def finish_x(started, after):
        if direct:
            sums = join_x(started, z_place, after)
        else:
            sums = plain_x([jnp.concatenate(p, axis=1) for p in zip(*started, strict=True)])
        return over_z(sums)

    split = []
    partner = {}
    for j in chunks:
        parts = [back[j][4]] + from_ranks(back[j][3], rows)
        split.append(
            split_attention(
                parts,
                ends_fwd[j][2],
                joined[j][1],
                joined[j][2],
                x_rows,
                places[j],
                rates,
                rows,
                last,
            )
        )
        last = (split[j][0],)
        if j == 0:
            out, partner["down"] = partner_part("down", last)
            last = (out,)
    out, partner["up_gate"] = partner_part("up_gate", last)
    last = (out,)
    d_attn_mine = [gather_ranks(split[j][0]) for j in chunks]
    flat = lambda a: a.reshape(a.shape[:-3] + (-1, BLOCK))
    started = {}
    for name, gathered in (("down", d_attn_mine[0]), ("up_gate", d_attn_mine[-1])):
        outs = own_part(name, partner[name], last + tuple(gathered[:-1]))
        last = (outs[0],)
        started[name] = start_x(outs)
    d_attn_rows = [
        [exchange(b, "head", core_swap) for b in mine] + mine for mine in d_attn_mine
    ]
    outs = outer(
        [b for d in d_attn_rows for b in d],
        [attn_out],
        0,
        1,
        tile,
        place=x_place,
        levels=direct,
        after=last,
    )
    last = (outs[0],)
    started["out"] = start_x(outs)
    order = (shares[:, None] * CHUNKS + jnp.arange(CHUNKS, dtype=jnp.int32)[None, :]).reshape(-1)
    moved = {}
    pairs_all = cols // LANES
    raws, gain_parts, late = [], [], []
    marks = []
    for pair in range(pairs_all):
        pair_back = []
        for j in chunks:
            pair_back.append(
                attend_back(
                    d_attn_rows[j],
                    q,
                    k,
                    v,
                    attn_out[j],
                    lse[j],
                    out_weight,
                    tiles[j],
                    starts[j],
                    rows,
                    pair,
                    last,
                )
            )
            last = (pair_back[-1][0],)
            marks.append(last[0])
            if pair == 0 and j == 0:
                moved["down_out"] = finish_x([started["down"], started["out"]], last)
                last = (moved["down_out"][0],)
        raw, gain_part, *outs = project_back(
            x_rows,
            q_rot,
            k_rot,
            gains,
            near,
            far,
            pair_back,
            order,
            rows,
            pair,
            x_place,
            direct,
            last,
        )
        last = (raw,)
        raws.append(raw)
        gain_parts.append(gain_part)
        late.append(start_x(outs))
        if pair == 0:
            last = last + tuple(moved["down_out"][1:])
            moved["up_gate"] = finish_x([started["up_gate"]], last)
            last = (moved["up_gate"][0],)
    arrived = moved["up_gate"][1:] + [a for pieces in late[:-1] for a in pieces[1:]]
    send, keep = input_back(raws, qkv_weight, order, rows, last + tuple(arrived))
    gain_grad = jnp.concatenate(gain_parts, axis=1)
    moved["late"] = finish_x(late, (keep,))

    def double(value, axis, size, anchors=()):
        step = 1
        turn = 0
        while step < size:
            got = exchange(value, axis, [(i, i ^ step) for i in range(size)])
            value = value + hold(got, anchors[turn] if turn < len(anchors) else None)
            step *= 2
            turn += 1
        return value

    rate_grad = double(
        jnp.concatenate([sum(s[2] for s in split), sum(e[3] for e in ends_fwd)], axis=0),
        "head",
        heads,
        marks,
    )
    both = sum(b[2] for b in back)
    scale_cols = mlp_scale.shape[1]
    scale_grad = both[:, :scale_cols] + exchange(both[:, scale_cols:], "head", core_swap)

    slot_order = block_order[0]
    panel, rest = slot_order // row_blocks, slot_order % row_blocks
    late_panels = 3 * pairs_all
    panels = slot_order.shape[0] // row_blocks
    down_panels = scale_cols // BLOCK
    late_panel = panel % pairs_all * 3 + panel // pairs_all
    down_panel = panel - (panels - down_panels) + late_panels
    held_panel = jnp.where(panel >= panels - down_panels, down_panel, panel + down_panels)
    place_of = jnp.where(panel < late_panels, late_panel, held_panel) * row_blocks + rest
    groups = [moved[n] for n in ("late", "down_out", "up_gate")]
    if direct:
        ordered = order_pieces(groups, place_of, piece, ())
    else:
        sums = [sum(a.astype(F32) for a in g).astype(BF16) for g in groups]
        pieces = jnp.concatenate(sums, axis=0).reshape(-1, piece, BLOCK)
        ordered = jnp.take(pieces, place_of, axis=0, mode="clip")
    got = exchange(send, "head", core_swap)
    parts = [keep, got]
    last = (ordered,)
    if ranks > 1:
        away = join_partner(keep, got, share, last)
        parts += from_ranks(away, share)
    per_owner = slot_order.shape[0] // owners
    owned = lax.all_to_all(
        ordered.reshape(owners, per_owner, piece, BLOCK),
        "batch",
        split_axis=0,
        concat_axis=0,
        tiled=True,
    )
    slots = min(8, per_owner)
    if piece % 16:
        owned = owned.transpose(1, 0, 2, 3).reshape(1, per_owner, BLOCK, BLOCK)
    g_spec = pl.BlockSpec(
        (owned.shape[0], slots) + owned.shape[2:], lambda i: (0, i, 0, 0)
    )
    blk = pl.BlockSpec((slots, BLOCK, BLOCK), lambda i: (i, 0, 0))
    row = pl.BlockSpec((slots, BLOCK), lambda i: (i, 0))
    cube = jax.ShapeDtypeStruct((per_owner, BLOCK, BLOCK), F32)
    grid = (per_owner // slots,)
    owned_grad, stepped, column_sq = pl.pallas_call(
        step_kernel,
        grid=grid,
        in_specs=[g_spec, blk, blk, blk],
        out_specs=[blk, blk, row],
        out_shape=[cube, cube, jax.ShapeDtypeStruct((per_owner, BLOCK), F32)],
        name="step",
        cost_estimate=COST,
    )(owned, left_root[0], right_root[0], master_blocks[0])
    new_left, new_right = launch(
        stats_kernel,
        "stats",
        grid,
        [(owned, g_spec), (left_stats[0], blk), (right_stats[0], blk)],
        [(cube, blk), (cube, blk)],
        after=(column_sq,),
    )
    my_blocks = lax.dynamic_slice_in_dim(
        slot_order, lax.axis_index("batch") * per_owner, per_owner, 0
    )
    member = (
        (my_blocks // row_blocks)[:, None] == jnp.arange(panels, dtype=jnp.int32)[None, :]
    ).astype(F32)
    precise = lax.Precision.HIGHEST
    sums = jnp.concatenate(
        [jnp.einsum("sp,sb->pb", member, column_sq, precision=precise)]
        + [a.reshape(-1, LANES) for a in (gain_grad, rate_grad, scale_grad)],
        axis=0,
    )
    d_input = sum_input(parts, [s[1] for s in split], rows, (new_left,))
    sums = double(sums, "batch", owners, (new_left, d_input))
    totals = sums[:panels]
    small = sums[panels:].reshape(-1)
    gain_sum = small[:cols]
    rate_sum = small[cols : cols + 2 * width].reshape(2, width)
    scale_sum = small[cols + 2 * width :].reshape(mlp_scale.shape)
    norms = jnp.einsum("sp,pb->sb", member, totals, precision=precise)
    new_master, new_ema = pl.pallas_call(
        finish_kernel,
        grid=grid,
        in_specs=[blk, blk, row],
        out_specs=[blk, blk],
        out_shape=[cube, cube],
        name="finish",
    )(stepped, ema_blocks[0], norms)
    gain_step = 0.5 / math.sqrt(total * owners)
    width_share = width // heads
    rate_here = lax.dynamic_slice_in_dim(rate_sum, here * width_share, width_share, 1)
    rate_slice = lax.dynamic_slice_in_dim(rates, here * width_share, width_share, 1)
    mlp_scale_out = jnp.stack([scale_sum, mlp_scale - gain_step * scale_sum])
    new_gains = jnp.concatenate(
        [(qk_scale - gain_step * gain_sum)[None, :], rate_slice - gain_step * rate_here], axis=0
    )
    out_share = jnp.concatenate([e[0] for e in ends_fwd], axis=0)
    return (
        out_share[None],
        d_input[None],
        owned_grad[None],
        new_master[None],
        new_ema[None],
        new_left[None],
        new_right[None],
        gain_sum,
        mlp_scale_out,
        rate_here.T,
        new_gains,
    )


def solution(mesh):
    return jax.shard_map(
        shards,
        mesh=mesh,
        in_specs=(
            P("batch", None, None),
            P("batch", None),
            P(None, None, "head"),
            P("head", None),
            P(None, None, "head"),
            P("head", None),
            P("head"),
            P(None, "head"),
            P(),
            P("batch", "head", None),
            P("head", None),
            P("head", "batch", None, None),
            P("head", "batch", None, None),
            P("head", "batch", None, None),
            P("head", "batch", None, None),
            P("head", "batch", None, None),
            P("head", "batch", None, None),
        ),
        out_specs=(
            P("batch", "head", None),
            P("batch", "head", None),
            P("head", "batch", None, None),
            P("head", "batch", None, None),
            P("head", "batch", None, None),
            P("head", "batch", None, None),
            P("head", "batch", None, None),
            P("head"),
            P(None, None, "head"),
            P("head", None),
            P(None, "head"),
        ),
        check_vma=False,
    )
```

```python
import functools
import math

import jax
import jax.numpy as jnp
from jax import lax
from jax.experimental import pallas as pl
from jax.experimental.pallas import tpu as pltpu
from jax.sharding import PartitionSpec as P

HEAD_DIM = 64
BLOCK = 128
LANES = 128
CHUNKS = 2
F32 = jnp.float32
BF16 = jnp.bfloat16
NN = (((1,), (0,)), ((), ()))
NT = (((1,), (1,)), ((), ()))
TN = (((0,), (0,)), ((), ()))
COST = pl.CostEstimate(flops=10**11, transcendentals=0, bytes_accessed=10**7)
SHORT = pl.CostEstimate(flops=10**10, transcendentals=0, bytes_accessed=10**7)


def mm(a, b, dims=NN):
    return lax.dot_general(a, b, dims, preferred_element_type=F32)


def whole(shape, single=False):
    zeros = (0,) * len(shape)
    if single:
        return pl.BlockSpec(shape, lambda *_: zeros, pipeline_mode=pl.Buffered(1))
    return pl.BlockSpec(shape, lambda *_: zeros)


def launch(kernel, name, grid, ins, outs, scratch=(), prefetch=(), after=(), alias=0, cost=COST):
    first, count, extra = len(prefetch), len(ins), len(after)

    def body(*refs):
        kernel(*refs[: first + count], *refs[first + count + extra :])

    return pl.pallas_call(
        body,
        grid_spec=pltpu.PrefetchScalarGridSpec(
            num_scalar_prefetch=first,
            grid=grid,
            in_specs=[s for _, s in ins] + [pl.BlockSpec(memory_space=pl.ANY)] * extra,
            out_specs=[s for _, s in outs],
            scratch_shapes=list(scratch),
        ),
        out_shape=[o for o, _ in outs],
        input_output_aliases={first + count + n: n for n in range(alias)},
        name=name,
        cost_estimate=cost,
    )(*prefetch, *[a for a, _ in ins], *after)


def like(shape, dtype):
    return jax.ShapeDtypeStruct(shape, dtype)


def rms_rows(value):
    return value * lax.rsqrt(jnp.mean(value * value, axis=-1, keepdims=True) + 1e-06)


def rms_factor(value):
    return lax.rsqrt(jnp.mean(value * value, axis=-1, keepdims=True) + 1e-06)


def rms_back(normed, factor, gradient):
    return factor * (gradient - normed * jnp.mean(gradient * normed, axis=-1, keepdims=True))


def lane_ids():
    return lax.broadcasted_iota(jnp.int32, (1, LANES), 1)


def head_mean(value, ones_block):
    high = value.astype(BF16)
    rest = (value - high.astype(F32)).astype(BF16)
    return (mm(high, ones_block) + mm(rest, ones_block)) * (1.0 / HEAD_DIM)


def ones_block():
    row = lax.broadcasted_iota(jnp.int32, (LANES, LANES), 0) // HEAD_DIM
    col = lax.broadcasted_iota(jnp.int32, (LANES, LANES), 1) // HEAD_DIM
    return jnp.where(row == col, 1.0, 0.0).astype(BF16)


def half_turn(value):
    first = (lane_ids() & (HEAD_DIM - 1)) < HEAD_DIM // 2
    return jnp.where(
        first,
        pltpu.roll(value, LANES - HEAD_DIM // 2, 1),
        pltpu.roll(value, HEAD_DIM // 2, 1),
    )


def angles(tile, near_ref, far_ref):
    cos_r, sin_r = near_ref[0], near_ref[1]
    cos_0 = far_ref[0, pl.ds(tile, 1), :]
    sin_0 = far_ref[1, pl.ds(tile, 1), :]
    first = (lane_ids() & (HEAD_DIM - 1)) < HEAD_DIM // 2
    sine = sin_0 * cos_r + cos_0 * sin_r
    return cos_0 * cos_r - sin_0 * sin_r, jnp.where(first, -sine, sine)


def project_kernel(
    x_ref, w_ref, gain_ref, near_ref, far_ref, q_ref, k_ref, v_ref, q_rot_ref, k_rot_ref
):
    tile = pl.program_id(0)
    cosine, sine = angles(tile, near_ref, far_ref)
    ones = ones_block()
    x = x_ref[...]
    for index, used_ref, rot_ref in ((0, q_ref, q_rot_ref), (1, k_ref, k_rot_ref)):
        raw = mm(x, w_ref[index])
        for pair in range(raw.shape[1] // LANES):
            lanes = slice(pair * LANES, (pair + 1) * LANES)
            value = raw[:, lanes]
            turned = value * cosine + half_turn(value) * sine
            factor = lax.rsqrt(head_mean(turned * turned, ones) + 1e-06)
            rot_ref[:, lanes] = turned
            used_ref[:, lanes] = (turned * factor * gain_ref[:, lanes]).astype(BF16)
    v_ref[...] = mm(x, w_ref[2]).astype(BF16)


def project(x, weight, gains, near, far):
    rows, width = x.shape
    cols = weight.shape[2]
    tile = near.shape[1]
    by_row = lambda w: pl.BlockSpec((tile, w), lambda i: (i, 0))
    return pl.pallas_call(
        project_kernel,
        grid=(rows // tile,),
        in_specs=[
            by_row(width),
            whole(weight.shape, True),
            whole((1, cols)),
            whole(near.shape),
            whole(far.shape),
        ],
        out_specs=[by_row(cols)] * 5,
        out_shape=[jax.ShapeDtypeStruct((rows, cols), BF16)] * 3
        + [jax.ShapeDtypeStruct((rows, cols), F32)] * 2,
        name="project",
        cost_estimate=COST,
    )(x, weight, gains, near, far)


def key_tiles(first_row, start, wide, narrow, visit):
    full = first_row // wide

    def step(index, carry):
        visit(pl.multiple_of(index * wide, wide), wide, False)
        return carry

    lax.fori_loop(start // wide, full, step, 0)
    diagonal = (first_row // narrow) * narrow

    @pl.when(diagonal > full * wide)
    def _():
        visit(pl.multiple_of(full * wide, narrow), narrow, False)

    visit(pl.multiple_of(diagonal, narrow), narrow, True)


def attend_kernel(
    wide, tiles, starts, q_ref, k_ref, v_ref, w_ref, o_ref, lse_ref, part_ref, acc, mixed
):
    index = pl.program_id(0)
    rows = q_ref.shape[0]
    first_row = tiles[index] * rows
    start = starts[index]
    narrow = wide // 2
    low = lane_ids() < HEAD_DIM
    zero = jnp.zeros((), BF16)

    def one_pair(pair, carry):
        lanes = pl.ds(pl.multiple_of(pair * LANES, LANES), LANES)
        q = q_ref[:, lanes] * jnp.asarray(1.0 / math.sqrt(HEAD_DIM), BF16)
        q_both = jnp.concatenate([jnp.where(low, q, zero), jnp.where(low, zero, q)], axis=0)
        acc[...] = jnp.zeros_like(acc)

        def visit(key_0, size, masked):
            keys = pl.ds(key_0, size)
            weights = jnp.exp(mm(q_both, k_ref[keys, lanes], NT))
            if masked:
                row = lax.broadcasted_iota(jnp.int32, (2 * rows, size), 0)
                row = jnp.where(row < rows, row, row - rows) + first_row
                col = lax.broadcasted_iota(jnp.int32, (2 * rows, size), 1) + key_0
                weights = jnp.where((col <= row) & (col >= start), weights, 0.0)
            total = weights[:, :LANES]
            for part in range(1, size // LANES):
                total = total + weights[:, part * LANES : (part + 1) * LANES]
            acc[:, LANES:] += total
            acc[:, :LANES] += mm(weights.astype(BF16), v_ref[keys, lanes])

        key_tiles(first_row, start, wide, narrow, visit)
        total_a = jnp.sum(acc[:rows, LANES:], axis=1, keepdims=True)
        total_b = jnp.sum(acc[rows:, LANES:], axis=1, keepdims=True)
        summed = jnp.where(low, acc[:rows, :LANES], acc[rows:, :LANES])
        out = (summed / jnp.where(low, total_a, total_b)).astype(BF16)
        o_ref[:, lanes] = out
        lse_ref[:, lanes] = jnp.log(jnp.where(low, total_b, total_a))
        mixed[:, lanes] = out
        return carry

    lax.fori_loop(0, q_ref.shape[1] // LANES, one_pair, 0)
    part_ref[...] = mm(mixed[...], w_ref[...]).astype(BF16)


def attend(q, k, v, weight, tiles, starts, rows, offset, places, after, alias=0):
    count = tiles.shape[0]
    cols = k.shape[1]
    width = weight.shape[1]
    at_place = pl.BlockSpec((rows, cols), lambda i, t, s: (i + offset, 0))
    return launch(
        functools.partial(attend_kernel, 4 * BLOCK),
        "attend",
        (count,),
        [
            (q, pl.BlockSpec((rows, cols), lambda i, t, s: (t[i], 0))),
            (k, whole(k.shape, True)),
            (v, whole(v.shape, True)),
            (weight, whole(weight.shape, True)),
        ],
        [
            (like((places * rows, cols), BF16), at_place),
            (like((places * rows, cols), F32), at_place),
            (like((count * rows, width), BF16), pl.BlockSpec((rows, width), lambda i, t, s: (i, 0))),
        ],
        scratch=[pltpu.VMEM((2 * rows, 2 * LANES), F32), pltpu.VMEM((rows, cols), BF16)],
        prefetch=(tiles, starts),
        after=after,
        alias=alias,
    )


def attend_back_kernel(blocks, wide, tiles, starts, *refs):
    row_refs = refs[:blocks]
    q_ref, k_ref, v_ref = refs[blocks : blocks + 3]
    o_refs = refs[blocks + 3 : blocks + 3 + CHUNKS]
    lse_refs = refs[blocks + 3 + CHUNKS : blocks + 3 + 2 * CHUNKS]
    w_ref, dq_ref, dk_ref, dv_ref, rows_s, o_ref, lse_ref, acc = refs[blocks + 3 + 2 * CHUNKS :]
    index = pl.program_id(0)
    rows = q_ref.shape[0]
    narrow = wide // 2

    @pl.when(index == 0)
    def _():
        dk_ref[...] = jnp.zeros_like(dk_ref)
        dv_ref[...] = jnp.zeros_like(dv_ref)

    for block in range(blocks):

        @pl.when(index == block)
        def _(block=block):
            rows_s[...] = row_refs[block][...]

    for chunk in range(CHUNKS):

        @pl.when(index // (blocks // CHUNKS) == chunk)
        def _(chunk=chunk):
            o_ref[...] = o_refs[chunk][...]
            lse_ref[...] = lse_refs[chunk][...]

    first_row = tiles[index] * rows
    start = starts[index]
    low = lane_ids() < HEAD_DIM
    place = lane_ids() & (HEAD_DIM - 1)
    zero = jnp.zeros((), BF16)
    ones = jnp.where(place < 3, 1.0, 0.0).astype(BF16)

    def parts(value):
        high = value.astype(BF16).astype(F32)
        rest = value - high
        middle = rest.astype(BF16).astype(F32)
        picked = jnp.where(place == 1, middle, jnp.where(place == 2, rest - middle, 0.0))
        return jnp.where(place == 0, high, picked).astype(BF16)

    d_rows = rows_s[...]
    d_attn = mm(d_rows, w_ref[...], NT).astype(BF16)
    for pair in range(q_ref.shape[1] // LANES):
        lanes = slice(pair * LANES, (pair + 1) * LANES)
        q = q_ref[:, lanes] * jnp.asarray(1.0 / math.sqrt(HEAD_DIM), BF16)
        d_out = d_attn[:, lanes]
        minus_lse = parts(-lse_ref[:, lanes])
        product = d_out.astype(F32) * o_ref[:, lanes].astype(F32)
        sum_a = jnp.sum(jnp.where(low, product, 0.0), axis=1, keepdims=True)
        sum_b = jnp.sum(jnp.where(low, 0.0, product), axis=1, keepdims=True)
        minus_delta = parts(-jnp.where(low, sum_b, sum_a))
        q_ext = (jnp.where(low, q, minus_lse), jnp.where(low, minus_lse, q))
        d_ext = (jnp.where(low, d_out, minus_delta), jnp.where(low, minus_delta, d_out))
        q_both = jnp.concatenate([jnp.where(low, q, zero), jnp.where(low, zero, q)], axis=0)
        d_both = jnp.concatenate(
            [jnp.where(low, d_out, zero), jnp.where(low, zero, d_out)], axis=0
        )
        acc[...] = jnp.zeros_like(acc)

        def visit(key_0, size, masked):
            keys = pl.ds(key_0, size)
            k = k_ref[keys, lanes]
            v = v_ref[keys, lanes]
            k_ext = (jnp.where(low, k, ones), jnp.where(low, ones, k))
            v_ext = (jnp.where(low, v, ones), jnp.where(low, ones, v))
            if masked:
                col = lax.broadcasted_iota(jnp.int32, (size, rows), 1) + first_row
                row = lax.broadcasted_iota(jnp.int32, (size, rows), 0) + key_0
                allowed = (row <= col) & (row >= start)
            probs = []
            d_scores = []
            for head in range(2):
                prob = jnp.exp(mm(k_ext[head], q_ext[head], NT))
                if masked:
                    prob = jnp.where(allowed, prob, 0.0)
                d_score = prob * mm(v_ext[head], d_ext[head], NT)
                probs.append(prob.astype(BF16))
                d_scores.append(d_score.astype(BF16))
            dv_ref[keys, lanes] += mm(jnp.concatenate(probs, axis=1), d_both)
            dk_ref[keys, lanes] += mm(jnp.concatenate(d_scores, axis=1), q_both)
            k_both = jnp.concatenate([jnp.where(low, k, zero), jnp.where(low, zero, k)], axis=0)
            acc[...] += mm(jnp.concatenate(d_scores, axis=0), k_both, TN)

        key_tiles(first_row, start, wide, narrow, visit)
        dq_ref[:, lanes] = acc[...] * (1.0 / math.sqrt(HEAD_DIM))


def attend_back(row_blocks, q, k, v, outs, lses, weight, tiles, starts, rows, pair, after):
    count = tiles.shape[0]
    total = k.shape[0]
    width = weight.shape[1]
    at_tile = pl.BlockSpec((rows, LANES), lambda i, t, s: (t[i], pair))
    each = count // CHUNKS

    def at_step(chunk):
        return pl.BlockSpec(
            (rows, LANES), lambda i, t, s: (jnp.clip(i - chunk * each, 0, each - 1), pair)
        )

    column = pl.BlockSpec((total, LANES), lambda *_: (0, pair), pipeline_mode=pl.Buffered(1))
    return launch(
        functools.partial(attend_back_kernel, len(row_blocks), 4 * BLOCK),
        "attend_back",
        (count,),
        [(b, whole(b.shape, True)) for b in row_blocks]
        + [
            (q, at_tile),
            (k, column),
            (v, column),
        ]
        + [(a, at_step(n)) for n, a in enumerate(outs)]
        + [(a, at_step(n)) for n, a in enumerate(lses)]
        + [
            (weight, pl.BlockSpec((LANES, width), lambda *_: (pair, 0))),
        ],
        [
            (like((count * rows, LANES), F32), pl.BlockSpec((rows, LANES), lambda i, *_: (i, 0))),
            (like((total, LANES), F32), whole((total, LANES))),
            (like((total, LANES), F32), whole((total, LANES))),
        ],
        scratch=[
            pltpu.VMEM((rows, width), BF16),
            pltpu.VMEM((rows, LANES), BF16),
            pltpu.VMEM((rows, LANES), F32),
            pltpu.VMEM((rows, LANES), F32),
        ],
        prefetch=(tiles, starts),
        after=after,
        cost=SHORT,
    )


def sum_parts(refs):
    total = refs[0][...].astype(F32)
    for ref in refs[1:]:
        total = total + ref[...].astype(F32)
    return total


def join_attention_kernel(parts, place, *refs):
    x_ref, rate_ref = refs[parts : parts + 2]
    low_ref, hidden_ref, branch_ref = refs[parts + 2 :]
    branch = sum_parts(refs[:parts])
    x = x_ref[...].astype(F32)
    hidden = rms_rows(x + rate_ref[0:1] * (rms_rows(branch) - x))
    branch_ref[...] = branch
    hidden_ref[...] = hidden
    low_ref[...] = hidden.astype(BF16)


def part_specs(parts, rows, width):
    return [
        pl.BlockSpec((rows, width), lambda i, *_, last=a.shape[0] // rows: (last - SUB + i, 0))
        for a in parts
    ]


SUB = 2


def join_attention(parts, x, place, rates, share, after):
    width = x.shape[1]
    rows = share // SUB
    here = pl.BlockSpec((rows, width), lambda i, p: (i, 0))
    return launch(
        functools.partial(join_attention_kernel, len(parts)),
        "join_attention",
        (SUB,),
        list(zip(parts, part_specs(parts, rows, width), strict=True))
        + [
            (x, pl.BlockSpec((rows, width), lambda i, p: (p[0] * SUB + i, 0))),
            (rates, whole(rates.shape)),
        ],
        [(like((share, width), d), here) for d in (BF16, F32, F32)],
        prefetch=(place,),
        after=after,
    )


def weight_tiles(weight, down, step, side):
    _, width, cols = weight.shape
    count = cols // step
    if side == 0:
        at = lambda t: jnp.minimum(t, count - 1)
    else:
        at = lambda t: jnp.maximum(t - count, 0)
    return [
        (weight, pl.BlockSpec((2, width, step), lambda t, *_: (0, 0, at(t)))),
        (down, pl.BlockSpec((step, width), lambda t, *_: (at(t), 0))),
    ]


def mlp_kernel(blocks, *refs):
    row_refs = refs[:blocks]
    sides = (refs[blocks : blocks + 2], refs[blocks + 2 : blocks + 4])
    scale_ref = refs[blocks + 4]
    up_ref, gate_ref, mixed_ref, away_ref, own_ref, x_s, acc = refs[blocks + 5 :]
    tile = pl.program_id(0)
    count = pl.num_programs(0)
    rows = row_refs[0].shape[0]

    @pl.when(tile == 0)
    def _():
        for block in range(blocks):
            x_s[block * rows : (block + 1) * rows] = row_refs[block][...]
        acc[...] = jnp.zeros_like(acc)

    def run(w_ref, down_ref):
        x = x_s[...]
        up = mm(x, w_ref[0])
        gate = mm(x, w_ref[1])
        up_ref[...] = up.astype(BF16)
        gate_ref[...] = gate.astype(BF16)
        scaled = gate * scale_ref[1:2]
        mixed = (up * scale_ref[0:1] * (scaled * jax.nn.sigmoid(scaled))).astype(BF16)
        mixed_ref[...] = mixed
        acc[...] += mm(mixed, down_ref[...])

    for side in range(2):

        @pl.when(tile // (count // 2) == side)
        def _(side=side):
            run(*sides[side])

    @pl.when(tile == count - 1)
    def _():
        last = (blocks - 1) * rows
        own_ref[...] = acc[last:]
        if blocks > 1:
            away_ref[...] = acc[:last].astype(BF16)


def mlp(row_blocks, weights, scales, step, after):
    rows, width = row_blocks[0].shape
    blocks = len(row_blocks)
    height = rows * blocks
    cols = 2 * weights[0][0].shape[2]
    at_tile = lambda h: pl.BlockSpec((h, step), lambda t: (0, t))
    far = max(blocks - 1, 1) * rows
    return launch(
        functools.partial(mlp_kernel, blocks),
        "mlp",
        (cols // step,),
        [(b, whole(b.shape, True)) for b in row_blocks]
        + weight_tiles(*weights[0], step, 0)
        + weight_tiles(*weights[1], step, 1)
        + [(scales, at_tile(2))],
        [(like((height, cols), BF16), at_tile(height))] * 3
        + [
            (like((far, width), BF16), whole((far, width))),
            (like((rows, width), F32), whole((rows, width))),
        ],
        scratch=[pltpu.VMEM((height, width), BF16), pltpu.VMEM((height, width), F32)],
        after=after,
    )


def join_mlp_kernel(parts, *refs):
    hidden_ref, cot_ref, rate_ref = refs[parts : parts + 3]
    out_ref, low_ref, d_hidden_ref, rate_grad_ref = refs[parts + 3 :]
    branch = sum_parts(refs[:parts])
    hidden = hidden_ref[...]
    rate = rate_ref[1:2]
    factor = rms_factor(branch)
    normed = branch * factor
    gap = normed - hidden
    before = hidden + rate * gap
    factor_out = rms_factor(before)
    out = before * factor_out
    d_before = rms_back(out, factor_out, cot_ref[...].astype(F32))
    out_ref[...] = out
    d_hidden_ref[...] = (1.0 - rate) * d_before
    low_ref[...] = rms_back(normed, factor, rate * d_before).astype(BF16)

    @pl.when(pl.program_id(0) == 0)
    def _():
        rate_grad_ref[...] = jnp.zeros_like(rate_grad_ref)

    rate_grad_ref[...] += jnp.sum(d_before * gap, axis=0, keepdims=True)


def join_mlp(parts, hidden, cotangent, chunk, rates, share, after):
    width = hidden.shape[1]
    rows = share // SUB
    here = pl.BlockSpec((rows, width), lambda i: (i, 0))
    return launch(
        functools.partial(join_mlp_kernel, len(parts)),
        "join_mlp",
        (SUB,),
        list(zip(parts, part_specs(parts, rows, width), strict=True))
        + [
            (hidden, here),
            (cotangent, pl.BlockSpec((rows, width), lambda i: (chunk * SUB + i, 0))),
            (rates, whole(rates.shape)),
        ],
        [(like((share, width), d), here) for d in (F32, BF16, F32)]
        + [(like((1, width), F32), whole((1, width)))],
        after=after,
    )


def mlp_back_kernel(blocks, *refs):
    row_refs = refs[:blocks]
    sides = (refs[blocks : blocks + 2], refs[blocks + 2 : blocks + 4])
    scale_ref, up_ref, gate_ref = refs[blocks + 4 : blocks + 7]
    d_up_ref, d_gate_ref, sums_ref, away_ref, own_ref, x_s, acc = refs[blocks + 7 :]
    tile = pl.program_id(0)
    count = pl.num_programs(0)
    rows = row_refs[0].shape[0]

    @pl.when(tile == 0)
    def _():
        for block in range(blocks):
            x_s[block * rows : (block + 1) * rows] = row_refs[block][...]
        acc[...] = jnp.zeros_like(acc)

    def run(w_ref, down_ref):
        d_mixed = mm(x_s[...], down_ref[...], NT)
        up_raw = up_ref[...].astype(F32)
        gate_raw = gate_ref[...].astype(F32)
        scale_up = scale_ref[0:1]
        scale_gate = scale_ref[1:2]
        gate = gate_raw * scale_gate
        sig = jax.nn.sigmoid(gate)
        d_up = d_mixed * (gate * sig)
        d_gate = d_mixed * (up_raw * scale_up) * (sig * (1.0 + gate * (1.0 - sig)))
        sums_ref[0:1] = jnp.sum(d_up * up_raw, axis=0, keepdims=True)
        sums_ref[1:2] = jnp.sum(d_gate * gate_raw, axis=0, keepdims=True)
        d_up = (d_up * scale_up).astype(BF16)
        d_gate = (d_gate * scale_gate).astype(BF16)
        d_up_ref[...] = d_up
        d_gate_ref[...] = d_gate
        acc[...] += mm(d_up, w_ref[0], NT) + mm(d_gate, w_ref[1], NT)

    for side in range(2):

        @pl.when(tile // (count // 2) == side)
        def _(side=side):
            run(*sides[side])

    @pl.when(tile == count - 1)
    def _():
        last = (blocks - 1) * rows
        own_ref[...] = acc[last:]
        if blocks > 1:
            away_ref[...] = acc[:last].astype(BF16)


def mlp_back(row_blocks, up, gate, weights, scales, step, after):
    rows, width = row_blocks[0].shape
    blocks = len(row_blocks)
    height = rows * blocks
    cols = 2 * weights[0][0].shape[2]
    at_tile = lambda h: pl.BlockSpec((h, step), lambda t: (0, t))
    far = max(blocks - 1, 1) * rows
    return launch(
        functools.partial(mlp_back_kernel, blocks),
        "mlp_back",
        (cols // step,),
        [(b, whole(b.shape, True)) for b in row_blocks]
        + weight_tiles(*weights[0], step, 0)
        + weight_tiles(*weights[1], step, 1)
        + [(scales, at_tile(2)), (up, at_tile(height)), (gate, at_tile(height))],
        [(like((height, cols), BF16), at_tile(height))] * 2
        + [
            (like((2, cols), F32), at_tile(2)),
            (like((far, width), BF16), whole((far, width))),
            (like((rows, width), F32), whole((rows, width))),
        ],
        scratch=[pltpu.VMEM((height, width), BF16), pltpu.VMEM((height, width), F32)],
        after=after,
    )


def split_attention_kernel(parts, place, *refs):
    d_hidden_ref, hidden_ref, branch_ref, x_ref, rate_ref = refs[parts : parts + 5]
    low_ref, d_input_ref, rate_grad_ref = refs[parts + 5 :]
    d_hidden = sum_parts(refs[:parts]) + d_hidden_ref[...]
    hidden = hidden_ref[...]
    branch = branch_ref[...]
    x = x_ref[...].astype(F32)
    rate = rate_ref[0:1]
    factor = rms_factor(branch)
    normed = branch * factor
    gap = normed - x
    d_before = rms_back(hidden, rms_factor(x + rate * gap), d_hidden)
    d_input_ref[...] = (1.0 - rate) * d_before
    low_ref[...] = rms_back(normed, factor, rate * d_before).astype(BF16)

    @pl.when(pl.program_id(0) == 0)
    def _():
        rate_grad_ref[...] = jnp.zeros_like(rate_grad_ref)

    rate_grad_ref[...] += jnp.sum(d_before * gap, axis=0, keepdims=True)


def split_attention(parts, d_hidden, hidden, branch, x, place, rates, share, after):
    width = x.shape[1]
    rows = share // SUB
    here = pl.BlockSpec((rows, width), lambda i, p: (i, 0))
    return launch(
        functools.partial(split_attention_kernel, len(parts)),
        "split_attention",
        (SUB,),
        list(zip(parts, part_specs(parts, rows, width), strict=True))
        + [(d_hidden, here), (hidden, here), (branch, here)]
        + [
            (x, pl.BlockSpec((rows, width), lambda i, p: (p[0] * SUB + i, 0))),
            (rates, whole(rates.shape)),
        ],
        [(like((share, width), d), here) for d in (BF16, F32)]
        + [(like((1, width), F32), whole((1, width)))],
        prefetch=(place,),
        after=after,
    )


def project_back_kernel(order, x_here, *refs):
    x_ref, q_rot_ref, k_rot_ref, gain_ref, near_ref, far_ref = refs[:6]
    d_refs = refs[6:9]
    raw_ref, gain_grad_ref = refs[9:11]
    grad_refs = refs[11:-2]
    acc, held = refs[-2:]
    index = pl.program_id(0)
    count = pl.num_programs(0)

    @pl.when(index == 0)
    def _():
        gain_grad_ref[...] = jnp.zeros_like(gain_grad_ref)
        acc[...] = jnp.zeros_like(acc)

    cosine, sine = angles(order[index], near_ref, far_ref)
    ones = ones_block()
    d_raw = []
    for which, rot_ref in ((0, q_rot_ref), (1, k_rot_ref)):
        d_used = d_refs[which][...]
        turned = rot_ref[...]
        factor = lax.rsqrt(head_mean(turned * turned, ones) + 1e-06)
        normed = turned * factor
        gain_grad_ref[...] += jnp.sum(d_used * normed, axis=0, keepdims=True)
        d_normed = d_used * gain_ref[...]
        d_turned = factor * (d_normed - normed * head_mean(d_normed * normed, ones))
        d_raw.append((d_turned * cosine - half_turn(d_turned) * sine).astype(BF16))
    d_raw.append(d_refs[2][...].astype(BF16))
    d_all = jnp.concatenate(d_raw, axis=1)
    raw_ref[...] = d_all
    acc[...] += mm(d_all, x_ref[...], TN)

    @pl.when(index == count - 1)
    def _():
        held[...] = acc[...].T.astype(BF16)
        if len(grad_refs) == 1:
            grad_refs[0][...] = held[...]
        else:
            store_pieces(held, x_here[0], *grad_refs)


def project_back(x, q_rot, k_rot, gains, near, far, parts, order, rows, pair, place, levels, after):
    total, width = x.shape
    count = order.shape[0]
    wide = 3 * LANES
    at_tile = lambda w, n: pl.BlockSpec((rows, w), lambda i, t, *_: (t[i], n))
    if levels:
        shape = (levels, 3 * (width // BLOCK), BLOCK // (2 * levels), BLOCK)
        grads = [(like(shape, BF16), whole(shape))] * 2
    else:
        grads = [(like((width, wide), BF16), whole((width, wide)))]
    return launch(
        project_back_kernel,
        "project_back",
        (count,),
        [
            (x, at_tile(width, 0)),
            (q_rot, at_tile(LANES, pair)),
            (k_rot, at_tile(LANES, pair)),
            (gains, pl.BlockSpec((1, LANES), lambda *_: (0, pair))),
            (near, whole(near.shape)),
            (far, whole(far.shape)),
        ]
        + [(parts[0], pl.BlockSpec((rows, LANES), lambda i, *_: (i, 0)))]
        + [(a, at_tile(LANES, 0)) for a in parts[1:]],
        [
            (like((total, wide), BF16), at_tile(wide, 0)),
            (like((1, LANES), F32), whole((1, LANES))),
        ]
        + grads,
        scratch=[pltpu.VMEM((wide, width), F32), pltpu.VMEM((width, wide), BF16)],
        prefetch=(order, place),
        after=after,
    )


def input_back_kernel(pairs, order, *refs):
    raw_refs = refs[:pairs]
    w_ref, send_ref, keep_ref = refs[pairs : pairs + 3]
    index = pl.program_id(0)
    count = pl.num_programs(0)
    d_x = None
    for which in range(3):
        lanes = slice(which * LANES, (which + 1) * LANES)
        d_all = jnp.concatenate([r[:, lanes] for r in raw_refs], axis=1)
        product = mm(d_all, w_ref[which], NT)
        d_x = product if d_x is None else d_x + product
    d_x = d_x.astype(BF16)

    @pl.when(index < count // 2)
    def _():
        send_ref[...] = d_x

    @pl.when(index >= count // 2)
    def _():
        keep_ref[...] = d_x


def input_back(raws, weight, order, rows, after):
    count = order.shape[0]
    half = count // 2
    width = weight.shape[1]
    out = like((half * rows, width), BF16)
    return launch(
        functools.partial(input_back_kernel, len(raws)),
        "input_back",
        (count,),
        [(r, pl.BlockSpec((rows, r.shape[1]), lambda i, t: (t[i], 0))) for r in raws]
        + [(weight, whole(weight.shape, True))],
        [
            (out, pl.BlockSpec((rows, width), lambda i, *_: (jnp.minimum(i, half - 1), 0))),
            (out, pl.BlockSpec((rows, width), lambda i, *_: (jnp.maximum(i - half, 0), 0))),
        ],
        prefetch=(order,),
        after=after,
    )


def join_x_kernel(units, place, *refs):
    out_refs = refs[2 * units :]
    levels = len(out_refs)
    for step in range(levels):
        level = (place[0] + step) % levels
        row = 0
        for unit in range(units):
            mine_ref, got_ref = refs[2 * unit : 2 * unit + 2]
            both = mine_ref[level].astype(F32) + got_ref[level].astype(F32)
            height = both.shape[0]
            out_refs[step][row : row + height] = both.astype(BF16)
            row += height


def join_x(units, z_place, after):
    levels, _, width = units[0][0].shape
    height = sum(u[0].shape[1] for u in units)
    arrays = [a for u in units for a in u]
    return launch(
        functools.partial(join_x_kernel, len(units)),
        "join_x",
        (1,),
        [(a, whole(a.shape)) for a in arrays],
        [(like((height, width), BF16), whole((height, width)))] * levels,
        prefetch=(z_place,),
        after=after,
    )


def join_partner_kernel(keep_ref, got_ref, out_ref):
    out_ref[...] = (keep_ref[...].astype(F32) + got_ref[...].astype(F32)).astype(BF16)


def join_partner(keep, got, size, after):
    width = keep.shape[1]
    away = keep.shape[0] - size
    block = pl.BlockSpec((size // 2, width), lambda i: (i, 0))
    return launch(
        join_partner_kernel,
        "join_partner",
        (away // (size // 2),),
        [(keep, block), (got, block)],
        [(like((away, width), BF16), block)],
        after=after,
    )[0]


def sum_input_kernel(parts, *refs):
    straight = refs[parts : parts + CHUNKS]
    out_ref = refs[-1]
    chunk = pl.program_id(0)
    value = straight[0][...]
    for other in range(1, CHUNKS):
        value = jnp.where(chunk == other, straight[other][...], value)
    out_ref[...] = value + sum_parts(refs[:parts])


def sum_input(parts, straight, rows, after):
    width = straight[0].shape[1]
    last = lambda a: a.shape[0] // rows - CHUNKS
    return launch(
        functools.partial(sum_input_kernel, len(parts)),
        "sum_input",
        (CHUNKS,),
        [
            (a, pl.BlockSpec((rows, width), lambda i, first=last(a): (first + i, 0)))
            for a in parts
        ]
        + [(a, whole(a.shape)) for a in straight],
        [
            (
                like((CHUNKS * rows, width), F32),
                pl.BlockSpec((rows, width), lambda i: (i, 0)),
            )
        ],
        after=after,
    )[0]


def order_kernel(counts, order, *refs):
    groups = []
    at = 0
    for n in counts:
        groups.append(refs[at : at + n])
        at += n
    out_ref, held = refs[at:]
    row = 0
    for group in groups:
        total = sum_parts(group)
        height = total.shape[0]
        held[row : row + height] = total.astype(BF16)
        row += height
    slots, piece, _ = out_ref.shape

    def move(slot, carry):
        start = pl.multiple_of(order[slot] * piece, piece)
        out_ref[slot] = held[pl.ds(start, piece)]
        return carry

    lax.fori_loop(0, slots, move, 0, unroll=8)


def order_pieces(groups, order, piece, after):
    arrays = [a for g in groups for a in g]
    slots = order.shape[0]
    shape = (slots, piece, BLOCK)
    return launch(
        functools.partial(order_kernel, [len(g) for g in groups]),
        "order_pieces",
        (1,),
        [(a, whole(a.shape)) for a in arrays],
        [(like(shape, BF16), whole(shape))],
        scratch=[pltpu.VMEM((slots * piece, BLOCK), BF16)],
        prefetch=(order,),
        after=after,
    )[0]


def outer_kernel(lefts, groups, rights, has_more, pieces, *refs):
    if pieces:
        place, refs = refs[0], refs[1:]
    left_refs = refs[:lefts]
    right_refs = refs[lefts : lefts + groups * rights]
    more_refs = refs[lefts + groups * rights : lefts + groups * rights + has_more]
    out_refs = refs[lefts + groups * rights + has_more : -2]
    turned, held = refs[-2:]
    rows = left_refs[0].shape[0]
    index = pl.program_id(0)

    @pl.when(index == 0)
    def _():
        for block in range(lefts):
            turned[:, block * rows : (block + 1) * rows] = left_refs[block][...].T

    def run(used):
        high = used[0].shape[0]
        total = mm(turned[:, :high], used[0][...])
        for n in range(1, rights):
            total = total + mm(turned[:, n * high : (n + 1) * high], used[n][...])
        for more in more_refs:
            total = total + more[...].astype(F32)
        if pieces:
            held[...] = total.astype(BF16)
        else:
            out_refs[0][...] = total.astype(BF16)

    if groups == 1:
        run(right_refs)
    else:
        for group in range(groups):

            @pl.when(index // (pl.num_programs(0) // groups) == group)
            def _(group=group):
                run(right_refs[group * rights : (group + 1) * rights])

    if pieces:
        store_pieces(held, place[0], *out_refs)


def store_pieces(held, x_here, *outs):
    levels, piece = outs[0].shape[0], outs[0].shape[-2]
    tall, wide = held.shape
    row_blocks = tall // BLOCK
    for side in range(2):
        shift = pl.multiple_of((x_here + side) % 2 * piece, piece)
        for panel in range(wide // BLOCK):
            lanes = slice(panel * BLOCK, (panel + 1) * BLOCK)
            for block in range(row_blocks):
                for level in range(levels):
                    start = block * BLOCK + 2 * level * piece
                    outs[side][level, panel * row_blocks + block] = held[
                        pl.ds(shift + start, piece), lanes
                    ]


def outer(left, groups, side, sides, step, more=(), place=None, levels=0, after=(), cost=COST):
    rows, width = left[0].shape
    cols = groups[0][0].shape[1] // sides
    step = min(step, cols)
    tiles = cols // step
    count = tiles * len(groups)

    def columns(array, group):
        if len(groups) == 1:
            at = lambda i, *_: (0, side * tiles + i)
        else:
            at = lambda i, *_: (0, side * tiles + jnp.clip(i - group * tiles, 0, tiles - 1))
        return array, pl.BlockSpec((array.shape[0], step), at)

    ins = (
        [(a, whole(a.shape, True)) for a in left]
        + [columns(a, n) for n, group in enumerate(groups) for a in group]
        + [(a, pl.BlockSpec((width, step), lambda i, *_: (0, i))) for a in more]
    )
    if not levels:
        outs = [
            (like((width, cols * len(groups)), BF16), pl.BlockSpec((width, step), lambda i: (0, i)))
        ]
    else:
        piece = BLOCK // (2 * levels)
        held = step // BLOCK * (width // BLOCK)
        outs = [
            (
                like((levels, held * count, piece, BLOCK), BF16),
                pl.BlockSpec((levels, held, piece, BLOCK), lambda i, p: (0, i, 0, 0)),
            )
        ] * 2
    return launch(
        functools.partial(
            outer_kernel, len(left), len(groups), len(groups[0]), len(more), levels > 0
        ),
        "outer",
        (count,),
        ins,
        outs,
        scratch=[pltpu.VMEM((width, rows * len(left)), BF16), pltpu.VMEM((width, step), BF16)],
        prefetch=(place,) if levels else (),
        after=after,
        cost=cost,
    )


def two_parts(value):
    high = value.astype(BF16)
    return high, (value - high.astype(F32)).astype(BF16)


def step_kernel(g_ref, left_ref, right_ref, master_ref, grad_ref, stepped_ref, square_ref):
    owners, slots, piece, width = g_ref.shape
    for slot in range(slots):
        low = jnp.concatenate([g_ref[o, slot] for o in range(owners)], axis=0)
        grad_ref[slot] = low.astype(F32)
        high, rest = two_parts(left_ref[slot])
        turned = mm(high, low) + mm(rest, low)
        t_high, t_rest = two_parts(turned)
        r_high, r_rest = two_parts(right_ref[slot])
        direction = mm(t_high, r_high) + mm(t_high, r_rest) + mm(t_rest, r_high)
        stepped = master_ref[slot] - 0.3 * direction
        stepped_ref[slot] = stepped
        square_ref[slot : slot + 1] = jnp.sum(stepped * stepped, axis=0, keepdims=True)


def stats_kernel(g_ref, left_ref, right_ref, new_left_ref, new_right_ref):
    owners, slots, piece, width = g_ref.shape
    for slot in range(slots):
        low = jnp.concatenate([g_ref[o, slot] for o in range(owners)], axis=0)
        new_left_ref[slot] = 0.5 * left_ref[slot] + 0.5 * mm(low, low, NT)
        new_right_ref[slot] = 0.5 * right_ref[slot] + 0.5 * mm(low, low, TN)


def finish_kernel(stepped_ref, ema_ref, norm_ref, master_ref, new_ema_ref):
    slots = stepped_ref.shape[0]
    for slot in range(slots):
        master = stepped_ref[slot] * lax.rsqrt(norm_ref[slot : slot + 1] + 1e-06)
        master_ref[slot] = master
        new_ema_ref[slot] = 0.5 * ema_ref[slot] + 0.5 * master


def block_specs(count, slots):
    return pl.BlockSpec((slots, BLOCK, BLOCK), lambda i: (i, 0, 0))


def exchange(value, axis, pairs):
    return lax.ppermute(value, axis, pairs)


def shards(
    tokens,
    seq_lengths,
    qkv_weight,
    out_weight,
    up_gate_weight,
    down_weight,
    qk_scale,
    mlp_scale,
    eigen_rates,
    cotangent,
    block_order,
    master_blocks,
    ema_blocks,
    left_stats,
    right_stats,
    left_root,
    right_root,
):
    x_rows = tokens[0]
    total, width = x_rows.shape
    cols = qk_scale.shape[0]
    heads = lax.axis_size("head")
    owners = lax.axis_size("batch")
    ranks = heads // 2
    here = lax.axis_index("head")
    rank, core = here // 2, here % 2
    share = total // heads
    rows = share // CHUNKS
    tiles_all = total // rows

    core_swap = [(i, i ^ 1) for i in range(heads)]
    shift_up = [
        [(i, (i // 2 + s) % ranks * 2 + i % 2) for i in range(heads)] for s in range(ranks)
    ]
    shift_down = [
        [(i, (i // 2 - s) % ranks * 2 + i % 2) for i in range(heads)] for s in range(ranks)
    ]
    far_steps = list(range(1, ranks))
    ring = far_steps + [0]

    shares = jnp.stack(
        [(rank - s) % ranks * 2 + (core + d) % 2 for d in (1, 0) for s in ring]
    ).astype(jnp.int32)
    lengths = seq_lengths[0]
    upto = jnp.arange(lengths.shape[0], dtype=jnp.int32)
    ends = jnp.sum(jnp.where(upto[None, :] <= upto[:, None], lengths[None, :], 0), axis=1)

    def begin_of(row):
        segment = jnp.sum((row[:, None] >= ends[None, :]).astype(jnp.int32), axis=1)
        member = segment[:, None] == jnp.arange(ends.shape[0], dtype=jnp.int32)[None, :]
        return jnp.sum(jnp.where(member, (ends - seq_lengths[0])[None, :], 0), axis=1)

    tile_rows = jnp.arange(tiles_all, dtype=jnp.int32) * rows
    tile_begin = begin_of(tile_rows)
    lane = jnp.arange(LANES, dtype=jnp.int32) % (HEAD_DIM // 2)
    freq = 10000.0 ** (-lane.astype(F32) * 2.0 / HEAD_DIM)
    near_angle = jnp.arange(rows, dtype=F32)[:, None] * freq[None, :]
    far_angle = (tile_rows - tile_begin).astype(F32)[:, None] * freq[None, :]
    near = jnp.stack([jnp.cos(near_angle), jnp.sin(near_angle)])
    far = jnp.stack([jnp.cos(far_angle), jnp.sin(far_angle)])
    gains = qk_scale[None, :]
    rates = eigen_rates.T

    q, k, v, q_rot, k_rot = project(x_rows, qkv_weight, gains, near, far)
    weights = [
        (up_gate_weight, down_weight),
        (exchange(up_gate_weight, "head", core_swap), exchange(down_weight, "head", core_swap)),
    ]
    scales = jnp.concatenate([mlp_scale, exchange(mlp_scale, "head", core_swap)], axis=1)

    def from_partner(send, keep, size):
        got = exchange(send, "head", core_swap)
        if ranks == 1:
            return keep[:size], [keep, got]
        away = (keep[:-size].astype(F32) + got[:-size].astype(F32)).astype(BF16)
        return away, [keep, got] + from_ranks(away, size)

    def from_ranks(away, size):
        return [
            exchange(away[n * size : (n + 1) * size], "head", shift_down[s])
            for n, s in enumerate(far_steps)
        ]

    def gather_ranks(own):
        return [exchange(own, "head", shift_up[s]) for s in far_steps] + [own]

    def gather_shares(own):
        mine = gather_ranks(own)
        return [exchange(b, "head", core_swap) for b in mine] + mine

    places = [(here * CHUNKS + j).astype(jnp.int32)[None] for j in range(CHUNKS)]
    tiles = [shares * CHUNKS + j for j in range(CHUNKS)]
    starts = [begin_of(t * rows) for t in tiles]
    chunks = range(CHUNKS)
    tile = 2 * BLOCK

    attn_out, lse, parts = [], [], []
    last = ()
    for j in chunks:
        half = heads // 2
        first = attend(
            q, k, v, out_weight, tiles[j][:half], starts[j][:half], rows, 0, heads, last
        )
        second = attend(
            q,
            k,
            v,
            out_weight,
            tiles[j][half:],
            starts[j][half:],
            rows,
            half,
            heads,
            (first[0], first[1]),
            2,
        )
        away, got = from_partner(first[2], second[2], rows)
        attn_out.append(second[0])
        lse.append(second[1])
        parts.append(got)
        last = (away,)
    joined = []
    for j in chunks:
        joined.append(join_attention(parts[j], x_rows, places[j], rates, rows, last))
        last = (joined[j][0],)
    hidden = [gather_ranks(joined[j][0]) for j in chunks]
    ffn = []
    for j in chunks:
        ffn.append(mlp(hidden[j], weights, scales, tile, last))
        last = (ffn[j][4],)
    ends_fwd = []
    for j in chunks:
        parts = [ffn[j][4]] + from_ranks(ffn[j][3], rows)
        ends_fwd.append(
            join_mlp(parts, joined[j][1], cotangent[0], j, rates, rows, last)
        )
        last = (ends_fwd[j][1],)
    d_rows = [gather_ranks(ends_fwd[j][1]) for j in chunks]
    back = []
    for j in chunks:
        back.append(mlp_back(d_rows[j], ffn[j][0], ffn[j][1], weights, scales, tile, last))
        last = (back[j][4],)

    row_blocks = width // BLOCK
    piece = BLOCK // owners
    across = ranks
    levels = owners // across
    z_here, x_here = lax.axis_index("batch") // across, lax.axis_index("batch") % across
    direct = levels if piece % 16 == 0 and across == 2 else 0
    x_place = x_here.astype(jnp.int32)[None]
    left_hidden = [b for h in hidden for b in h]
    left_down = [b for d in d_rows for b in d]
    rights = {
        "down": (left_down, [[f[2] for f in ffn]]),
        "up_gate": (left_hidden, [[b[0] for b in back], [b[1] for b in back]]),
    }

    def partner_part(name, after):
        out = outer(*rights[name], 1, 2, tile, after=after)[0]
        return out, exchange(out, "head", core_swap)

    def own_part(name, more, after):
        return outer(
            *rights[name],
            0,
            2,
            tile,
            more=(more,),
            place=x_place,
            levels=direct,
            after=after,
            cost=COST if name == "down" else SHORT,
        )

    def as_pieces(matrix):
        panels = matrix.shape[1] // BLOCK
        return (
            matrix.reshape(row_blocks, levels, across, piece, panels, BLOCK)
            .transpose(1, 2, 4, 0, 3, 5)
            .reshape(levels, across, panels * row_blocks * piece, BLOCK)
        )

    def from_this_x(pieces):
        return [
            lax.dynamic_index_in_dim(pieces, (x_here + s) % across, 1, keepdims=False)
            for s in range(across)
        ]

    def hold(value, anchor):
        return value if anchor is None else lax.optimization_barrier((value, anchor))[0]

    x_step = lambda s: [
        (i, i // across * across + (i % across + s) % across) for i in range(owners)
    ]
    z_step = lambda s: [
        (i, (i // across + s) % levels * across + i % across) for i in range(owners)
    ]
    z_place = z_here.astype(jnp.int32)[None]

    def over_z(parts):
        return [parts[0]] + [
            exchange(parts[s], "batch", z_step(s)) for s in range(1, levels)
        ]

    def plain_x(pieces):
        total = pieces[0].astype(F32)
        for s in range(1, across):
            total = total + exchange(pieces[s], "batch", x_step(s)).astype(F32)
        total = total.astype(BF16)
        return [
            lax.dynamic_index_in_dim(total, (z_here + s) % levels, 0, keepdims=False)
            for s in range(levels)
        ]

    def start_x(outs):
        if direct:
            mine, other = [flat(o) for o in outs]
            return mine, exchange(other, "batch", x_step(1))
        return from_this_x(as_pieces(outs[0]))

    def finish_x(started, after):
        if direct:
            sums = join_x(started, z_place, after)
        else:
            sums = plain_x([jnp.concatenate(p, axis=1) for p in zip(*started, strict=True)])
        return over_z(sums)

    split = []
    partner = {}
    for j in chunks:
        parts = [back[j][4]] + from_ranks(back[j][3], rows)
        split.append(
            split_attention(
                parts,
                ends_fwd[j][2],
                joined[j][1],
                joined[j][2],
                x_rows,
                places[j],
                rates,
                rows,
                last,
            )
        )
        last = (split[j][0],)
        if j == 0:
            out, partner["down"] = partner_part("down", last)
            last = (out,)
    out, partner["up_gate"] = partner_part("up_gate", last)
    last = (out,)
    d_attn_mine = [gather_ranks(split[j][0]) for j in chunks]
    flat = lambda a: a.reshape(a.shape[:-3] + (-1, BLOCK))
    started = {}
    for name, gathered in (("down", d_attn_mine[0]), ("up_gate", d_attn_mine[-1])):
        outs = own_part(name, partner[name], last + tuple(gathered[:-1]))
        last = (outs[0],)
        started[name] = start_x(outs)
        turn = outs[0] if name == "down" else turn
    d_attn_rows = [
        [exchange(hold(b, turn), "head", core_swap) for b in mine] + mine
        for mine in d_attn_mine
    ]
    outs = outer(
        [b for d in d_attn_rows for b in d],
        [attn_out],
        0,
        1,
        tile,
        place=x_place,
        levels=direct,
        after=last,
        cost=SHORT,
    )
    last = (outs[0],)
    started["out"] = start_x(outs)
    order = jnp.concatenate(tiles)
    order_starts = jnp.concatenate(starts)
    moved = {}
    pairs_all = cols // LANES
    raws, gain_parts, late = [], [], []
    marks = []
    for pair in range(pairs_all):
        pair_back = attend_back(
            [b for d in d_attn_rows for b in d],
            q,
            k,
            v,
            attn_out,
            lse,
            out_weight,
            order,
            order_starts,
            rows,
            pair,
            last,
        )
        last = (pair_back[0],)
        marks.append(last[0])
        if pair == 0:
            moved["down_out"] = finish_x([started["down"], started["out"]], last)
            last = (moved["down_out"][0],)
        raw, gain_part, *outs = project_back(
            x_rows,
            q_rot,
            k_rot,
            gains,
            near,
            far,
            pair_back,
            order,
            rows,
            pair,
            x_place,
            direct,
            last,
        )
        last = (raw,)
        raws.append(raw)
        gain_parts.append(gain_part)
        late.append(start_x(outs))
        if pair == 0:
            last = last + tuple(moved["down_out"][1:])
            moved["up_gate"] = finish_x([started["up_gate"]], last)
            last = (moved["up_gate"][0],)
    arrived = moved["up_gate"][1:] + [a for pieces in late[:-1] for a in pieces[1:]]
    send, keep = input_back(raws, qkv_weight, shares, share, last + tuple(arrived))
    gain_grad = jnp.concatenate(gain_parts, axis=1)
    moved["late"] = finish_x(late, (keep,))

    def double(value, axis, size, anchors=()):
        step = 1
        turn = 0
        while step < size:
            got = exchange(value, axis, [(i, i ^ step) for i in range(size)])
            value = value + hold(got, anchors[turn] if turn < len(anchors) else None)
            step *= 2
            turn += 1
        return value

    rate_grad = double(
        jnp.concatenate([sum(s[2] for s in split), sum(e[3] for e in ends_fwd)], axis=0),
        "head",
        heads,
        marks,
    )
    both = sum(b[2] for b in back)
    scale_cols = mlp_scale.shape[1]
    scale_grad = both[:, :scale_cols] + exchange(both[:, scale_cols:], "head", core_swap)

    slot_order = block_order[0]
    panel, rest = slot_order // row_blocks, slot_order % row_blocks
    late_panels = 3 * pairs_all
    panels = slot_order.shape[0] // row_blocks
    down_panels = scale_cols // BLOCK
    late_panel = panel % pairs_all * 3 + panel // pairs_all
    down_panel = panel - (panels - down_panels) + late_panels
    held_panel = jnp.where(panel >= panels - down_panels, down_panel, panel + down_panels)
    place_of = jnp.where(panel < late_panels, late_panel, held_panel) * row_blocks + rest
    groups = [moved[n] for n in ("late", "down_out", "up_gate")]
    if direct:
        ordered = order_pieces(groups, place_of, piece, ())
    else:
        sums = [sum(a.astype(F32) for a in g).astype(BF16) for g in groups]
        pieces = jnp.concatenate(sums, axis=0).reshape(-1, piece, BLOCK)
        ordered = jnp.take(pieces, place_of, axis=0, mode="clip")
    got = exchange(send, "head", core_swap)
    parts = [keep, got]
    last = (ordered,)
    if ranks > 1:
        away = join_partner(keep, got, share, last)
        last = (away,)
        parts += from_ranks(away, share)
    per_owner = slot_order.shape[0] // owners
    owned = lax.all_to_all(
        ordered.reshape(owners, per_owner, piece, BLOCK),
        "batch",
        split_axis=0,
        concat_axis=0,
        tiled=True,
    )
    slots = min(8, per_owner)
    if piece % 16:
        owned = owned.transpose(1, 0, 2, 3).reshape(1, per_owner, BLOCK, BLOCK)
    g_spec = pl.BlockSpec(
        (owned.shape[0], slots) + owned.shape[2:], lambda i: (0, i, 0, 0)
    )
    blk = pl.BlockSpec((slots, BLOCK, BLOCK), lambda i: (i, 0, 0))
    row = pl.BlockSpec((slots, BLOCK), lambda i: (i, 0))
    cube = jax.ShapeDtypeStruct((per_owner, BLOCK, BLOCK), F32)
    grid = (per_owner // slots,)
    owned_grad, stepped, column_sq = launch(
        step_kernel,
        "step",
        grid,
        [(owned, g_spec), (left_root[0], blk), (right_root[0], blk), (master_blocks[0], blk)],
        [(cube, blk), (cube, blk), (like((per_owner, BLOCK), F32), row)],
        after=last,
    )
    new_left, new_right = launch(
        stats_kernel,
        "stats",
        grid,
        [(owned, g_spec), (left_stats[0], blk), (right_stats[0], blk)],
        [(cube, blk), (cube, blk)],
        after=(column_sq,),
    )
    my_blocks = lax.dynamic_slice_in_dim(
        slot_order, lax.axis_index("batch") * per_owner, per_owner, 0
    )
    member = (
        (my_blocks // row_blocks)[:, None] == jnp.arange(panels, dtype=jnp.int32)[None, :]
    ).astype(F32)
    precise = lax.Precision.HIGHEST
    sums = jnp.concatenate(
        [jnp.einsum("sp,sb->pb", member, column_sq, precision=precise)]
        + [a.reshape(-1, LANES) for a in (gain_grad, rate_grad, scale_grad)],
        axis=0,
    )
    d_input = sum_input(parts, [s[1] for s in split], rows, (new_left,))
    sums = double(sums, "batch", owners, (new_left, d_input))
    totals = sums[:panels]
    small = sums[panels:].reshape(-1)
    gain_sum = small[:cols]
    rate_sum = small[cols : cols + 2 * width].reshape(2, width)
    scale_sum = small[cols + 2 * width :].reshape(mlp_scale.shape)
    norms = jnp.einsum("sp,pb->sb", member, totals, precision=precise)
    new_master, new_ema = pl.pallas_call(
        finish_kernel,
        grid=grid,
        in_specs=[blk, blk, row],
        out_specs=[blk, blk],
        out_shape=[cube, cube],
        name="finish",
    )(stepped, ema_blocks[0], norms)
    gain_step = 0.5 / math.sqrt(total * owners)
    width_share = width // heads
    rate_here = lax.dynamic_slice_in_dim(rate_sum, here * width_share, width_share, 1)
    rate_slice = lax.dynamic_slice_in_dim(rates, here * width_share, width_share, 1)
    mlp_scale_out = jnp.stack([scale_sum, mlp_scale - gain_step * scale_sum])
    new_gains = jnp.concatenate(
        [(qk_scale - gain_step * gain_sum)[None, :], rate_slice - gain_step * rate_here], axis=0
    )
    out_share = jnp.concatenate([e[0] for e in ends_fwd], axis=0)
    return (
        out_share[None],
        d_input[None],
        owned_grad[None],
        new_master[None],
        new_ema[None],
        new_left[None],
        new_right[None],
        gain_sum,
        mlp_scale_out,
        rate_here.T,
        new_gains,
    )


def solution(mesh):
    return jax.shard_map(
        shards,
        mesh=mesh,
        in_specs=(
            P("batch", None, None),
            P("batch", None),
            P(None, None, "head"),
            P("head", None),
            P(None, None, "head"),
            P("head", None),
            P("head"),
            P(None, "head"),
            P(),
            P("batch", "head", None),
            P("head", None),
            P("head", "batch", None, None),
            P("head", "batch", None, None),
            P("head", "batch", None, None),
            P("head", "batch", None, None),
            P("head", "batch", None, None),
            P("head", "batch", None, None),
        ),
        out_specs=(
            P("batch", "head", None),
            P("batch", "head", None),
            P("head", "batch", None, None),
            P("head", "batch", None, None),
            P("head", "batch", None, None),
            P("head", "batch", None, None),
            P("head", "batch", None, None),
            P("head"),
            P(None, None, "head"),
            P("head", None),
            P(None, "head"),
        ),
        check_vma=False,
    )
```

```python
import functools
import math

import jax
import jax.numpy as jnp
from jax import lax
from jax.experimental import pallas as pl
from jax.experimental.pallas import tpu as pltpu
from jax.sharding import PartitionSpec as P

HEAD_DIM = 64
BLOCK = 128
LANES = 128
CHUNKS = 2
F32 = jnp.float32
BF16 = jnp.bfloat16
NN = (((1,), (0,)), ((), ()))
NT = (((1,), (1,)), ((), ()))
TN = (((0,), (0,)), ((), ()))
COST = pl.CostEstimate(flops=10**11, transcendentals=0, bytes_accessed=10**7)
TINY = pl.CostEstimate(flops=10**9, transcendentals=0, bytes_accessed=10**7)
SHORT = pl.CostEstimate(flops=10**10, transcendentals=0, bytes_accessed=10**7)


def mm(a, b, dims=NN):
    return lax.dot_general(a, b, dims, preferred_element_type=F32)


def whole(shape, single=False):
    zeros = (0,) * len(shape)
    if single:
        return pl.BlockSpec(shape, lambda *_: zeros, pipeline_mode=pl.Buffered(1))
    return pl.BlockSpec(shape, lambda *_: zeros)


def launch(kernel, name, grid, ins, outs, scratch=(), prefetch=(), after=(), alias=0, cost=COST):
    first, count, extra = len(prefetch), len(ins), len(after)

    def body(*refs):
        kernel(*refs[: first + count], *refs[first + count + extra :])

    return pl.pallas_call(
        body,
        grid_spec=pltpu.PrefetchScalarGridSpec(
            num_scalar_prefetch=first,
            grid=grid,
            in_specs=[s for _, s in ins] + [pl.BlockSpec(memory_space=pl.ANY)] * extra,
            out_specs=[s for _, s in outs],
            scratch_shapes=list(scratch),
        ),
        out_shape=[o for o, _ in outs],
        input_output_aliases={first + count + n: n for n in range(alias)},
        name=name,
        cost_estimate=cost,
    )(*prefetch, *[a for a, _ in ins], *after)


def like(shape, dtype):
    return jax.ShapeDtypeStruct(shape, dtype)


def rms_rows(value):
    return value * lax.rsqrt(jnp.mean(value * value, axis=-1, keepdims=True) + 1e-06)


def rms_factor(value):
    return lax.rsqrt(jnp.mean(value * value, axis=-1, keepdims=True) + 1e-06)


def rms_back(normed, factor, gradient):
    return factor * (gradient - normed * jnp.mean(gradient * normed, axis=-1, keepdims=True))


def lane_ids():
    return lax.broadcasted_iota(jnp.int32, (1, LANES), 1)


def head_mean(value, ones_block):
    high = value.astype(BF16)
    rest = (value - high.astype(F32)).astype(BF16)
    return (mm(high, ones_block) + mm(rest, ones_block)) * (1.0 / HEAD_DIM)


def ones_block():
    row = lax.broadcasted_iota(jnp.int32, (LANES, LANES), 0) // HEAD_DIM
    col = lax.broadcasted_iota(jnp.int32, (LANES, LANES), 1) // HEAD_DIM
    return jnp.where(row == col, 1.0, 0.0).astype(BF16)


def half_turn(value):
    first = (lane_ids() & (HEAD_DIM - 1)) < HEAD_DIM // 2
    return jnp.where(
        first,
        pltpu.roll(value, LANES - HEAD_DIM // 2, 1),
        pltpu.roll(value, HEAD_DIM // 2, 1),
    )


def angles(tile, near_ref, far_ref):
    cos_r, sin_r = near_ref[0], near_ref[1]
    cos_0 = far_ref[0, pl.ds(tile, 1), :]
    sin_0 = far_ref[1, pl.ds(tile, 1), :]
    first = (lane_ids() & (HEAD_DIM - 1)) < HEAD_DIM // 2
    sine = sin_0 * cos_r + cos_0 * sin_r
    return cos_0 * cos_r - sin_0 * sin_r, jnp.where(first, -sine, sine)


def project_kernel(
    x_ref, w_ref, gain_ref, near_ref, far_ref, q_ref, k_ref, v_ref, q_rot_ref, k_rot_ref
):
    tile = pl.program_id(0)
    cosine, sine = angles(tile, near_ref, far_ref)
    ones = ones_block()
    x = x_ref[...]
    for index, used_ref, rot_ref in ((0, q_ref, q_rot_ref), (1, k_ref, k_rot_ref)):
        raw = mm(x, w_ref[index])
        for pair in range(raw.shape[1] // LANES):
            lanes = slice(pair * LANES, (pair + 1) * LANES)
            value = raw[:, lanes]
            turned = value * cosine + half_turn(value) * sine
            factor = lax.rsqrt(head_mean(turned * turned, ones) + 1e-06)
            rot_ref[:, lanes] = turned
            used_ref[:, lanes] = (turned * factor * gain_ref[:, lanes]).astype(BF16)
    v_ref[...] = mm(x, w_ref[2]).astype(BF16)


def project(x, weight, gains, near, far):
    rows, width = x.shape
    cols = weight.shape[2]
    tile = near.shape[1]
    by_row = lambda w: pl.BlockSpec((tile, w), lambda i: (i, 0))
    return pl.pallas_call(
        project_kernel,
        grid=(rows // tile,),
        in_specs=[
            by_row(width),
            whole(weight.shape, True),
            whole((1, cols)),
            whole(near.shape),
            whole(far.shape),
        ],
        out_specs=[by_row(cols)] * 5,
        out_shape=[jax.ShapeDtypeStruct((rows, cols), BF16)] * 3
        + [jax.ShapeDtypeStruct((rows, cols), F32)] * 2,
        name="project",
        cost_estimate=COST,
    )(x, weight, gains, near, far)


def key_tiles(first_row, start, wide, narrow, visit):
    full = first_row // wide

    def step(index, carry):
        visit(pl.multiple_of(index * wide, wide), wide, False)
        return carry

    lax.fori_loop(start // wide, full, step, 0)
    diagonal = (first_row // narrow) * narrow

    @pl.when(diagonal > full * wide)
    def _():
        visit(pl.multiple_of(full * wide, narrow), narrow, False)

    visit(pl.multiple_of(diagonal, narrow), narrow, True)


def attend_kernel(
    wide, tiles, starts, q_ref, k_ref, v_ref, w_ref, o_ref, lse_ref, part_ref, acc, mixed
):
    index = pl.program_id(0)
    rows = q_ref.shape[0]
    first_row = tiles[index] * rows
    start = starts[index]
    narrow = wide // 2
    low = lane_ids() < HEAD_DIM
    zero = jnp.zeros((), BF16)

    def one_pair(pair, carry):
        lanes = pl.ds(pl.multiple_of(pair * LANES, LANES), LANES)
        q = q_ref[:, lanes] * jnp.asarray(1.0 / math.sqrt(HEAD_DIM), BF16)
        q_both = jnp.concatenate([jnp.where(low, q, zero), jnp.where(low, zero, q)], axis=0)
        acc[...] = jnp.zeros_like(acc)

        def visit(key_0, size, masked):
            keys = pl.ds(key_0, size)
            weights = jnp.exp(mm(q_both, k_ref[keys, lanes], NT))
            if masked:
                row = lax.broadcasted_iota(jnp.int32, (2 * rows, size), 0)
                row = jnp.where(row < rows, row, row - rows) + first_row
                col = lax.broadcasted_iota(jnp.int32, (2 * rows, size), 1) + key_0
                weights = jnp.where((col <= row) & (col >= start), weights, 0.0)
            total = weights[:, :LANES]
            for part in range(1, size // LANES):
                total = total + weights[:, part * LANES : (part + 1) * LANES]
            acc[:, LANES:] += total
            acc[:, :LANES] += mm(weights.astype(BF16), v_ref[keys, lanes])

        key_tiles(first_row, start, wide, narrow, visit)
        total_a = jnp.sum(acc[:rows, LANES:], axis=1, keepdims=True)
        total_b = jnp.sum(acc[rows:, LANES:], axis=1, keepdims=True)
        summed = jnp.where(low, acc[:rows, :LANES], acc[rows:, :LANES])
        out = (summed / jnp.where(low, total_a, total_b)).astype(BF16)
        o_ref[:, lanes] = out
        lse_ref[:, lanes] = jnp.log(jnp.where(low, total_b, total_a))
        mixed[:, lanes] = out
        return carry

    lax.fori_loop(0, q_ref.shape[1] // LANES, one_pair, 0)
    part_ref[...] = mm(mixed[...], w_ref[...]).astype(BF16)


def attend(q, k, v, weight, tiles, starts, rows, offset, places, after, alias=0):
    count = tiles.shape[0]
    cols = k.shape[1]
    width = weight.shape[1]
    at_place = pl.BlockSpec((rows, cols), lambda i, t, s: (i + offset, 0))
    return launch(
        functools.partial(attend_kernel, 4 * BLOCK),
        "attend",
        (count,),
        [
            (q, pl.BlockSpec((rows, cols), lambda i, t, s: (t[i], 0))),
            (k, whole(k.shape, True)),
            (v, whole(v.shape, True)),
            (weight, whole(weight.shape, True)),
        ],
        [
            (like((places * rows, cols), BF16), at_place),
            (like((places * rows, cols), F32), at_place),
            (like((count * rows, width), BF16), pl.BlockSpec((rows, width), lambda i, t, s: (i, 0))),
        ],
        scratch=[pltpu.VMEM((2 * rows, 2 * LANES), F32), pltpu.VMEM((rows, cols), BF16)],
        prefetch=(tiles, starts),
        after=after,
        alias=alias,
    )


def attend_back_kernel(blocks, wide, tiles, starts, *refs):
    row_refs = refs[:blocks]
    q_ref, k_ref, v_ref = refs[blocks : blocks + 3]
    o_refs = refs[blocks + 3 : blocks + 3 + CHUNKS]
    lse_refs = refs[blocks + 3 + CHUNKS : blocks + 3 + 2 * CHUNKS]
    w_ref, dq_ref, dk_ref, dv_ref, rows_s, o_ref, lse_ref, acc = refs[blocks + 3 + 2 * CHUNKS :]
    index = pl.program_id(0)
    rows = q_ref.shape[0]
    narrow = wide // 2

    @pl.when(index == 0)
    def _():
        dk_ref[...] = jnp.zeros_like(dk_ref)
        dv_ref[...] = jnp.zeros_like(dv_ref)

    for block in range(blocks):

        @pl.when(index == block)
        def _(block=block):
            rows_s[...] = row_refs[block][...]

    for chunk in range(CHUNKS):

        @pl.when(index // (blocks // CHUNKS) == chunk)
        def _(chunk=chunk):
            o_ref[...] = o_refs[chunk][...]
            lse_ref[...] = lse_refs[chunk][...]

    first_row = tiles[index] * rows
    start = starts[index]
    low = lane_ids() < HEAD_DIM
    place = lane_ids() & (HEAD_DIM - 1)
    zero = jnp.zeros((), BF16)
    ones = jnp.where(place < 3, 1.0, 0.0).astype(BF16)

    def parts(value):
        high = value.astype(BF16).astype(F32)
        rest = value - high
        middle = rest.astype(BF16).astype(F32)
        picked = jnp.where(place == 1, middle, jnp.where(place == 2, rest - middle, 0.0))
        return jnp.where(place == 0, high, picked).astype(BF16)

    d_rows = rows_s[...]
    d_attn = mm(d_rows, w_ref[...], NT).astype(BF16)
    for pair in range(q_ref.shape[1] // LANES):
        lanes = slice(pair * LANES, (pair + 1) * LANES)
        q = q_ref[:, lanes] * jnp.asarray(1.0 / math.sqrt(HEAD_DIM), BF16)
        d_out = d_attn[:, lanes]
        minus_lse = parts(-lse_ref[:, lanes])
        product = d_out.astype(F32) * o_ref[:, lanes].astype(F32)
        sum_a = jnp.sum(jnp.where(low, product, 0.0), axis=1, keepdims=True)
        sum_b = jnp.sum(jnp.where(low, 0.0, product), axis=1, keepdims=True)
        minus_delta = parts(-jnp.where(low, sum_b, sum_a))
        q_ext = (jnp.where(low, q, minus_lse), jnp.where(low, minus_lse, q))
        d_ext = (jnp.where(low, d_out, minus_delta), jnp.where(low, minus_delta, d_out))
        q_both = jnp.concatenate([jnp.where(low, q, zero), jnp.where(low, zero, q)], axis=0)
        d_both = jnp.concatenate(
            [jnp.where(low, d_out, zero), jnp.where(low, zero, d_out)], axis=0
        )
        acc[...] = jnp.zeros_like(acc)

        def visit(key_0, size, masked):
            keys = pl.ds(key_0, size)
            k = k_ref[keys, lanes]
            v = v_ref[keys, lanes]
            k_ext = (jnp.where(low, k, ones), jnp.where(low, ones, k))
            v_ext = (jnp.where(low, v, ones), jnp.where(low, ones, v))
            if masked:
                col = lax.broadcasted_iota(jnp.int32, (size, rows), 1) + first_row
                row = lax.broadcasted_iota(jnp.int32, (size, rows), 0) + key_0
                allowed = (row <= col) & (row >= start)
            probs = []
            d_scores = []
            for head in range(2):
                prob = jnp.exp(mm(k_ext[head], q_ext[head], NT))
                if masked:
                    prob = jnp.where(allowed, prob, 0.0)
                d_score = prob * mm(v_ext[head], d_ext[head], NT)
                probs.append(prob.astype(BF16))
                d_scores.append(d_score.astype(BF16))
            dv_ref[keys, lanes] += mm(jnp.concatenate(probs, axis=1), d_both)
            dk_ref[keys, lanes] += mm(jnp.concatenate(d_scores, axis=1), q_both)
            k_both = jnp.concatenate([jnp.where(low, k, zero), jnp.where(low, zero, k)], axis=0)
            acc[...] += mm(jnp.concatenate(d_scores, axis=0), k_both, TN)

        key_tiles(first_row, start, wide, narrow, visit)
        dq_ref[:, lanes] = acc[...] * (1.0 / math.sqrt(HEAD_DIM))


def attend_back(row_blocks, q, k, v, outs, lses, weight, tiles, starts, rows, pair, after):
    count = tiles.shape[0]
    total = k.shape[0]
    width = weight.shape[1]
    at_tile = pl.BlockSpec((rows, LANES), lambda i, t, s: (t[i], pair))
    each = count // CHUNKS

    def at_step(chunk):
        return pl.BlockSpec(
            (rows, LANES), lambda i, t, s: (jnp.clip(i - chunk * each, 0, each - 1), pair)
        )

    column = pl.BlockSpec((total, LANES), lambda *_: (0, pair), pipeline_mode=pl.Buffered(1))
    return launch(
        functools.partial(attend_back_kernel, len(row_blocks), 4 * BLOCK),
        "attend_back",
        (count,),
        [(b, whole(b.shape, True)) for b in row_blocks]
        + [
            (q, at_tile),
            (k, column),
            (v, column),
        ]
        + [(a, at_step(n)) for n, a in enumerate(outs)]
        + [(a, at_step(n)) for n, a in enumerate(lses)]
        + [
            (weight, pl.BlockSpec((LANES, width), lambda *_: (pair, 0))),
        ],
        [
            (like((count * rows, LANES), F32), pl.BlockSpec((rows, LANES), lambda i, *_: (i, 0))),
            (like((total, LANES), F32), whole((total, LANES))),
            (like((total, LANES), F32), whole((total, LANES))),
        ],
        scratch=[
            pltpu.VMEM((rows, width), BF16),
            pltpu.VMEM((rows, LANES), BF16),
            pltpu.VMEM((rows, LANES), F32),
            pltpu.VMEM((rows, LANES), F32),
        ],
        prefetch=(tiles, starts),
        after=after,
        cost=SHORT,
    )


def sum_parts(refs):
    total = refs[0][...].astype(F32)
    for ref in refs[1:]:
        total = total + ref[...].astype(F32)
    return total


def join_attention_kernel(parts, place, *refs):
    x_ref, rate_ref = refs[parts : parts + 2]
    low_ref, hidden_ref, branch_ref = refs[parts + 2 :]
    branch = sum_parts(refs[:parts])
    x = x_ref[...].astype(F32)
    hidden = rms_rows(x + rate_ref[0:1] * (rms_rows(branch) - x))
    branch_ref[...] = branch
    hidden_ref[...] = hidden
    low_ref[...] = hidden.astype(BF16)


def part_specs(parts, rows, width):
    return [
        pl.BlockSpec((rows, width), lambda i, *_, last=a.shape[0] // rows: (last - SUB + i, 0))
        for a in parts
    ]


SUB = 2


def join_attention(parts, x, place, rates, share, after):
    width = x.shape[1]
    rows = share // SUB
    here = pl.BlockSpec((rows, width), lambda i, p: (i, 0))
    return launch(
        functools.partial(join_attention_kernel, len(parts)),
        "join_attention",
        (SUB,),
        list(zip(parts, part_specs(parts, rows, width), strict=True))
        + [
            (x, pl.BlockSpec((rows, width), lambda i, p: (p[0] * SUB + i, 0))),
            (rates, whole(rates.shape)),
        ],
        [(like((share, width), d), here) for d in (BF16, F32, F32)],
        prefetch=(place,),
        after=after,
    )


def weight_tiles(weight, down, step, side):
    _, width, cols = weight.shape
    count = cols // step
    if side == 0:
        at = lambda t: jnp.minimum(t, count - 1)
    else:
        at = lambda t: jnp.maximum(t - count, 0)
    return [
        (weight, pl.BlockSpec((2, width, step), lambda t, *_: (0, 0, at(t)))),
        (down, pl.BlockSpec((step, width), lambda t, *_: (at(t), 0))),
    ]


def mlp_kernel(blocks, *refs):
    row_refs = refs[:blocks]
    sides = (refs[blocks : blocks + 2], refs[blocks + 2 : blocks + 4])
    scale_ref = refs[blocks + 4]
    up_ref, gate_ref, mixed_ref, away_ref, own_ref, x_s, acc = refs[blocks + 5 :]
    tile = pl.program_id(0)
    count = pl.num_programs(0)
    rows = row_refs[0].shape[0]

    @pl.when(tile == 0)
    def _():
        for block in range(blocks):
            x_s[block * rows : (block + 1) * rows] = row_refs[block][...]
        acc[...] = jnp.zeros_like(acc)

    def run(w_ref, down_ref):
        x = x_s[...]
        up = mm(x, w_ref[0])
        gate = mm(x, w_ref[1])
        up_ref[...] = up.astype(BF16)
        gate_ref[...] = gate.astype(BF16)
        scaled = gate * scale_ref[1:2]
        mixed = (up * scale_ref[0:1] * (scaled * jax.nn.sigmoid(scaled))).astype(BF16)
        mixed_ref[...] = mixed
        acc[...] += mm(mixed, down_ref[...])

    for side in range(2):

        @pl.when(tile // (count // 2) == side)
        def _(side=side):
            run(*sides[side])

    @pl.when(tile == count - 1)
    def _():
        last = (blocks - 1) * rows
        own_ref[...] = acc[last:]
        if blocks > 1:
            away_ref[...] = acc[:last].astype(BF16)


def mlp(row_blocks, weights, scales, step, after):
    rows, width = row_blocks[0].shape
    blocks = len(row_blocks)
    height = rows * blocks
    cols = 2 * weights[0][0].shape[2]
    at_tile = lambda h: pl.BlockSpec((h, step), lambda t: (0, t))
    far = max(blocks - 1, 1) * rows
    return launch(
        functools.partial(mlp_kernel, blocks),
        "mlp",
        (cols // step,),
        [(b, whole(b.shape, True)) for b in row_blocks]
        + weight_tiles(*weights[0], step, 0)
        + weight_tiles(*weights[1], step, 1)
        + [(scales, at_tile(2))],
        [(like((height, cols), BF16), at_tile(height))] * 3
        + [
            (like((far, width), BF16), whole((far, width))),
            (like((rows, width), F32), whole((rows, width))),
        ],
        scratch=[pltpu.VMEM((height, width), BF16), pltpu.VMEM((height, width), F32)],
        after=after,
    )


def join_mlp_kernel(parts, *refs):
    hidden_ref, cot_ref, rate_ref = refs[parts : parts + 3]
    out_ref, low_ref, d_hidden_ref, rate_grad_ref = refs[parts + 3 :]
    branch = sum_parts(refs[:parts])
    hidden = hidden_ref[...]
    rate = rate_ref[1:2]
    factor = rms_factor(branch)
    normed = branch * factor
    gap = normed - hidden
    before = hidden + rate * gap
    factor_out = rms_factor(before)
    out = before * factor_out
    d_before = rms_back(out, factor_out, cot_ref[...].astype(F32))
    out_ref[...] = out
    d_hidden_ref[...] = (1.0 - rate) * d_before
    low_ref[...] = rms_back(normed, factor, rate * d_before).astype(BF16)

    @pl.when(pl.program_id(0) == 0)
    def _():
        rate_grad_ref[...] = jnp.zeros_like(rate_grad_ref)

    rate_grad_ref[...] += jnp.sum(d_before * gap, axis=0, keepdims=True)


def join_mlp(parts, hidden, cotangent, chunk, rates, share, after):
    width = hidden.shape[1]
    rows = share // SUB
    here = pl.BlockSpec((rows, width), lambda i: (i, 0))
    return launch(
        functools.partial(join_mlp_kernel, len(parts)),
        "join_mlp",
        (SUB,),
        list(zip(parts, part_specs(parts, rows, width), strict=True))
        + [
            (hidden, here),
            (cotangent, pl.BlockSpec((rows, width), lambda i: (chunk * SUB + i, 0))),
            (rates, whole(rates.shape)),
        ],
        [(like((share, width), d), here) for d in (F32, BF16, F32)]
        + [(like((1, width), F32), whole((1, width)))],
        after=after,
    )


def mlp_back_kernel(blocks, *refs):
    row_refs = refs[:blocks]
    sides = (refs[blocks : blocks + 2], refs[blocks + 2 : blocks + 4])
    scale_ref, up_ref, gate_ref = refs[blocks + 4 : blocks + 7]
    d_up_ref, d_gate_ref, sums_ref, away_ref, own_ref, x_s, acc = refs[blocks + 7 :]
    tile = pl.program_id(0)
    count = pl.num_programs(0)
    rows = row_refs[0].shape[0]

    @pl.when(tile == 0)
    def _():
        for block in range(blocks):
            x_s[block * rows : (block + 1) * rows] = row_refs[block][...]
        acc[...] = jnp.zeros_like(acc)

    def run(w_ref, down_ref):
        d_mixed = mm(x_s[...], down_ref[...], NT)
        up_raw = up_ref[...].astype(F32)
        gate_raw = gate_ref[...].astype(F32)
        scale_up = scale_ref[0:1]
        scale_gate = scale_ref[1:2]
        gate = gate_raw * scale_gate
        sig = jax.nn.sigmoid(gate)
        d_up = d_mixed * (gate * sig)
        d_gate = d_mixed * (up_raw * scale_up) * (sig * (1.0 + gate * (1.0 - sig)))
        sums_ref[0:1] = jnp.sum(d_up * up_raw, axis=0, keepdims=True)
        sums_ref[1:2] = jnp.sum(d_gate * gate_raw, axis=0, keepdims=True)
        d_up = (d_up * scale_up).astype(BF16)
        d_gate = (d_gate * scale_gate).astype(BF16)
        d_up_ref[...] = d_up
        d_gate_ref[...] = d_gate
        acc[...] += mm(d_up, w_ref[0], NT) + mm(d_gate, w_ref[1], NT)

    for side in range(2):

        @pl.when(tile // (count // 2) == side)
        def _(side=side):
            run(*sides[side])

    @pl.when(tile == count - 1)
    def _():
        last = (blocks - 1) * rows
        own_ref[...] = acc[last:]
        if blocks > 1:
            away_ref[...] = acc[:last].astype(BF16)


def mlp_back(row_blocks, up, gate, weights, scales, step, after):
    rows, width = row_blocks[0].shape
    blocks = len(row_blocks)
    height = rows * blocks
    cols = 2 * weights[0][0].shape[2]
    at_tile = lambda h: pl.BlockSpec((h, step), lambda t: (0, t))
    far = max(blocks - 1, 1) * rows
    return launch(
        functools.partial(mlp_back_kernel, blocks),
        "mlp_back",
        (cols // step,),
        [(b, whole(b.shape, True)) for b in row_blocks]
        + weight_tiles(*weights[0], step, 0)
        + weight_tiles(*weights[1], step, 1)
        + [(scales, at_tile(2)), (up, at_tile(height)), (gate, at_tile(height))],
        [(like((height, cols), BF16), at_tile(height))] * 2
        + [
            (like((2, cols), F32), at_tile(2)),
            (like((far, width), BF16), whole((far, width))),
            (like((rows, width), F32), whole((rows, width))),
        ],
        scratch=[pltpu.VMEM((height, width), BF16), pltpu.VMEM((height, width), F32)],
        after=after,
    )


def split_attention_kernel(parts, place, *refs):
    d_hidden_ref, hidden_ref, branch_ref, x_ref, rate_ref = refs[parts : parts + 5]
    low_ref, d_input_ref, rate_grad_ref = refs[parts + 5 :]
    d_hidden = sum_parts(refs[:parts]) + d_hidden_ref[...]
    hidden = hidden_ref[...]
    branch = branch_ref[...]
    x = x_ref[...].astype(F32)
    rate = rate_ref[0:1]
    factor = rms_factor(branch)
    normed = branch * factor
    gap = normed - x
    d_before = rms_back(hidden, rms_factor(x + rate * gap), d_hidden)
    d_input_ref[...] = (1.0 - rate) * d_before
    low_ref[...] = rms_back(normed, factor, rate * d_before).astype(BF16)

    @pl.when(pl.program_id(0) == 0)
    def _():
        rate_grad_ref[...] = jnp.zeros_like(rate_grad_ref)

    rate_grad_ref[...] += jnp.sum(d_before * gap, axis=0, keepdims=True)


def split_attention(parts, d_hidden, hidden, branch, x, place, rates, share, after):
    width = x.shape[1]
    rows = share // SUB
    here = pl.BlockSpec((rows, width), lambda i, p: (i, 0))
    return launch(
        functools.partial(split_attention_kernel, len(parts)),
        "split_attention",
        (SUB,),
        list(zip(parts, part_specs(parts, rows, width), strict=True))
        + [(d_hidden, here), (hidden, here), (branch, here)]
        + [
            (x, pl.BlockSpec((rows, width), lambda i, p: (p[0] * SUB + i, 0))),
            (rates, whole(rates.shape)),
        ],
        [(like((share, width), d), here) for d in (BF16, F32)]
        + [(like((1, width), F32), whole((1, width)))],
        prefetch=(place,),
        after=after,
    )


def project_back_kernel(order, x_here, *refs):
    x_ref, q_rot_ref, k_rot_ref, gain_ref, near_ref, far_ref = refs[:6]
    d_refs = refs[6:9]
    raw_ref, gain_grad_ref = refs[9:11]
    grad_refs = refs[11:-2]
    acc, held = refs[-2:]
    index = pl.program_id(0)
    count = pl.num_programs(0)

    @pl.when(index == 0)
    def _():
        gain_grad_ref[...] = jnp.zeros_like(gain_grad_ref)
        acc[...] = jnp.zeros_like(acc)

    cosine, sine = angles(order[index], near_ref, far_ref)
    ones = ones_block()
    d_raw = []
    for which, rot_ref in ((0, q_rot_ref), (1, k_rot_ref)):
        d_used = d_refs[which][...]
        turned = rot_ref[...]
        factor = lax.rsqrt(head_mean(turned * turned, ones) + 1e-06)
        normed = turned * factor
        gain_grad_ref[...] += jnp.sum(d_used * normed, axis=0, keepdims=True)
        d_normed = d_used * gain_ref[...]
        d_turned = factor * (d_normed - normed * head_mean(d_normed * normed, ones))
        d_raw.append((d_turned * cosine - half_turn(d_turned) * sine).astype(BF16))
    d_raw.append(d_refs[2][...].astype(BF16))
    d_all = jnp.concatenate(d_raw, axis=1)
    raw_ref[...] = d_all
    acc[...] += mm(d_all, x_ref[...], TN)

    @pl.when(index == count - 1)
    def _():
        held[...] = acc[...].T.astype(BF16)
        if len(grad_refs) == 1:
            grad_refs[0][...] = held[...]
        else:
            store_pieces(held, x_here[0], *grad_refs)


def project_back(x, q_rot, k_rot, gains, near, far, parts, order, rows, pair, place, levels, after):
    total, width = x.shape
    count = order.shape[0]
    wide = 3 * LANES
    at_tile = lambda w, n: pl.BlockSpec((rows, w), lambda i, t, *_: (t[i], n))
    if levels:
        shape = (levels, 3 * (width // BLOCK), BLOCK // (2 * levels), BLOCK)
        grads = [(like(shape, BF16), whole(shape))] * 2
    else:
        grads = [(like((width, wide), BF16), whole((width, wide)))]
    return launch(
        project_back_kernel,
        "project_back",
        (count,),
        [
            (x, at_tile(width, 0)),
            (q_rot, at_tile(LANES, pair)),
            (k_rot, at_tile(LANES, pair)),
            (gains, pl.BlockSpec((1, LANES), lambda *_: (0, pair))),
            (near, whole(near.shape)),
            (far, whole(far.shape)),
        ]
        + [(parts[0], pl.BlockSpec((rows, LANES), lambda i, *_: (i, 0)))]
        + [(a, at_tile(LANES, 0)) for a in parts[1:]],
        [
            (like((total, wide), BF16), at_tile(wide, 0)),
            (like((1, LANES), F32), whole((1, LANES))),
        ]
        + grads,
        scratch=[pltpu.VMEM((wide, width), F32), pltpu.VMEM((width, wide), BF16)],
        prefetch=(order, place),
        after=after,
    )


def input_back_kernel(pairs, order, *refs):
    raw_refs = refs[:pairs]
    w_ref, send_ref, keep_ref = refs[pairs : pairs + 3]
    index = pl.program_id(0)
    count = pl.num_programs(0)
    d_x = None
    for which in range(3):
        lanes = slice(which * LANES, (which + 1) * LANES)
        d_all = jnp.concatenate([r[:, lanes] for r in raw_refs], axis=1)
        product = mm(d_all, w_ref[which], NT)
        d_x = product if d_x is None else d_x + product
    d_x = d_x.astype(BF16)

    @pl.when(index < count // 2)
    def _():
        send_ref[...] = d_x

    @pl.when(index >= count // 2)
    def _():
        keep_ref[...] = d_x


def input_back(raws, weight, order, rows, after):
    count = order.shape[0]
    half = count // 2
    width = weight.shape[1]
    out = like((half * rows, width), BF16)
    return launch(
        functools.partial(input_back_kernel, len(raws)),
        "input_back",
        (count,),
        [(r, pl.BlockSpec((rows, r.shape[1]), lambda i, t: (t[i], 0))) for r in raws]
        + [(weight, whole(weight.shape, True))],
        [
            (out, pl.BlockSpec((rows, width), lambda i, *_: (jnp.minimum(i, half - 1), 0))),
            (out, pl.BlockSpec((rows, width), lambda i, *_: (jnp.maximum(i - half, 0), 0))),
        ],
        prefetch=(order,),
        after=after,
    )


def join_x_kernel(units, place, *refs):
    out_refs = refs[2 * units :]
    levels = len(out_refs)
    for step in range(levels):
        level = (place[0] + step) % levels
        row = 0
        for unit in range(units):
            mine_ref, got_ref = refs[2 * unit : 2 * unit + 2]
            both = mine_ref[level].astype(F32) + got_ref[level].astype(F32)
            height = both.shape[0]
            out_refs[step][row : row + height] = both.astype(BF16)
            row += height


def join_x(units, z_place, after):
    levels, _, width = units[0][0].shape
    height = sum(u[0].shape[1] for u in units)
    arrays = [a for u in units for a in u]
    return launch(
        functools.partial(join_x_kernel, len(units)),
        "join_x",
        (1,),
        [(a, whole(a.shape)) for a in arrays],
        [(like((height, width), BF16), whole((height, width)))] * levels,
        prefetch=(z_place,),
        after=after,
    )


def join_partner_kernel(keep_ref, got_ref, out_ref):
    out_ref[...] = (keep_ref[...].astype(F32) + got_ref[...].astype(F32)).astype(BF16)


def join_partner(keep, got, size, after):
    width = keep.shape[1]
    away = keep.shape[0] - size
    block = pl.BlockSpec((size // 2, width), lambda i: (i, 0))
    return launch(
        join_partner_kernel,
        "join_partner",
        (away // (size // 2),),
        [(keep, block), (got, block)],
        [(like((away, width), BF16), block)],
        after=after,
    )[0]


def sum_input_kernel(parts, *refs):
    straight = refs[parts : parts + CHUNKS]
    out_ref = refs[-1]
    chunk = pl.program_id(0)
    value = straight[0][...]
    for other in range(1, CHUNKS):
        value = jnp.where(chunk == other, straight[other][...], value)
    out_ref[...] = value + sum_parts(refs[:parts])


def sum_input(parts, straight, rows, after):
    width = straight[0].shape[1]
    last = lambda a: a.shape[0] // rows - CHUNKS
    return launch(
        functools.partial(sum_input_kernel, len(parts)),
        "sum_input",
        (CHUNKS,),
        [
            (a, pl.BlockSpec((rows, width), lambda i, first=last(a): (first + i, 0)))
            for a in parts
        ]
        + [(a, whole(a.shape)) for a in straight],
        [
            (
                like((CHUNKS * rows, width), F32),
                pl.BlockSpec((rows, width), lambda i: (i, 0)),
            )
        ],
        after=after,
    )[0]


def order_kernel(counts, order, *refs):
    groups = []
    at = 0
    for n in counts:
        groups.append(refs[at : at + n])
        at += n
    out_ref, held = refs[at:]
    row = 0
    for group in groups:
        total = sum_parts(group)
        height = total.shape[0]
        held[row : row + height] = total.astype(BF16)
        row += height
    slots, piece, _ = out_ref.shape

    def move(slot, carry):
        start = pl.multiple_of(order[slot] * piece, piece)
        out_ref[slot] = held[pl.ds(start, piece)]
        return carry

    lax.fori_loop(0, slots, move, 0, unroll=8)


def order_pieces(groups, order, piece, after):
    arrays = [a for g in groups for a in g]
    slots = order.shape[0]
    shape = (slots, piece, BLOCK)
    return launch(
        functools.partial(order_kernel, [len(g) for g in groups]),
        "order_pieces",
        (1,),
        [(a, whole(a.shape)) for a in arrays],
        [(like(shape, BF16), whole(shape))],
        scratch=[pltpu.VMEM((slots * piece, BLOCK), BF16)],
        prefetch=(order,),
        after=after,
    )[0]


def outer_kernel(lefts, groups, rights, has_more, pieces, *refs):
    if pieces:
        place, refs = refs[0], refs[1:]
    left_refs = refs[:lefts]
    right_refs = refs[lefts : lefts + groups * rights]
    more_refs = refs[lefts + groups * rights : lefts + groups * rights + has_more]
    out_refs = refs[lefts + groups * rights + has_more : -2]
    turned, held = refs[-2:]
    rows = left_refs[0].shape[0]
    index = pl.program_id(0)

    @pl.when(index == 0)
    def _():
        for block in range(lefts):
            turned[:, block * rows : (block + 1) * rows] = left_refs[block][...].T

    def run(used):
        high = used[0].shape[0]
        total = mm(turned[:, :high], used[0][...])
        for n in range(1, rights):
            total = total + mm(turned[:, n * high : (n + 1) * high], used[n][...])
        for more in more_refs:
            total = total + more[...].astype(F32)
        if pieces:
            held[...] = total.astype(BF16)
        else:
            out_refs[0][...] = total.astype(BF16)

    if groups == 1:
        run(right_refs)
    else:
        for group in range(groups):

            @pl.when(index // (pl.num_programs(0) // groups) == group)
            def _(group=group):
                run(right_refs[group * rights : (group + 1) * rights])

    if pieces:
        store_pieces(held, place[0], *out_refs)


def store_pieces(held, x_here, *outs):
    levels, piece = outs[0].shape[0], outs[0].shape[-2]
    tall, wide = held.shape
    row_blocks = tall // BLOCK
    for side in range(2):
        shift = pl.multiple_of((x_here + side) % 2 * piece, piece)
        for panel in range(wide // BLOCK):
            lanes = slice(panel * BLOCK, (panel + 1) * BLOCK)
            for block in range(row_blocks):
                for level in range(levels):
                    start = block * BLOCK + 2 * level * piece
                    outs[side][level, panel * row_blocks + block] = held[
                        pl.ds(shift + start, piece), lanes
                    ]


def outer(left, groups, side, sides, step, more=(), place=None, levels=0, after=(), cost=COST):
    rows, width = left[0].shape
    cols = groups[0][0].shape[1] // sides
    step = min(step, cols)
    tiles = cols // step
    count = tiles * len(groups)

    def columns(array, group):
        if len(groups) == 1:
            at = lambda i, *_: (0, side * tiles + i)
        else:
            at = lambda i, *_: (0, side * tiles + jnp.clip(i - group * tiles, 0, tiles - 1))
        return array, pl.BlockSpec((array.shape[0], step), at)

    ins = (
        [(a, whole(a.shape, True)) for a in left]
        + [columns(a, n) for n, group in enumerate(groups) for a in group]
        + [(a, pl.BlockSpec((width, step), lambda i, *_: (0, i))) for a in more]
    )
    if not levels:
        outs = [
            (like((width, cols * len(groups)), BF16), pl.BlockSpec((width, step), lambda i: (0, i)))
        ]
    else:
        piece = BLOCK // (2 * levels)
        held = step // BLOCK * (width // BLOCK)
        outs = [
            (
                like((levels, held * count, piece, BLOCK), BF16),
                pl.BlockSpec((levels, held, piece, BLOCK), lambda i, p: (0, i, 0, 0)),
            )
        ] * 2
    return launch(
        functools.partial(
            outer_kernel, len(left), len(groups), len(groups[0]), len(more), levels > 0
        ),
        "outer",
        (count,),
        ins,
        outs,
        scratch=[pltpu.VMEM((width, rows * len(left)), BF16), pltpu.VMEM((width, step), BF16)],
        prefetch=(place,) if levels else (),
        after=after,
        cost=cost,
    )


def two_parts(value):
    high = value.astype(BF16)
    return high, (value - high.astype(F32)).astype(BF16)


def step_kernel(g_ref, left_ref, right_ref, master_ref, grad_ref, stepped_ref, square_ref):
    owners, slots, piece, width = g_ref.shape
    for slot in range(slots):
        low = jnp.concatenate([g_ref[o, slot] for o in range(owners)], axis=0)
        grad_ref[slot] = low.astype(F32)
        high, rest = two_parts(left_ref[slot])
        turned = mm(high, low) + mm(rest, low)
        t_high, t_rest = two_parts(turned)
        r_high, r_rest = two_parts(right_ref[slot])
        direction = mm(t_high, r_high) + mm(t_high, r_rest) + mm(t_rest, r_high)
        stepped = master_ref[slot] - 0.3 * direction
        stepped_ref[slot] = stepped
        square_ref[slot : slot + 1] = jnp.sum(stepped * stepped, axis=0, keepdims=True)


def stats_kernel(g_ref, left_ref, right_ref, new_left_ref, new_right_ref):
    owners, slots, piece, width = g_ref.shape
    for slot in range(slots):
        low = jnp.concatenate([g_ref[o, slot] for o in range(owners)], axis=0)
        new_left_ref[slot] = 0.5 * left_ref[slot] + 0.5 * mm(low, low, NT)
        new_right_ref[slot] = 0.5 * right_ref[slot] + 0.5 * mm(low, low, TN)


def finish_kernel(stepped_ref, ema_ref, norm_ref, master_ref, new_ema_ref):
    slots = stepped_ref.shape[0]
    for slot in range(slots):
        master = stepped_ref[slot] * lax.rsqrt(norm_ref[slot : slot + 1] + 1e-06)
        master_ref[slot] = master
        new_ema_ref[slot] = 0.5 * ema_ref[slot] + 0.5 * master


def block_specs(count, slots):
    return pl.BlockSpec((slots, BLOCK, BLOCK), lambda i: (i, 0, 0))


def exchange(value, axis, pairs):
    return lax.ppermute(value, axis, pairs)


def shards(
    tokens,
    seq_lengths,
    qkv_weight,
    out_weight,
    up_gate_weight,
    down_weight,
    qk_scale,
    mlp_scale,
    eigen_rates,
    cotangent,
    block_order,
    master_blocks,
    ema_blocks,
    left_stats,
    right_stats,
    left_root,
    right_root,
):
    x_rows = tokens[0]
    total, width = x_rows.shape
    cols = qk_scale.shape[0]
    heads = lax.axis_size("head")
    owners = lax.axis_size("batch")
    ranks = heads // 2
    here = lax.axis_index("head")
    rank, core = here // 2, here % 2
    share = total // heads
    rows = share // CHUNKS
    tiles_all = total // rows

    core_swap = [(i, i ^ 1) for i in range(heads)]
    shift_up = [
        [(i, (i // 2 + s) % ranks * 2 + i % 2) for i in range(heads)] for s in range(ranks)
    ]
    shift_down = [
        [(i, (i // 2 - s) % ranks * 2 + i % 2) for i in range(heads)] for s in range(ranks)
    ]
    far_steps = list(range(1, ranks))
    ring = far_steps + [0]

    shares = jnp.stack(
        [(rank - s) % ranks * 2 + (core + d) % 2 for d in (1, 0) for s in ring]
    ).astype(jnp.int32)
    lengths = seq_lengths[0]
    upto = jnp.arange(lengths.shape[0], dtype=jnp.int32)
    ends = jnp.sum(jnp.where(upto[None, :] <= upto[:, None], lengths[None, :], 0), axis=1)

    def begin_of(row):
        segment = jnp.sum((row[:, None] >= ends[None, :]).astype(jnp.int32), axis=1)
        member = segment[:, None] == jnp.arange(ends.shape[0], dtype=jnp.int32)[None, :]
        return jnp.sum(jnp.where(member, (ends - seq_lengths[0])[None, :], 0), axis=1)

    tile_rows = jnp.arange(tiles_all, dtype=jnp.int32) * rows
    tile_begin = begin_of(tile_rows)
    lane = jnp.arange(LANES, dtype=jnp.int32) % (HEAD_DIM // 2)
    freq = 10000.0 ** (-lane.astype(F32) * 2.0 / HEAD_DIM)
    near_angle = jnp.arange(rows, dtype=F32)[:, None] * freq[None, :]
    far_angle = (tile_rows - tile_begin).astype(F32)[:, None] * freq[None, :]
    near = jnp.stack([jnp.cos(near_angle), jnp.sin(near_angle)])
    far = jnp.stack([jnp.cos(far_angle), jnp.sin(far_angle)])
    gains = qk_scale[None, :]
    rates = eigen_rates.T

    q, k, v, q_rot, k_rot = project(x_rows, qkv_weight, gains, near, far)
    weights = [
        (up_gate_weight, down_weight),
        (exchange(up_gate_weight, "head", core_swap), exchange(down_weight, "head", core_swap)),
    ]
    scales = jnp.concatenate([mlp_scale, exchange(mlp_scale, "head", core_swap)], axis=1)

    def from_partner(send, keep, size):
        got = exchange(send, "head", core_swap)
        if ranks == 1:
            return keep[:size], [keep, got]
        away = (keep[:-size].astype(F32) + got[:-size].astype(F32)).astype(BF16)
        return away, [keep, got] + from_ranks(away, size)

    def from_ranks(away, size):
        return [
            exchange(away[n * size : (n + 1) * size], "head", shift_down[s])
            for n, s in enumerate(far_steps)
        ]

    def gather_ranks(own):
        return [exchange(own, "head", shift_up[s]) for s in far_steps] + [own]

    def gather_shares(own):
        mine = gather_ranks(own)
        return [exchange(b, "head", core_swap) for b in mine] + mine

    places = [(here * CHUNKS + j).astype(jnp.int32)[None] for j in range(CHUNKS)]
    tiles = [shares * CHUNKS + j for j in range(CHUNKS)]
    starts = [begin_of(t * rows) for t in tiles]
    chunks = range(CHUNKS)
    tile = 2 * BLOCK

    attn_out, lse, parts = [], [], []
    last = ()
    for j in chunks:
        half = heads // 2
        first = attend(
            q, k, v, out_weight, tiles[j][:half], starts[j][:half], rows, 0, heads, last
        )
        second = attend(
            q,
            k,
            v,
            out_weight,
            tiles[j][half:],
            starts[j][half:],
            rows,
            half,
            heads,
            (first[0], first[1]),
            2,
        )
        away, got = from_partner(first[2], second[2], rows)
        attn_out.append(second[0])
        lse.append(second[1])
        parts.append(got)
        last = (away,)
    joined = []
    for j in chunks:
        joined.append(join_attention(parts[j], x_rows, places[j], rates, rows, last))
        last = (joined[j][0],)
    hidden = [gather_ranks(joined[j][0]) for j in chunks]
    ffn = []
    for j in chunks:
        ffn.append(mlp(hidden[j], weights, scales, tile, last))
        last = (ffn[j][4],)
    ends_fwd = []
    for j in chunks:
        parts = [ffn[j][4]] + from_ranks(ffn[j][3], rows)
        ends_fwd.append(
            join_mlp(parts, joined[j][1], cotangent[0], j, rates, rows, last)
        )
        last = (ends_fwd[j][1],)
    d_rows = [gather_ranks(ends_fwd[j][1]) for j in chunks]
    back = []
    for j in chunks:
        back.append(mlp_back(d_rows[j], ffn[j][0], ffn[j][1], weights, scales, tile, last))
        last = (back[j][4],)

    row_blocks = width // BLOCK
    piece = BLOCK // owners
    across = ranks
    levels = owners // across
    z_here, x_here = lax.axis_index("batch") // across, lax.axis_index("batch") % across
    direct = levels if piece % 16 == 0 and across == 2 else 0
    x_place = x_here.astype(jnp.int32)[None]
    left_hidden = [b for h in hidden for b in h]
    left_down = [b for d in d_rows for b in d]
    rights = {
        "down": (left_down, [[f[2] for f in ffn]]),
        "up_gate": (left_hidden, [[b[0] for b in back], [b[1] for b in back]]),
    }

    def partner_part(name, after):
        out = outer(*rights[name], 1, 2, tile, after=after)[0]
        return out, exchange(out, "head", core_swap)

    def own_part(name, more, after):
        return outer(
            *rights[name],
            0,
            2,
            tile,
            more=(more,),
            place=x_place,
            levels=direct,
            after=after,
            cost=COST if name == "down" else TINY,
        )

    def as_pieces(matrix):
        panels = matrix.shape[1] // BLOCK
        return (
            matrix.reshape(row_blocks, levels, across, piece, panels, BLOCK)
            .transpose(1, 2, 4, 0, 3, 5)
            .reshape(levels, across, panels * row_blocks * piece, BLOCK)
        )

    def from_this_x(pieces):
        return [
            lax.dynamic_index_in_dim(pieces, (x_here + s) % across, 1, keepdims=False)
            for s in range(across)
        ]

    def hold(value, anchor):
        return value if anchor is None else lax.optimization_barrier((value, anchor))[0]

    x_step = lambda s: [
        (i, i // across * across + (i % across + s) % across) for i in range(owners)
    ]
    z_step = lambda s: [
        (i, (i // across + s) % levels * across + i % across) for i in range(owners)
    ]
    z_place = z_here.astype(jnp.int32)[None]

    def over_z(parts):
        return [parts[0]] + [
            exchange(parts[s], "batch", z_step(s)) for s in range(1, levels)
        ]

    def plain_x(pieces):
        total = pieces[0].astype(F32)
        for s in range(1, across):
            total = total + exchange(pieces[s], "batch", x_step(s)).astype(F32)
        total = total.astype(BF16)
        return [
            lax.dynamic_index_in_dim(total, (z_here + s) % levels, 0, keepdims=False)
            for s in range(levels)
        ]

    def start_x(outs):
        if direct:
            mine, other = [flat(o) for o in outs]
            return mine, exchange(other, "batch", x_step(1))
        return from_this_x(as_pieces(outs[0]))

    def finish_x(started, after):
        if direct:
            sums = join_x(started, z_place, after)
        else:
            sums = plain_x([jnp.concatenate(p, axis=1) for p in zip(*started, strict=True)])
        return over_z(sums)

    split = []
    partner = {}
    for j in chunks:
        parts = [back[j][4]] + from_ranks(back[j][3], rows)
        split.append(
            split_attention(
                parts,
                ends_fwd[j][2],
                joined[j][1],
                joined[j][2],
                x_rows,
                places[j],
                rates,
                rows,
                last,
            )
        )
        last = (split[j][0],)
        if j == 0:
            out, partner["down"] = partner_part("down", last)
            last = (out,)
    out, partner["up_gate"] = partner_part("up_gate", last)
    last = (out,)
    d_attn_mine = [gather_ranks(split[j][0]) for j in chunks]
    flat = lambda a: a.reshape(a.shape[:-3] + (-1, BLOCK))
    started = {}
    for name, gathered in (("down", d_attn_mine[0]), ("up_gate", d_attn_mine[-1])):
        outs = own_part(name, partner[name], last + tuple(gathered[:-1]))
        last = (outs[0],)
        started[name] = start_x(outs)
        turn = outs[0] if name == "down" else turn
    d_attn_rows = [
        [exchange(hold(b, turn), "head", core_swap) for b in mine] + mine
        for mine in d_attn_mine
    ]
    outs = outer(
        [b for d in d_attn_rows for b in d],
        [attn_out],
        0,
        1,
        tile,
        place=x_place,
        levels=direct,
        after=last,
        cost=SHORT,
    )
    last = (outs[0],)
    started["out"] = start_x(outs)
    order = jnp.concatenate(tiles)
    order_starts = jnp.concatenate(starts)
    moved = {}
    pairs_all = cols // LANES
    raws, gain_parts, late = [], [], []
    marks = []
    for pair in range(pairs_all):
        pair_back = attend_back(
            [b for d in d_attn_rows for b in d],
            q,
            k,
            v,
            attn_out,
            lse,
            out_weight,
            order,
            order_starts,
            rows,
            pair,
            last,
        )
        last = (pair_back[0],)
        marks.append(last[0])
        if pair == 0:
            moved["down_out"] = finish_x([started["down"], started["out"]], last)
            last = (moved["down_out"][0],)
        raw, gain_part, *outs = project_back(
            x_rows,
            q_rot,
            k_rot,
            gains,
            near,
            far,
            pair_back,
            order,
            rows,
            pair,
            x_place,
            direct,
            last,
        )
        last = (raw,)
        raws.append(raw)
        gain_parts.append(gain_part)
        late.append(start_x(outs))
        if pair == 0:
            last = last + tuple(moved["down_out"][1:])
            moved["up_gate"] = finish_x([started["up_gate"]], last)
            last = (moved["up_gate"][0],)
    arrived = moved["up_gate"][1:] + [a for pieces in late[:-1] for a in pieces[1:]]
    send, keep = input_back(raws, qkv_weight, shares, share, last + tuple(arrived))
    gain_grad = jnp.concatenate(gain_parts, axis=1)
    moved["late"] = finish_x(late, (keep,))

    def double(value, axis, size, anchors=()):
        step = 1
        turn = 0
        while step < size:
            got = exchange(value, axis, [(i, i ^ step) for i in range(size)])
            value = value + hold(got, anchors[turn] if turn < len(anchors) else None)
            step *= 2
            turn += 1
        return value

    rate_grad = double(
        hold(
            jnp.concatenate([sum(s[2] for s in split), sum(e[3] for e in ends_fwd)], axis=0),
            raws[-1],
        ),
        "head",
        heads,
    )
    both = hold(sum(b[2] for b in back), raws[-1])
    scale_cols = mlp_scale.shape[1]
    scale_grad = both[:, :scale_cols] + exchange(both[:, scale_cols:], "head", core_swap)

    slot_order = block_order[0]
    panel, rest = slot_order // row_blocks, slot_order % row_blocks
    late_panels = 3 * pairs_all
    panels = slot_order.shape[0] // row_blocks
    down_panels = scale_cols // BLOCK
    late_panel = panel % pairs_all * 3 + panel // pairs_all
    down_panel = panel - (panels - down_panels) + late_panels
    held_panel = jnp.where(panel >= panels - down_panels, down_panel, panel + down_panels)
    place_of = jnp.where(panel < late_panels, late_panel, held_panel) * row_blocks + rest
    groups = [moved[n] for n in ("late", "down_out", "up_gate")]
    if direct:
        ordered = order_pieces(groups, place_of, piece, ())
    else:
        sums = [sum(a.astype(F32) for a in g).astype(BF16) for g in groups]
        pieces = jnp.concatenate(sums, axis=0).reshape(-1, piece, BLOCK)
        ordered = jnp.take(pieces, place_of, axis=0, mode="clip")
    got = exchange(send, "head", core_swap)
    parts = [keep, got]
    last = (ordered,)
    if ranks > 1:
        away = join_partner(keep, got, share, last)
        last = (away,)
        parts += from_ranks(away, share)
    per_owner = slot_order.shape[0] // owners
    owned = lax.all_to_all(
        ordered.reshape(owners, per_owner, piece, BLOCK),
        "batch",
        split_axis=0,
        concat_axis=0,
        tiled=True,
    )
    slots = min(8, per_owner)
    if piece % 16:
        owned = owned.transpose(1, 0, 2, 3).reshape(1, per_owner, BLOCK, BLOCK)
    g_spec = pl.BlockSpec(
        (owned.shape[0], slots) + owned.shape[2:], lambda i: (0, i, 0, 0)
    )
    blk = pl.BlockSpec((slots, BLOCK, BLOCK), lambda i: (i, 0, 0))
    row = pl.BlockSpec((slots, BLOCK), lambda i: (i, 0))
    cube = jax.ShapeDtypeStruct((per_owner, BLOCK, BLOCK), F32)
    grid = (per_owner // slots,)
    owned_grad, stepped, column_sq = launch(
        step_kernel,
        "step",
        grid,
        [(owned, g_spec), (left_root[0], blk), (right_root[0], blk), (master_blocks[0], blk)],
        [(cube, blk), (cube, blk), (like((per_owner, BLOCK), F32), row)],
        after=last,
    )
    new_left, new_right = launch(
        stats_kernel,
        "stats",
        grid,
        [(owned, g_spec), (left_stats[0], blk), (right_stats[0], blk)],
        [(cube, blk), (cube, blk)],
        after=(column_sq,),
    )
    my_blocks = lax.dynamic_slice_in_dim(
        slot_order, lax.axis_index("batch") * per_owner, per_owner, 0
    )
    member = (
        (my_blocks // row_blocks)[:, None] == jnp.arange(panels, dtype=jnp.int32)[None, :]
    ).astype(F32)
    precise = lax.Precision.HIGHEST
    sums = jnp.concatenate(
        [jnp.einsum("sp,sb->pb", member, column_sq, precision=precise)]
        + [a.reshape(-1, LANES) for a in (gain_grad, rate_grad, scale_grad)],
        axis=0,
    )
    d_input = sum_input(parts, [s[1] for s in split], rows, (new_left,))
    sums = double(sums, "batch", owners, (new_left, d_input))
    totals = sums[:panels]
    small = sums[panels:].reshape(-1)
    gain_sum = small[:cols]
    rate_sum = small[cols : cols + 2 * width].reshape(2, width)
    scale_sum = small[cols + 2 * width :].reshape(mlp_scale.shape)
    norms = jnp.einsum("sp,pb->sb", member, totals, precision=precise)
    new_master, new_ema = pl.pallas_call(
        finish_kernel,
        grid=grid,
        in_specs=[blk, blk, row],
        out_specs=[blk, blk],
        out_shape=[cube, cube],
        name="finish",
    )(stepped, ema_blocks[0], norms)
    gain_step = 0.5 / math.sqrt(total * owners)
    width_share = width // heads
    rate_here = lax.dynamic_slice_in_dim(rate_sum, here * width_share, width_share, 1)
    rate_slice = lax.dynamic_slice_in_dim(rates, here * width_share, width_share, 1)
    mlp_scale_out = jnp.stack([scale_sum, mlp_scale - gain_step * scale_sum])
    new_gains = jnp.concatenate(
        [(qk_scale - gain_step * gain_sum)[None, :], rate_slice - gain_step * rate_here], axis=0
    )
    out_share = jnp.concatenate([e[0] for e in ends_fwd], axis=0)
    return (
        out_share[None],
        d_input[None],
        owned_grad[None],
        new_master[None],
        new_ema[None],
        new_left[None],
        new_right[None],
        gain_sum,
        mlp_scale_out,
        rate_here.T,
        new_gains,
    )


def solution(mesh):
    return jax.shard_map(
        shards,
        mesh=mesh,
        in_specs=(
            P("batch", None, None),
            P("batch", None),
            P(None, None, "head"),
            P("head", None),
            P(None, None, "head"),
            P("head", None),
            P("head"),
            P(None, "head"),
            P(),
            P("batch", "head", None),
            P("head", None),
            P("head", "batch", None, None),
            P("head", "batch", None, None),
            P("head", "batch", None, None),
            P("head", "batch", None, None),
            P("head", "batch", None, None),
            P("head", "batch", None, None),
        ),
        out_specs=(
            P("batch", "head", None),
            P("batch", "head", None),
            P("head", "batch", None, None),
            P("head", "batch", None, None),
            P("head", "batch", None, None),
            P("head", "batch", None, None),
            P("head", "batch", None, None),
            P("head"),
            P(None, None, "head"),
            P("head", None),
            P(None, "head"),
        ),
        check_vma=False,
    )
```

```python
import functools
import math

import jax
import jax.numpy as jnp
from jax import lax
from jax.experimental import pallas as pl
from jax.experimental.pallas import tpu as pltpu
from jax.sharding import PartitionSpec as P

HEAD_DIM = 64
BLOCK = 128
LANES = 128
CHUNKS = 2
F32 = jnp.float32
BF16 = jnp.bfloat16
NN = (((1,), (0,)), ((), ()))
NT = (((1,), (1,)), ((), ()))
TN = (((0,), (0,)), ((), ()))
COST = pl.CostEstimate(flops=10**11, transcendentals=0, bytes_accessed=10**7)
TINY = pl.CostEstimate(flops=10**9, transcendentals=0, bytes_accessed=10**7)
SHORT = pl.CostEstimate(flops=10**10, transcendentals=0, bytes_accessed=10**7)


def mm(a, b, dims=NN):
    return lax.dot_general(a, b, dims, preferred_element_type=F32)


def whole(shape, single=False):
    zeros = (0,) * len(shape)
    if single:
        return pl.BlockSpec(shape, lambda *_: zeros, pipeline_mode=pl.Buffered(1))
    return pl.BlockSpec(shape, lambda *_: zeros)


def launch(kernel, name, grid, ins, outs, scratch=(), prefetch=(), after=(), alias=0, cost=COST):
    first, count, extra = len(prefetch), len(ins), len(after)

    def body(*refs):
        kernel(*refs[: first + count], *refs[first + count + extra :])

    return pl.pallas_call(
        body,
        grid_spec=pltpu.PrefetchScalarGridSpec(
            num_scalar_prefetch=first,
            grid=grid,
            in_specs=[s for _, s in ins] + [pl.BlockSpec(memory_space=pl.ANY)] * extra,
            out_specs=[s for _, s in outs],
            scratch_shapes=list(scratch),
        ),
        out_shape=[o for o, _ in outs],
        input_output_aliases={first + count + n: n for n in range(alias)},
        name=name,
        cost_estimate=cost,
    )(*prefetch, *[a for a, _ in ins], *after)


def like(shape, dtype):
    return jax.ShapeDtypeStruct(shape, dtype)


def rms_rows(value):
    return value * lax.rsqrt(jnp.mean(value * value, axis=-1, keepdims=True) + 1e-06)


def rms_factor(value):
    return lax.rsqrt(jnp.mean(value * value, axis=-1, keepdims=True) + 1e-06)


def rms_back(normed, factor, gradient):
    return factor * (gradient - normed * jnp.mean(gradient * normed, axis=-1, keepdims=True))


def lane_ids():
    return lax.broadcasted_iota(jnp.int32, (1, LANES), 1)


def head_mean(value, ones_block):
    high = value.astype(BF16)
    rest = (value - high.astype(F32)).astype(BF16)
    return (mm(high, ones_block) + mm(rest, ones_block)) * (1.0 / HEAD_DIM)


def ones_block():
    row = lax.broadcasted_iota(jnp.int32, (LANES, LANES), 0) // HEAD_DIM
    col = lax.broadcasted_iota(jnp.int32, (LANES, LANES), 1) // HEAD_DIM
    return jnp.where(row == col, 1.0, 0.0).astype(BF16)


def half_turn(value):
    first = (lane_ids() & (HEAD_DIM - 1)) < HEAD_DIM // 2
    return jnp.where(
        first,
        pltpu.roll(value, LANES - HEAD_DIM // 2, 1),
        pltpu.roll(value, HEAD_DIM // 2, 1),
    )


def angles(tile, near_ref, far_ref):
    cos_r, sin_r = near_ref[0], near_ref[1]
    cos_0 = far_ref[0, pl.ds(tile, 1), :]
    sin_0 = far_ref[1, pl.ds(tile, 1), :]
    first = (lane_ids() & (HEAD_DIM - 1)) < HEAD_DIM // 2
    sine = sin_0 * cos_r + cos_0 * sin_r
    return cos_0 * cos_r - sin_0 * sin_r, jnp.where(first, -sine, sine)


def project_kernel(
    x_ref, w_ref, gain_ref, near_ref, far_ref, q_ref, k_ref, v_ref, q_rot_ref, k_rot_ref
):
    tile = pl.program_id(0)
    cosine, sine = angles(tile, near_ref, far_ref)
    ones = ones_block()
    x = x_ref[...]
    for index, used_ref, rot_ref in ((0, q_ref, q_rot_ref), (1, k_ref, k_rot_ref)):
        raw = mm(x, w_ref[index])
        for pair in range(raw.shape[1] // LANES):
            lanes = slice(pair * LANES, (pair + 1) * LANES)
            value = raw[:, lanes]
            turned = value * cosine + half_turn(value) * sine
            factor = lax.rsqrt(head_mean(turned * turned, ones) + 1e-06)
            rot_ref[:, lanes] = turned
            used_ref[:, lanes] = (turned * factor * gain_ref[:, lanes]).astype(BF16)
    v_ref[...] = mm(x, w_ref[2]).astype(BF16)


def project(x, weight, gains, near, far):
    rows, width = x.shape
    cols = weight.shape[2]
    tile = near.shape[1]
    by_row = lambda w: pl.BlockSpec((tile, w), lambda i: (i, 0))
    return pl.pallas_call(
        project_kernel,
        grid=(rows // tile,),
        in_specs=[
            by_row(width),
            whole(weight.shape, True),
            whole((1, cols)),
            whole(near.shape),
            whole(far.shape),
        ],
        out_specs=[by_row(cols)] * 5,
        out_shape=[jax.ShapeDtypeStruct((rows, cols), BF16)] * 3
        + [jax.ShapeDtypeStruct((rows, cols), F32)] * 2,
        name="project",
        cost_estimate=COST,
    )(x, weight, gains, near, far)


def key_tiles(first_row, start, wide, narrow, visit):
    full = first_row // wide

    def step(index, carry):
        visit(pl.multiple_of(index * wide, wide), wide, False)
        return carry

    lax.fori_loop(start // wide, full, step, 0)
    diagonal = (first_row // narrow) * narrow

    @pl.when(diagonal > full * wide)
    def _():
        visit(pl.multiple_of(full * wide, narrow), narrow, False)

    visit(pl.multiple_of(diagonal, narrow), narrow, True)


def attend_kernel(
    wide, tiles, starts, q_ref, k_ref, v_ref, w_ref, o_ref, lse_ref, part_ref, acc, mixed
):
    index = pl.program_id(0)
    rows = q_ref.shape[0]
    first_row = tiles[index] * rows
    start = starts[index]
    narrow = wide // 2
    low = lane_ids() < HEAD_DIM
    zero = jnp.zeros((), BF16)

    def one_pair(pair, carry):
        lanes = pl.ds(pl.multiple_of(pair * LANES, LANES), LANES)
        q = q_ref[:, lanes] * jnp.asarray(1.0 / math.sqrt(HEAD_DIM), BF16)
        q_both = jnp.concatenate([jnp.where(low, q, zero), jnp.where(low, zero, q)], axis=0)
        acc[...] = jnp.zeros_like(acc)

        def visit(key_0, size, masked):
            keys = pl.ds(key_0, size)
            weights = jnp.exp(mm(q_both, k_ref[keys, lanes], NT))
            if masked:
                row = lax.broadcasted_iota(jnp.int32, (2 * rows, size), 0)
                row = jnp.where(row < rows, row, row - rows) + first_row
                col = lax.broadcasted_iota(jnp.int32, (2 * rows, size), 1) + key_0
                weights = jnp.where((col <= row) & (col >= start), weights, 0.0)
            total = weights[:, :LANES]
            for part in range(1, size // LANES):
                total = total + weights[:, part * LANES : (part + 1) * LANES]
            acc[:, LANES:] += total
            acc[:, :LANES] += mm(weights.astype(BF16), v_ref[keys, lanes])

        key_tiles(first_row, start, wide, narrow, visit)
        total_a = jnp.sum(acc[:rows, LANES:], axis=1, keepdims=True)
        total_b = jnp.sum(acc[rows:, LANES:], axis=1, keepdims=True)
        summed = jnp.where(low, acc[:rows, :LANES], acc[rows:, :LANES])
        out = (summed / jnp.where(low, total_a, total_b)).astype(BF16)
        o_ref[:, lanes] = out
        lse_ref[:, lanes] = jnp.log(jnp.where(low, total_b, total_a))
        mixed[:, lanes] = out
        return carry

    lax.fori_loop(0, q_ref.shape[1] // LANES, one_pair, 0)
    part_ref[...] = mm(mixed[...], w_ref[...]).astype(BF16)


def attend(q, k, v, weight, tiles, starts, rows, offset, places, after, alias=0):
    count = tiles.shape[0]
    cols = k.shape[1]
    width = weight.shape[1]
    at_place = pl.BlockSpec((rows, cols), lambda i, t, s: (i + offset, 0))
    return launch(
        functools.partial(attend_kernel, 4 * BLOCK),
        "attend",
        (count,),
        [
            (q, pl.BlockSpec((rows, cols), lambda i, t, s: (t[i], 0))),
            (k, whole(k.shape, True)),
            (v, whole(v.shape, True)),
            (weight, whole(weight.shape, True)),
        ],
        [
            (like((places * rows, cols), BF16), at_place),
            (like((places * rows, cols), F32), at_place),
            (like((count * rows, width), BF16), pl.BlockSpec((rows, width), lambda i, t, s: (i, 0))),
        ],
        scratch=[pltpu.VMEM((2 * rows, 2 * LANES), F32), pltpu.VMEM((rows, cols), BF16)],
        prefetch=(tiles, starts),
        after=after,
        alias=alias,
    )


def attend_back_kernel(blocks, wide, tiles, starts, *refs):
    row_refs = refs[:blocks]
    q_ref, k_ref, v_ref = refs[blocks : blocks + 3]
    o_refs = refs[blocks + 3 : blocks + 3 + CHUNKS]
    lse_refs = refs[blocks + 3 + CHUNKS : blocks + 3 + 2 * CHUNKS]
    w_ref, dq_ref, dk_ref, dv_ref, rows_s, o_ref, lse_ref, acc = refs[blocks + 3 + 2 * CHUNKS :]
    index = pl.program_id(0)
    rows = q_ref.shape[0]
    narrow = wide // 2

    @pl.when(index == 0)
    def _():
        dk_ref[...] = jnp.zeros_like(dk_ref)
        dv_ref[...] = jnp.zeros_like(dv_ref)

    for block in range(blocks):

        @pl.when(index == block)
        def _(block=block):
            rows_s[...] = row_refs[block][...]

    for chunk in range(CHUNKS):

        @pl.when(index // (blocks // CHUNKS) == chunk)
        def _(chunk=chunk):
            o_ref[...] = o_refs[chunk][...]
            lse_ref[...] = lse_refs[chunk][...]

    first_row = tiles[index] * rows
    start = starts[index]
    low = lane_ids() < HEAD_DIM
    place = lane_ids() & (HEAD_DIM - 1)
    zero = jnp.zeros((), BF16)
    ones = jnp.where(place < 3, 1.0, 0.0).astype(BF16)

    def parts(value):
        high = value.astype(BF16).astype(F32)
        rest = value - high
        middle = rest.astype(BF16).astype(F32)
        picked = jnp.where(place == 1, middle, jnp.where(place == 2, rest - middle, 0.0))
        return jnp.where(place == 0, high, picked).astype(BF16)

    d_rows = rows_s[...]
    d_attn = mm(d_rows, w_ref[...], NT).astype(BF16)
    for pair in range(q_ref.shape[1] // LANES):
        lanes = slice(pair * LANES, (pair + 1) * LANES)
        q = q_ref[:, lanes] * jnp.asarray(1.0 / math.sqrt(HEAD_DIM), BF16)
        d_out = d_attn[:, lanes]
        minus_lse = parts(-lse_ref[:, lanes])
        product = d_out.astype(F32) * o_ref[:, lanes].astype(F32)
        sum_a = jnp.sum(jnp.where(low, product, 0.0), axis=1, keepdims=True)
        sum_b = jnp.sum(jnp.where(low, 0.0, product), axis=1, keepdims=True)
        minus_delta = parts(-jnp.where(low, sum_b, sum_a))
        q_ext = (jnp.where(low, q, minus_lse), jnp.where(low, minus_lse, q))
        d_ext = (jnp.where(low, d_out, minus_delta), jnp.where(low, minus_delta, d_out))
        q_both = jnp.concatenate([jnp.where(low, q, zero), jnp.where(low, zero, q)], axis=0)
        d_both = jnp.concatenate(
            [jnp.where(low, d_out, zero), jnp.where(low, zero, d_out)], axis=0
        )
        acc[...] = jnp.zeros_like(acc)

        def visit(key_0, size, masked):
            keys = pl.ds(key_0, size)
            k = k_ref[keys, lanes]
            v = v_ref[keys, lanes]
            k_ext = (jnp.where(low, k, ones), jnp.where(low, ones, k))
            v_ext = (jnp.where(low, v, ones), jnp.where(low, ones, v))
            if masked:
                col = lax.broadcasted_iota(jnp.int32, (size, rows), 1) + first_row
                row = lax.broadcasted_iota(jnp.int32, (size, rows), 0) + key_0
                allowed = (row <= col) & (row >= start)
            probs = []
            d_scores = []
            for head in range(2):
                prob = jnp.exp(mm(k_ext[head], q_ext[head], NT))
                if masked:
                    prob = jnp.where(allowed, prob, 0.0)
                d_score = prob * mm(v_ext[head], d_ext[head], NT)
                probs.append(prob.astype(BF16))
                d_scores.append(d_score.astype(BF16))
            dv_ref[keys, lanes] += mm(jnp.concatenate(probs, axis=1), d_both)
            dk_ref[keys, lanes] += mm(jnp.concatenate(d_scores, axis=1), q_both)
            k_both = jnp.concatenate([jnp.where(low, k, zero), jnp.where(low, zero, k)], axis=0)
            acc[...] += mm(jnp.concatenate(d_scores, axis=0), k_both, TN)

        key_tiles(first_row, start, wide, narrow, visit)
        dq_ref[:, lanes] = acc[...] * (1.0 / math.sqrt(HEAD_DIM))


def attend_back(row_blocks, q, k, v, outs, lses, weight, tiles, starts, rows, pair, after):
    count = tiles.shape[0]
    total = k.shape[0]
    width = weight.shape[1]
    at_tile = pl.BlockSpec((rows, LANES), lambda i, t, s: (t[i], pair))
    each = count // CHUNKS

    def at_step(chunk):
        return pl.BlockSpec(
            (rows, LANES), lambda i, t, s: (jnp.clip(i - chunk * each, 0, each - 1), pair)
        )

    column = pl.BlockSpec((total, LANES), lambda *_: (0, pair), pipeline_mode=pl.Buffered(1))
    return launch(
        functools.partial(attend_back_kernel, len(row_blocks), 4 * BLOCK),
        "attend_back",
        (count,),
        [(b, whole(b.shape, True)) for b in row_blocks]
        + [
            (q, at_tile),
            (k, column),
            (v, column),
        ]
        + [(a, at_step(n)) for n, a in enumerate(outs)]
        + [(a, at_step(n)) for n, a in enumerate(lses)]
        + [
            (weight, pl.BlockSpec((LANES, width), lambda *_: (pair, 0))),
        ],
        [
            (like((count * rows, LANES), F32), pl.BlockSpec((rows, LANES), lambda i, *_: (i, 0))),
            (like((total, LANES), F32), whole((total, LANES))),
            (like((total, LANES), F32), whole((total, LANES))),
        ],
        scratch=[
            pltpu.VMEM((rows, width), BF16),
            pltpu.VMEM((rows, LANES), BF16),
            pltpu.VMEM((rows, LANES), F32),
            pltpu.VMEM((rows, LANES), F32),
        ],
        prefetch=(tiles, starts),
        after=after,
        cost=SHORT,
    )


def sum_parts(refs):
    total = refs[0][...].astype(F32)
    for ref in refs[1:]:
        total = total + ref[...].astype(F32)
    return total


def join_attention_kernel(parts, place, *refs):
    x_ref, rate_ref = refs[parts : parts + 2]
    low_ref, hidden_ref, branch_ref = refs[parts + 2 :]
    branch = sum_parts(refs[:parts])
    x = x_ref[...].astype(F32)
    hidden = rms_rows(x + rate_ref[0:1] * (rms_rows(branch) - x))
    branch_ref[...] = branch
    hidden_ref[...] = hidden
    low_ref[...] = hidden.astype(BF16)


def part_specs(parts, rows, width):
    return [
        pl.BlockSpec((rows, width), lambda i, *_, last=a.shape[0] // rows: (last - SUB + i, 0))
        for a in parts
    ]


SUB = 2


def join_attention(parts, x, place, rates, share, after):
    width = x.shape[1]
    rows = share // SUB
    here = pl.BlockSpec((rows, width), lambda i, p: (i, 0))
    return launch(
        functools.partial(join_attention_kernel, len(parts)),
        "join_attention",
        (SUB,),
        list(zip(parts, part_specs(parts, rows, width), strict=True))
        + [
            (x, pl.BlockSpec((rows, width), lambda i, p: (p[0] * SUB + i, 0))),
            (rates, whole(rates.shape)),
        ],
        [(like((share, width), d), here) for d in (BF16, F32, F32)],
        prefetch=(place,),
        after=after,
    )


def weight_tiles(weight, down, step, side):
    _, width, cols = weight.shape
    count = cols // step
    if side == 0:
        at = lambda t: jnp.minimum(t, count - 1)
    else:
        at = lambda t: jnp.maximum(t - count, 0)
    return [
        (weight, pl.BlockSpec((2, width, step), lambda t, *_: (0, 0, at(t)))),
        (down, pl.BlockSpec((step, width), lambda t, *_: (at(t), 0))),
    ]


def mlp_kernel(blocks, *refs):
    row_refs = refs[:blocks]
    sides = (refs[blocks : blocks + 2], refs[blocks + 2 : blocks + 4])
    scale_ref = refs[blocks + 4]
    up_ref, gate_ref, mixed_ref, away_ref, own_ref, x_s, acc = refs[blocks + 5 :]
    tile = pl.program_id(0)
    count = pl.num_programs(0)
    rows = row_refs[0].shape[0]

    @pl.when(tile == 0)
    def _():
        for block in range(blocks):
            x_s[block * rows : (block + 1) * rows] = row_refs[block][...]
        acc[...] = jnp.zeros_like(acc)

    def run(w_ref, down_ref):
        x = x_s[...]
        up = mm(x, w_ref[0])
        gate = mm(x, w_ref[1])
        up_ref[...] = up.astype(BF16)
        gate_ref[...] = gate.astype(BF16)
        scaled = gate * scale_ref[1:2]
        mixed = (up * scale_ref[0:1] * (scaled * jax.nn.sigmoid(scaled))).astype(BF16)
        mixed_ref[...] = mixed
        acc[...] += mm(mixed, down_ref[...])

    for side in range(2):

        @pl.when(tile // (count // 2) == side)
        def _(side=side):
            run(*sides[side])

    @pl.when(tile == count - 1)
    def _():
        last = (blocks - 1) * rows
        own_ref[...] = acc[last:]
        if blocks > 1:
            away_ref[...] = acc[:last].astype(BF16)


def mlp(row_blocks, weights, scales, step, after):
    rows, width = row_blocks[0].shape
    blocks = len(row_blocks)
    height = rows * blocks
    cols = 2 * weights[0][0].shape[2]
    at_tile = lambda h: pl.BlockSpec((h, step), lambda t: (0, t))
    far = max(blocks - 1, 1) * rows
    return launch(
        functools.partial(mlp_kernel, blocks),
        "mlp",
        (cols // step,),
        [(b, whole(b.shape, True)) for b in row_blocks]
        + weight_tiles(*weights[0], step, 0)
        + weight_tiles(*weights[1], step, 1)
        + [(scales, at_tile(2))],
        [(like((height, cols), BF16), at_tile(height))] * 3
        + [
            (like((far, width), BF16), whole((far, width))),
            (like((rows, width), F32), whole((rows, width))),
        ],
        scratch=[pltpu.VMEM((height, width), BF16), pltpu.VMEM((height, width), F32)],
        after=after,
    )


def join_mlp_kernel(parts, *refs):
    hidden_ref, cot_ref, rate_ref = refs[parts : parts + 3]
    out_ref, low_ref, d_hidden_ref, rate_grad_ref = refs[parts + 3 :]
    branch = sum_parts(refs[:parts])
    hidden = hidden_ref[...]
    rate = rate_ref[1:2]
    factor = rms_factor(branch)
    normed = branch * factor
    gap = normed - hidden
    before = hidden + rate * gap
    factor_out = rms_factor(before)
    out = before * factor_out
    d_before = rms_back(out, factor_out, cot_ref[...].astype(F32))
    out_ref[...] = out
    d_hidden_ref[...] = (1.0 - rate) * d_before
    low_ref[...] = rms_back(normed, factor, rate * d_before).astype(BF16)

    @pl.when(pl.program_id(0) == 0)
    def _():
        rate_grad_ref[...] = jnp.zeros_like(rate_grad_ref)

    rate_grad_ref[...] += jnp.sum(d_before * gap, axis=0, keepdims=True)


def join_mlp(parts, hidden, cotangent, chunk, rates, share, after, alias):
    width = hidden.shape[1]
    rows = share // SUB
    here = pl.BlockSpec((rows, width), lambda i: (i, 0))
    return launch(
        functools.partial(join_mlp_kernel, len(parts)),
        "join_mlp",
        (SUB,),
        list(zip(parts, part_specs(parts, rows, width), strict=True))
        + [
            (hidden, here),
            (cotangent, pl.BlockSpec((rows, width), lambda i: (chunk * SUB + i, 0))),
            (rates, whole(rates.shape)),
        ],
        [
            (
                like((CHUNKS * share, width), F32),
                pl.BlockSpec((rows, width), lambda i: (chunk * SUB + i, 0)),
            )
        ]
        + [(like((share, width), d), here) for d in (BF16, F32)]
        + [(like((1, width), F32), whole((1, width)))],
        after=after,
        alias=alias,
    )


def mlp_back_kernel(blocks, *refs):
    row_refs = refs[:blocks]
    sides = (refs[blocks : blocks + 2], refs[blocks + 2 : blocks + 4])
    scale_ref, up_ref, gate_ref = refs[blocks + 4 : blocks + 7]
    d_up_ref, d_gate_ref, sums_ref, away_ref, own_ref, x_s, acc = refs[blocks + 7 :]
    tile = pl.program_id(0)
    count = pl.num_programs(0)
    rows = row_refs[0].shape[0]

    @pl.when(tile == 0)
    def _():
        for block in range(blocks):
            x_s[block * rows : (block + 1) * rows] = row_refs[block][...]
        acc[...] = jnp.zeros_like(acc)

    def run(w_ref, down_ref):
        d_mixed = mm(x_s[...], down_ref[...], NT)
        up_raw = up_ref[...].astype(F32)
        gate_raw = gate_ref[...].astype(F32)
        scale_up = scale_ref[0:1]
        scale_gate = scale_ref[1:2]
        gate = gate_raw * scale_gate
        sig = jax.nn.sigmoid(gate)
        d_up = d_mixed * (gate * sig)
        d_gate = d_mixed * (up_raw * scale_up) * (sig * (1.0 + gate * (1.0 - sig)))
        sums_ref[0:1] = jnp.sum(d_up * up_raw, axis=0, keepdims=True)
        sums_ref[1:2] = jnp.sum(d_gate * gate_raw, axis=0, keepdims=True)
        d_up = (d_up * scale_up).astype(BF16)
        d_gate = (d_gate * scale_gate).astype(BF16)
        d_up_ref[...] = d_up
        d_gate_ref[...] = d_gate
        acc[...] += mm(d_up, w_ref[0], NT) + mm(d_gate, w_ref[1], NT)

    for side in range(2):

        @pl.when(tile // (count // 2) == side)
        def _(side=side):
            run(*sides[side])

    @pl.when(tile == count - 1)
    def _():
        last = (blocks - 1) * rows
        own_ref[...] = acc[last:]
        if blocks > 1:
            away_ref[...] = acc[:last].astype(BF16)


def mlp_back(row_blocks, up, gate, weights, scales, step, after):
    rows, width = row_blocks[0].shape
    blocks = len(row_blocks)
    height = rows * blocks
    cols = 2 * weights[0][0].shape[2]
    at_tile = lambda h: pl.BlockSpec((h, step), lambda t: (0, t))
    far = max(blocks - 1, 1) * rows
    return launch(
        functools.partial(mlp_back_kernel, blocks),
        "mlp_back",
        (cols // step,),
        [(b, whole(b.shape, True)) for b in row_blocks]
        + weight_tiles(*weights[0], step, 0)
        + weight_tiles(*weights[1], step, 1)
        + [(scales, at_tile(2)), (up, at_tile(height)), (gate, at_tile(height))],
        [(like((height, cols), BF16), at_tile(height))] * 2
        + [
            (like((2, cols), F32), at_tile(2)),
            (like((far, width), BF16), whole((far, width))),
            (like((rows, width), F32), whole((rows, width))),
        ],
        scratch=[pltpu.VMEM((height, width), BF16), pltpu.VMEM((height, width), F32)],
        after=after,
    )


def split_attention_kernel(parts, place, *refs):
    d_hidden_ref, hidden_ref, branch_ref, x_ref, rate_ref = refs[parts : parts + 5]
    low_ref, d_input_ref, rate_grad_ref = refs[parts + 5 :]
    d_hidden = sum_parts(refs[:parts]) + d_hidden_ref[...]
    hidden = hidden_ref[...]
    branch = branch_ref[...]
    x = x_ref[...].astype(F32)
    rate = rate_ref[0:1]
    factor = rms_factor(branch)
    normed = branch * factor
    gap = normed - x
    d_before = rms_back(hidden, rms_factor(x + rate * gap), d_hidden)
    d_input_ref[...] = (1.0 - rate) * d_before
    low_ref[...] = rms_back(normed, factor, rate * d_before).astype(BF16)

    @pl.when(pl.program_id(0) == 0)
    def _():
        rate_grad_ref[...] = jnp.zeros_like(rate_grad_ref)

    rate_grad_ref[...] += jnp.sum(d_before * gap, axis=0, keepdims=True)


def split_attention(parts, d_hidden, hidden, branch, x, place, rates, share, after):
    width = x.shape[1]
    rows = share // SUB
    here = pl.BlockSpec((rows, width), lambda i, p: (i, 0))
    return launch(
        functools.partial(split_attention_kernel, len(parts)),
        "split_attention",
        (SUB,),
        list(zip(parts, part_specs(parts, rows, width), strict=True))
        + [(d_hidden, here), (hidden, here), (branch, here)]
        + [
            (x, pl.BlockSpec((rows, width), lambda i, p: (p[0] * SUB + i, 0))),
            (rates, whole(rates.shape)),
        ],
        [(like((share, width), d), here) for d in (BF16, F32)]
        + [(like((1, width), F32), whole((1, width)))],
        prefetch=(place,),
        after=after,
    )


def project_back_kernel(order, x_here, *refs):
    x_ref, q_rot_ref, k_rot_ref, gain_ref, near_ref, far_ref = refs[:6]
    d_refs = refs[6:9]
    raw_ref, gain_grad_ref = refs[9:11]
    grad_refs = refs[11:-2]
    acc, held = refs[-2:]
    index = pl.program_id(0)
    count = pl.num_programs(0)

    @pl.when(index == 0)
    def _():
        gain_grad_ref[...] = jnp.zeros_like(gain_grad_ref)
        acc[...] = jnp.zeros_like(acc)

    cosine, sine = angles(order[index], near_ref, far_ref)
    ones = ones_block()
    d_raw = []
    for which, rot_ref in ((0, q_rot_ref), (1, k_rot_ref)):
        d_used = d_refs[which][...]
        turned = rot_ref[...]
        factor = lax.rsqrt(head_mean(turned * turned, ones) + 1e-06)
        normed = turned * factor
        gain_grad_ref[...] += jnp.sum(d_used * normed, axis=0, keepdims=True)
        d_normed = d_used * gain_ref[...]
        d_turned = factor * (d_normed - normed * head_mean(d_normed * normed, ones))
        d_raw.append((d_turned * cosine - half_turn(d_turned) * sine).astype(BF16))
    d_raw.append(d_refs[2][...].astype(BF16))
    d_all = jnp.concatenate(d_raw, axis=1)
    raw_ref[...] = d_all
    acc[...] += mm(d_all, x_ref[...], TN)

    @pl.when(index == count - 1)
    def _():
        held[...] = acc[...].T.astype(BF16)
        if len(grad_refs) == 1:
            grad_refs[0][...] = held[...]
        else:
            store_pieces(held, x_here[0], *grad_refs)


def project_back(x, q_rot, k_rot, gains, near, far, parts, order, rows, pair, place, levels, after):
    total, width = x.shape
    count = order.shape[0]
    wide = 3 * LANES
    at_tile = lambda w, n: pl.BlockSpec((rows, w), lambda i, t, *_: (t[i], n))
    if levels:
        shape = (levels, 3 * (width // BLOCK), BLOCK // (2 * levels), BLOCK)
        grads = [(like(shape, BF16), whole(shape))] * 2
    else:
        grads = [(like((width, wide), BF16), whole((width, wide)))]
    return launch(
        project_back_kernel,
        "project_back",
        (count,),
        [
            (x, at_tile(width, 0)),
            (q_rot, at_tile(LANES, pair)),
            (k_rot, at_tile(LANES, pair)),
            (gains, pl.BlockSpec((1, LANES), lambda *_: (0, pair))),
            (near, whole(near.shape)),
            (far, whole(far.shape)),
        ]
        + [(parts[0], pl.BlockSpec((rows, LANES), lambda i, *_: (i, 0)))]
        + [(a, at_tile(LANES, 0)) for a in parts[1:]],
        [
            (like((total, wide), BF16), at_tile(wide, 0)),
            (like((1, LANES), F32), whole((1, LANES))),
        ]
        + grads,
        scratch=[pltpu.VMEM((wide, width), F32), pltpu.VMEM((width, wide), BF16)],
        prefetch=(order, place),
        after=after,
    )


def input_back_kernel(pairs, order, *refs):
    raw_refs = refs[:pairs]
    w_ref, send_ref, keep_ref = refs[pairs : pairs + 3]
    index = pl.program_id(0)
    count = pl.num_programs(0)
    d_x = None
    for which in range(3):
        lanes = slice(which * LANES, (which + 1) * LANES)
        d_all = jnp.concatenate([r[:, lanes] for r in raw_refs], axis=1)
        product = mm(d_all, w_ref[which], NT)
        d_x = product if d_x is None else d_x + product
    d_x = d_x.astype(BF16)

    @pl.when(index < count // 2)
    def _():
        send_ref[...] = d_x

    @pl.when(index >= count // 2)
    def _():
        keep_ref[...] = d_x


def input_back(raws, weight, order, rows, after):
    count = order.shape[0]
    half = count // 2
    width = weight.shape[1]
    out = like((half * rows, width), BF16)
    return launch(
        functools.partial(input_back_kernel, len(raws)),
        "input_back",
        (count,),
        [(r, pl.BlockSpec((rows, r.shape[1]), lambda i, t: (t[i], 0))) for r in raws]
        + [(weight, whole(weight.shape, True))],
        [
            (out, pl.BlockSpec((rows, width), lambda i, *_: (jnp.minimum(i, half - 1), 0))),
            (out, pl.BlockSpec((rows, width), lambda i, *_: (jnp.maximum(i - half, 0), 0))),
        ],
        prefetch=(order,),
        after=after,
    )


def join_x_kernel(units, place, *refs):
    out_refs = refs[2 * units :]
    levels = len(out_refs)
    for step in range(levels):
        level = (place[0] + step) % levels
        row = 0
        for unit in range(units):
            mine_ref, got_ref = refs[2 * unit : 2 * unit + 2]
            both = mine_ref[level].astype(F32) + got_ref[level].astype(F32)
            height = both.shape[0]
            out_refs[step][row : row + height] = both.astype(BF16)
            row += height


def join_x(units, z_place, after):
    levels, _, width = units[0][0].shape
    height = sum(u[0].shape[1] for u in units)
    arrays = [a for u in units for a in u]
    return launch(
        functools.partial(join_x_kernel, len(units)),
        "join_x",
        (1,),
        [(a, whole(a.shape)) for a in arrays],
        [(like((height, width), BF16), whole((height, width)))] * levels,
        prefetch=(z_place,),
        after=after,
    )


def join_partner_kernel(keep_ref, got_ref, out_ref):
    out_ref[...] = (keep_ref[...].astype(F32) + got_ref[...].astype(F32)).astype(BF16)


def join_partner(keep, got, size, after):
    width = keep.shape[1]
    away = keep.shape[0] - size
    block = pl.BlockSpec((size // 2, width), lambda i: (i, 0))
    return launch(
        join_partner_kernel,
        "join_partner",
        (away // (size // 2),),
        [(keep, block), (got, block)],
        [(like((away, width), BF16), block)],
        after=after,
    )[0]


def sum_input_kernel(parts, *refs):
    straight = refs[parts : parts + CHUNKS]
    out_ref = refs[-1]
    chunk = pl.program_id(0)
    value = straight[0][...]
    for other in range(1, CHUNKS):
        value = jnp.where(chunk == other, straight[other][...], value)
    out_ref[...] = value + sum_parts(refs[:parts])


def sum_input(parts, straight, rows, after):
    width = straight[0].shape[1]
    last = lambda a: a.shape[0] // rows - CHUNKS
    return launch(
        functools.partial(sum_input_kernel, len(parts)),
        "sum_input",
        (CHUNKS,),
        [
            (a, pl.BlockSpec((rows, width), lambda i, first=last(a): (first + i, 0)))
            for a in parts
        ]
        + [(a, whole(a.shape)) for a in straight],
        [
            (
                like((CHUNKS * rows, width), F32),
                pl.BlockSpec((rows, width), lambda i: (i, 0)),
            )
        ],
        after=after,
    )[0]


def order_kernel(counts, order, *refs):
    groups = []
    at = 0
    for n in counts:
        groups.append(refs[at : at + n])
        at += n
    out_ref, held = refs[at:]
    row = 0
    for group in groups:
        total = sum_parts(group)
        height = total.shape[0]
        held[row : row + height] = total.astype(BF16)
        row += height
    slots, piece, _ = out_ref.shape

    def move(slot, carry):
        start = pl.multiple_of(order[slot] * piece, piece)
        out_ref[slot] = held[pl.ds(start, piece)]
        return carry

    lax.fori_loop(0, slots, move, 0, unroll=8)


def order_pieces(groups, order, piece, after):
    arrays = [a for g in groups for a in g]
    slots = order.shape[0]
    shape = (slots, piece, BLOCK)
    return launch(
        functools.partial(order_kernel, [len(g) for g in groups]),
        "order_pieces",
        (1,),
        [(a, whole(a.shape)) for a in arrays],
        [(like(shape, BF16), whole(shape))],
        scratch=[pltpu.VMEM((slots * piece, BLOCK), BF16)],
        prefetch=(order,),
        after=after,
    )[0]


def outer_kernel(lefts, groups, rights, has_more, pieces, *refs):
    if pieces:
        place, refs = refs[0], refs[1:]
    left_refs = refs[:lefts]
    right_refs = refs[lefts : lefts + groups * rights]
    more_refs = refs[lefts + groups * rights : lefts + groups * rights + has_more]
    out_refs = refs[lefts + groups * rights + has_more : -2]
    turned, held = refs[-2:]
    rows = left_refs[0].shape[0]
    index = pl.program_id(0)

    @pl.when(index == 0)
    def _():
        for block in range(lefts):
            turned[:, block * rows : (block + 1) * rows] = left_refs[block][...].T

    def run(used):
        high = used[0].shape[0]
        total = mm(turned[:, :high], used[0][...])
        for n in range(1, rights):
            total = total + mm(turned[:, n * high : (n + 1) * high], used[n][...])
        for more in more_refs:
            total = total + more[...].astype(F32)
        if pieces:
            held[...] = total.astype(BF16)
        else:
            out_refs[0][...] = total.astype(BF16)

    if groups == 1:
        run(right_refs)
    else:
        for group in range(groups):

            @pl.when(index // (pl.num_programs(0) // groups) == group)
            def _(group=group):
                run(right_refs[group * rights : (group + 1) * rights])

    if pieces:
        store_pieces(held, place[0], *out_refs)


def store_pieces(held, x_here, *outs):
    levels, piece = outs[0].shape[0], outs[0].shape[-2]
    tall, wide = held.shape
    row_blocks = tall // BLOCK
    for side in range(2):
        shift = pl.multiple_of((x_here + side) % 2 * piece, piece)
        for panel in range(wide // BLOCK):
            lanes = slice(panel * BLOCK, (panel + 1) * BLOCK)
            for block in range(row_blocks):
                for level in range(levels):
                    start = block * BLOCK + 2 * level * piece
                    outs[side][level, panel * row_blocks + block] = held[
                        pl.ds(shift + start, piece), lanes
                    ]


def outer(left, groups, side, sides, step, more=(), place=None, levels=0, after=(), cost=COST):
    rows, width = left[0].shape
    cols = groups[0][0].shape[1] // sides
    step = min(step, cols)
    tiles = cols // step
    count = tiles * len(groups)

    def columns(array, group):
        if len(groups) == 1:
            at = lambda i, *_: (0, side * tiles + i)
        else:
            at = lambda i, *_: (0, side * tiles + jnp.clip(i - group * tiles, 0, tiles - 1))
        return array, pl.BlockSpec((array.shape[0], step), at)

    ins = (
        [(a, whole(a.shape, True)) for a in left]
        + [columns(a, n) for n, group in enumerate(groups) for a in group]
        + [(a, pl.BlockSpec((width, step), lambda i, *_: (0, i))) for a in more]
    )
    if not levels:
        outs = [
            (like((width, cols * len(groups)), BF16), pl.BlockSpec((width, step), lambda i: (0, i)))
        ]
    else:
        piece = BLOCK // (2 * levels)
        held = step // BLOCK * (width // BLOCK)
        outs = [
            (
                like((levels, held * count, piece, BLOCK), BF16),
                pl.BlockSpec((levels, held, piece, BLOCK), lambda i, p: (0, i, 0, 0)),
            )
        ] * 2
    return launch(
        functools.partial(
            outer_kernel, len(left), len(groups), len(groups[0]), len(more), levels > 0
        ),
        "outer",
        (count,),
        ins,
        outs,
        scratch=[pltpu.VMEM((width, rows * len(left)), BF16), pltpu.VMEM((width, step), BF16)],
        prefetch=(place,) if levels else (),
        after=after,
        cost=cost,
    )


def two_parts(value):
    high = value.astype(BF16)
    return high, (value - high.astype(F32)).astype(BF16)


def step_kernel(g_ref, left_ref, right_ref, master_ref, grad_ref, stepped_ref, square_ref):
    owners, slots, piece, width = g_ref.shape
    for slot in range(slots):
        low = jnp.concatenate([g_ref[o, slot] for o in range(owners)], axis=0)
        grad_ref[slot] = low.astype(F32)
        high, rest = two_parts(left_ref[slot])
        turned = mm(high, low) + mm(rest, low)
        t_high, t_rest = two_parts(turned)
        r_high, r_rest = two_parts(right_ref[slot])
        direction = mm(t_high, r_high) + mm(t_high, r_rest) + mm(t_rest, r_high)
        stepped = master_ref[slot] - 0.3 * direction
        stepped_ref[slot] = stepped
        square_ref[slot : slot + 1] = jnp.sum(stepped * stepped, axis=0, keepdims=True)


def stats_kernel(g_ref, left_ref, right_ref, new_left_ref, new_right_ref):
    owners, slots, piece, width = g_ref.shape
    for slot in range(slots):
        low = jnp.concatenate([g_ref[o, slot] for o in range(owners)], axis=0)
        new_left_ref[slot] = 0.5 * left_ref[slot] + 0.5 * mm(low, low, NT)
        new_right_ref[slot] = 0.5 * right_ref[slot] + 0.5 * mm(low, low, TN)


def finish_kernel(stepped_ref, ema_ref, norm_ref, master_ref, new_ema_ref):
    slots = stepped_ref.shape[0]
    for slot in range(slots):
        master = stepped_ref[slot] * lax.rsqrt(norm_ref[slot : slot + 1] + 1e-06)
        master_ref[slot] = master
        new_ema_ref[slot] = 0.5 * ema_ref[slot] + 0.5 * master


def block_specs(count, slots):
    return pl.BlockSpec((slots, BLOCK, BLOCK), lambda i: (i, 0, 0))


def exchange(value, axis, pairs):
    return lax.ppermute(value, axis, pairs)


def shards(
    tokens,
    seq_lengths,
    qkv_weight,
    out_weight,
    up_gate_weight,
    down_weight,
    qk_scale,
    mlp_scale,
    eigen_rates,
    cotangent,
    block_order,
    master_blocks,
    ema_blocks,
    left_stats,
    right_stats,
    left_root,
    right_root,
):
    x_rows = tokens[0]
    total, width = x_rows.shape
    cols = qk_scale.shape[0]
    heads = lax.axis_size("head")
    owners = lax.axis_size("batch")
    ranks = heads // 2
    here = lax.axis_index("head")
    rank, core = here // 2, here % 2
    share = total // heads
    rows = share // CHUNKS
    tiles_all = total // rows

    core_swap = [(i, i ^ 1) for i in range(heads)]
    shift_up = [
        [(i, (i // 2 + s) % ranks * 2 + i % 2) for i in range(heads)] for s in range(ranks)
    ]
    shift_down = [
        [(i, (i // 2 - s) % ranks * 2 + i % 2) for i in range(heads)] for s in range(ranks)
    ]
    far_steps = list(range(1, ranks))
    ring = far_steps + [0]

    shares = jnp.stack(
        [(rank - s) % ranks * 2 + (core + d) % 2 for d in (1, 0) for s in ring]
    ).astype(jnp.int32)
    lengths = seq_lengths[0]
    upto = jnp.arange(lengths.shape[0], dtype=jnp.int32)
    ends = jnp.sum(jnp.where(upto[None, :] <= upto[:, None], lengths[None, :], 0), axis=1)

    def begin_of(row):
        segment = jnp.sum((row[:, None] >= ends[None, :]).astype(jnp.int32), axis=1)
        member = segment[:, None] == jnp.arange(ends.shape[0], dtype=jnp.int32)[None, :]
        return jnp.sum(jnp.where(member, (ends - seq_lengths[0])[None, :], 0), axis=1)

    tile_rows = jnp.arange(tiles_all, dtype=jnp.int32) * rows
    tile_begin = begin_of(tile_rows)
    lane = jnp.arange(LANES, dtype=jnp.int32) % (HEAD_DIM // 2)
    freq = 10000.0 ** (-lane.astype(F32) * 2.0 / HEAD_DIM)
    near_angle = jnp.arange(rows, dtype=F32)[:, None] * freq[None, :]
    far_angle = (tile_rows - tile_begin).astype(F32)[:, None] * freq[None, :]
    near = jnp.stack([jnp.cos(near_angle), jnp.sin(near_angle)])
    far = jnp.stack([jnp.cos(far_angle), jnp.sin(far_angle)])
    gains = qk_scale[None, :]
    rates = eigen_rates.T

    q, k, v, q_rot, k_rot = project(x_rows, qkv_weight, gains, near, far)
    weights = [
        (up_gate_weight, down_weight),
        (exchange(up_gate_weight, "head", core_swap), exchange(down_weight, "head", core_swap)),
    ]
    scales = jnp.concatenate([mlp_scale, exchange(mlp_scale, "head", core_swap)], axis=1)

    def from_partner(send, keep, size):
        got = exchange(send, "head", core_swap)
        if ranks == 1:
            return keep[:size], [keep, got]
        away = (keep[:-size].astype(F32) + got[:-size].astype(F32)).astype(BF16)
        return away, [keep, got] + from_ranks(away, size)

    def from_ranks(away, size):
        return [
            exchange(away[n * size : (n + 1) * size], "head", shift_down[s])
            for n, s in enumerate(far_steps)
        ]

    def gather_ranks(own):
        return [exchange(own, "head", shift_up[s]) for s in far_steps] + [own]

    def gather_shares(own):
        mine = gather_ranks(own)
        return [exchange(b, "head", core_swap) for b in mine] + mine

    places = [(here * CHUNKS + j).astype(jnp.int32)[None] for j in range(CHUNKS)]
    tiles = [shares * CHUNKS + j for j in range(CHUNKS)]
    starts = [begin_of(t * rows) for t in tiles]
    chunks = range(CHUNKS)
    tile = 2 * BLOCK

    attn_out, lse, parts = [], [], []
    last = ()
    for j in chunks:
        half = heads // 2
        first = attend(
            q, k, v, out_weight, tiles[j][:half], starts[j][:half], rows, 0, heads, last
        )
        second = attend(
            q,
            k,
            v,
            out_weight,
            tiles[j][half:],
            starts[j][half:],
            rows,
            half,
            heads,
            (first[0], first[1]),
            2,
        )
        away, got = from_partner(first[2], second[2], rows)
        attn_out.append(second[0])
        lse.append(second[1])
        parts.append(got)
        last = (away,)
    joined = []
    for j in chunks:
        joined.append(join_attention(parts[j], x_rows, places[j], rates, rows, last))
        last = (joined[j][0],)
    hidden = [gather_ranks(joined[j][0]) for j in chunks]
    ffn = []
    for j in chunks:
        ffn.append(mlp(hidden[j], weights, scales, tile, last))
        last = (ffn[j][4],)
    ends_fwd = []
    for j in chunks:
        parts = [ffn[j][4]] + from_ranks(ffn[j][3], rows)
        ends_fwd.append(
            join_mlp(
                parts,
                joined[j][1],
                cotangent[0],
                j,
                rates,
                rows,
                ((ends_fwd[-1][0],) if j else ()) + last,
                1 if j else 0,
            )
        )
        last = (ends_fwd[j][1],)
    d_rows = [gather_ranks(ends_fwd[j][1]) for j in chunks]
    back = []
    for j in chunks:
        back.append(mlp_back(d_rows[j], ffn[j][0], ffn[j][1], weights, scales, tile, last))
        last = (back[j][4],)

    row_blocks = width // BLOCK
    piece = BLOCK // owners
    across = ranks
    levels = owners // across
    z_here, x_here = lax.axis_index("batch") // across, lax.axis_index("batch") % across
    direct = levels if piece % 16 == 0 and across == 2 else 0
    x_place = x_here.astype(jnp.int32)[None]
    left_hidden = [b for h in hidden for b in h]
    left_down = [b for d in d_rows for b in d]
    rights = {
        "down": (left_down, [[f[2] for f in ffn]]),
        "up_gate": (left_hidden, [[b[0] for b in back], [b[1] for b in back]]),
    }

    def partner_part(name, after):
        out = outer(*rights[name], 1, 2, tile, after=after)[0]
        return out, exchange(out, "head", core_swap)

    def own_part(name, more, after):
        return outer(
            *rights[name],
            0,
            2,
            tile,
            more=(more,),
            place=x_place,
            levels=direct,
            after=after,
            cost=COST if name == "down" else TINY,
        )

    def as_pieces(matrix):
        panels = matrix.shape[1] // BLOCK
        return (
            matrix.reshape(row_blocks, levels, across, piece, panels, BLOCK)
            .transpose(1, 2, 4, 0, 3, 5)
            .reshape(levels, across, panels * row_blocks * piece, BLOCK)
        )

    def from_this_x(pieces):
        return [
            lax.dynamic_index_in_dim(pieces, (x_here + s) % across, 1, keepdims=False)
            for s in range(across)
        ]

    def hold(value, anchor):
        return value if anchor is None else lax.optimization_barrier((value, anchor))[0]

    x_step = lambda s: [
        (i, i // across * across + (i % across + s) % across) for i in range(owners)
    ]
    z_step = lambda s: [
        (i, (i // across + s) % levels * across + i % across) for i in range(owners)
    ]
    z_place = z_here.astype(jnp.int32)[None]

    def over_z(parts):
        return [parts[0]] + [
            exchange(parts[s], "batch", z_step(s)) for s in range(1, levels)
        ]

    def plain_x(pieces):
        total = pieces[0].astype(F32)
        for s in range(1, across):
            total = total + exchange(pieces[s], "batch", x_step(s)).astype(F32)
        total = total.astype(BF16)
        return [
            lax.dynamic_index_in_dim(total, (z_here + s) % levels, 0, keepdims=False)
            for s in range(levels)
        ]

    def start_x(outs):
        if direct:
            mine, other = [flat(o) for o in outs]
            return mine, exchange(other, "batch", x_step(1))
        return from_this_x(as_pieces(outs[0]))

    def finish_x(started, after):
        if direct:
            sums = join_x(started, z_place, after)
        else:
            sums = plain_x([jnp.concatenate(p, axis=1) for p in zip(*started, strict=True)])
        return over_z(sums)

    split = []
    partner = {}
    for j in chunks:
        parts = [back[j][4]] + from_ranks(back[j][3], rows)
        split.append(
            split_attention(
                parts,
                ends_fwd[j][2],
                joined[j][1],
                joined[j][2],
                x_rows,
                places[j],
                rates,
                rows,
                last,
            )
        )
        last = (split[j][0],)
        if j == 0:
            out, partner["down"] = partner_part("down", last)
            last = (out,)
    out, partner["up_gate"] = partner_part("up_gate", last)
    last = (out,)
    d_attn_mine = [gather_ranks(split[j][0]) for j in chunks]
    flat = lambda a: a.reshape(a.shape[:-3] + (-1, BLOCK))
    started = {}
    for name, gathered in (("down", d_attn_mine[0]), ("up_gate", d_attn_mine[-1])):
        outs = own_part(name, partner[name], last + tuple(gathered[:-1]))
        last = (outs[0],)
        started[name] = start_x(outs)
        turn = outs[0] if name == "down" else turn
    d_attn_rows = [
        [exchange(hold(b, turn), "head", core_swap) for b in mine] + mine
        for mine in d_attn_mine
    ]
    outs = outer(
        [b for d in d_attn_rows for b in d],
        [attn_out],
        0,
        1,
        tile,
        place=x_place,
        levels=direct,
        after=last,
        cost=SHORT,
    )
    last = (outs[0],)
    started["out"] = start_x(outs)
    order = jnp.concatenate(tiles)
    order_starts = jnp.concatenate(starts)
    moved = {}
    pairs_all = cols // LANES
    raws, gain_parts, late = [], [], []
    marks = []
    for pair in range(pairs_all):
        pair_back = attend_back(
            [b for d in d_attn_rows for b in d],
            q,
            k,
            v,
            attn_out,
            lse,
            out_weight,
            order,
            order_starts,
            rows,
            pair,
            last,
        )
        last = (pair_back[0],)
        marks.append(last[0])
        if pair == 0:
            moved["down_out"] = finish_x([started["down"], started["out"]], last)
            last = (moved["down_out"][0],)
        raw, gain_part, *outs = project_back(
            x_rows,
            q_rot,
            k_rot,
            gains,
            near,
            far,
            pair_back,
            order,
            rows,
            pair,
            x_place,
            direct,
            last,
        )
        last = (raw,)
        raws.append(raw)
        gain_parts.append(gain_part)
        late.append(start_x(outs))
        if pair == 0:
            last = last + tuple(moved["down_out"][1:])
            moved["up_gate"] = finish_x([started["up_gate"]], last)
            last = (moved["up_gate"][0],)
    arrived = moved["up_gate"][1:] + [a for pieces in late[:-1] for a in pieces[1:]]
    send, keep = input_back(raws, qkv_weight, shares, share, last + tuple(arrived))
    gain_grad = jnp.concatenate(gain_parts, axis=1)
    moved["late"] = finish_x(late, (keep,))

    def double(value, axis, size, anchors=()):
        step = 1
        turn = 0
        while step < size:
            got = exchange(value, axis, [(i, i ^ step) for i in range(size)])
            value = value + hold(got, anchors[turn] if turn < len(anchors) else None)
            step *= 2
            turn += 1
        return value

    rate_grad = double(
        hold(
            jnp.concatenate([sum(s[2] for s in split), sum(e[3] for e in ends_fwd)], axis=0),
            raws[-1],
        ),
        "head",
        heads,
    )
    both = hold(sum(b[2] for b in back), raws[-1])
    scale_cols = mlp_scale.shape[1]
    scale_grad = both[:, :scale_cols] + exchange(both[:, scale_cols:], "head", core_swap)

    slot_order = block_order[0]
    panel, rest = slot_order // row_blocks, slot_order % row_blocks
    late_panels = 3 * pairs_all
    panels = slot_order.shape[0] // row_blocks
    down_panels = scale_cols // BLOCK
    late_panel = panel % pairs_all * 3 + panel // pairs_all
    down_panel = panel - (panels - down_panels) + late_panels
    held_panel = jnp.where(panel >= panels - down_panels, down_panel, panel + down_panels)
    place_of = jnp.where(panel < late_panels, late_panel, held_panel) * row_blocks + rest
    groups = [moved[n] for n in ("late", "down_out", "up_gate")]
    if direct:
        ordered = order_pieces(groups, place_of, piece, ())
    else:
        sums = [sum(a.astype(F32) for a in g).astype(BF16) for g in groups]
        pieces = jnp.concatenate(sums, axis=0).reshape(-1, piece, BLOCK)
        ordered = jnp.take(pieces, place_of, axis=0, mode="clip")
    got = exchange(send, "head", core_swap)
    parts = [keep, got]
    last = (ordered,)
    if ranks > 1:
        away = join_partner(keep, got, share, last)
        last = (away,)
        parts += from_ranks(away, share)
    per_owner = slot_order.shape[0] // owners
    owned = lax.all_to_all(
        ordered.reshape(owners, per_owner, piece, BLOCK),
        "batch",
        split_axis=0,
        concat_axis=0,
        tiled=True,
    )
    slots = min(8, per_owner)
    if piece % 16:
        owned = owned.transpose(1, 0, 2, 3).reshape(1, per_owner, BLOCK, BLOCK)
    g_spec = pl.BlockSpec(
        (owned.shape[0], slots) + owned.shape[2:], lambda i: (0, i, 0, 0)
    )
    blk = pl.BlockSpec((slots, BLOCK, BLOCK), lambda i: (i, 0, 0))
    row = pl.BlockSpec((slots, BLOCK), lambda i: (i, 0))
    cube = jax.ShapeDtypeStruct((per_owner, BLOCK, BLOCK), F32)
    grid = (per_owner // slots,)
    owned_grad, stepped, column_sq = launch(
        step_kernel,
        "step",
        grid,
        [(owned, g_spec), (left_root[0], blk), (right_root[0], blk), (master_blocks[0], blk)],
        [(cube, blk), (cube, blk), (like((per_owner, BLOCK), F32), row)],
        after=last,
    )
    new_left, new_right = launch(
        stats_kernel,
        "stats",
        grid,
        [(owned, g_spec), (left_stats[0], blk), (right_stats[0], blk)],
        [(cube, blk), (cube, blk)],
        after=(column_sq,),
    )
    my_blocks = lax.dynamic_slice_in_dim(
        slot_order, lax.axis_index("batch") * per_owner, per_owner, 0
    )
    member = (
        (my_blocks // row_blocks)[:, None] == jnp.arange(panels, dtype=jnp.int32)[None, :]
    ).astype(F32)
    precise = lax.Precision.HIGHEST
    sums = jnp.concatenate(
        [jnp.einsum("sp,sb->pb", member, column_sq, precision=precise)]
        + [a.reshape(-1, LANES) for a in (gain_grad, rate_grad, scale_grad)],
        axis=0,
    )
    d_input = sum_input(parts, [s[1] for s in split], rows, (new_left,))
    sums = double(sums, "batch", owners, (new_left, d_input))
    totals = sums[:panels]
    small = sums[panels:].reshape(-1)
    gain_sum = small[:cols]
    rate_sum = small[cols : cols + 2 * width].reshape(2, width)
    scale_sum = small[cols + 2 * width :].reshape(mlp_scale.shape)
    norms = jnp.einsum("sp,pb->sb", member, totals, precision=precise)
    new_master, new_ema = pl.pallas_call(
        finish_kernel,
        grid=grid,
        in_specs=[blk, blk, row],
        out_specs=[blk, blk],
        out_shape=[cube, cube],
        name="finish",
    )(stepped, ema_blocks[0], norms)
    gain_step = 0.5 / math.sqrt(total * owners)
    width_share = width // heads
    rate_here = lax.dynamic_slice_in_dim(rate_sum, here * width_share, width_share, 1)
    rate_slice = lax.dynamic_slice_in_dim(rates, here * width_share, width_share, 1)
    mlp_scale_out = jnp.stack([scale_sum, mlp_scale - gain_step * scale_sum])
    new_gains = jnp.concatenate(
        [(qk_scale - gain_step * gain_sum)[None, :], rate_slice - gain_step * rate_here], axis=0
    )
    out_share = ends_fwd[-1][0]
    return (
        out_share[None],
        d_input[None],
        owned_grad[None],
        new_master[None],
        new_ema[None],
        new_left[None],
        new_right[None],
        gain_sum,
        mlp_scale_out,
        rate_here.T,
        new_gains,
    )


def solution(mesh):
    return jax.shard_map(
        shards,
        mesh=mesh,
        in_specs=(
            P("batch", None, None),
            P("batch", None),
            P(None, None, "head"),
            P("head", None),
            P(None, None, "head"),
            P("head", None),
            P("head"),
            P(None, "head"),
            P(),
            P("batch", "head", None),
            P("head", None),
            P("head", "batch", None, None),
            P("head", "batch", None, None),
            P("head", "batch", None, None),
            P("head", "batch", None, None),
            P("head", "batch", None, None),
            P("head", "batch", None, None),
        ),
        out_specs=(
            P("batch", "head", None),
            P("batch", "head", None),
            P("head", "batch", None, None),
            P("head", "batch", None, None),
            P("head", "batch", None, None),
            P("head", "batch", None, None),
            P("head", "batch", None, None),
            P("head"),
            P(None, None, "head"),
            P("head", None),
            P(None, "head"),
        ),
        check_vma=False,
    )
```
